32 devices in a mesh: fsdp: 4 (over y, x), context: 2 (over core), tensor: 4 (over z).
Axes of the slice: x: 2, y: 2, z: 4, core: 2. Of those that a mesh axis runs over, the one named last changes fastest.
Arguments:
- tokens: bfloat16 [2048, 640], P(('fsdp', 'context')), may hold values from -16 to 16
- lengths: int32 [4, 4], P('fsdp'), may hold values from 1 to 256, 512 in all within a row
- weight_query: bfloat16 [640, 1024], P('fsdp', 'tensor'), may hold values from -1 to 1
- weight_key: bfloat16 [640, 256], P('fsdp'), may hold values from -1 to 1
- weight_value: bfloat16 [640, 256], P('fsdp'), may hold values from -0.25 to 0.25
- weight_out: bfloat16 [1024, 640], P('tensor', 'fsdp'), may hold values from -0.1875 to 0.1875
- weight_gate: bfloat16 [640, 2048], P('fsdp', 'tensor'), may hold values from -0.25 to 0.25
- weight_up: bfloat16 [640, 2048], P('fsdp', 'tensor'), may hold values from -0.25 to 0.25
- weight_down: bfloat16 [2048, 640], P('tensor', 'fsdp'), may hold values from -0.125 to 0.125
- gain_attn_in: bfloat16 [640], P('fsdp'), may hold values from 0.099609375 to 1.8984375
- gain_attn_out: bfloat16 [640], P('fsdp'), may hold values from 0.099609375 to 1.8984375
- gain_ffn_in: bfloat16 [640], P('fsdp'), may hold values from 0.099609375 to 1.8984375
- gain_ffn_out: bfloat16 [640], P('fsdp'), may hold values from 0.099609375 to 1.8984375
- gain_query: bfloat16 [256], P('fsdp'), may hold values from 0.5 to 2
- gain_key: bfloat16 [256], P('fsdp'), may hold values from 0.5 to 2
- cotangent: bfloat16 [2048, 640], P(('fsdp', 'context')), may hold values from -6 to 6
Outputs:
- layer_output: float32 [2048, 640], P(('fsdp', 'context'))
- grad_input: float32 [2048, 640], P(('fsdp', 'context'))
- grad_weight_query: float32 [640, 1024], P('fsdp', 'tensor')
- grad_weight_key: float32 [640, 256], P('fsdp')
- grad_weight_value: float32 [640, 256], P('fsdp')
- grad_weight_out: float32 [1024, 640], P('tensor', 'fsdp')
- grad_weight_gate: float32 [640, 2048], P('fsdp', 'tensor')
- grad_weight_up: float32 [640, 2048], P('fsdp', 'tensor')
- grad_weight_down: float32 [2048, 640], P('tensor', 'fsdp')
- grad_gain_attn_in: float32 [640], P('fsdp')
- grad_gain_attn_out: float32 [640], P('fsdp')
- grad_gain_ffn_in: float32 [640], P('fsdp')
- grad_gain_ffn_out: float32 [640], P('fsdp')
- grad_gain_query: float32 [256], P('fsdp')
- grad_gain_key: float32 [256], P('fsdp')
The draws below stay inside these ranges and needn't reach their ends.
Inputs may be any that keep to these rules, and one draw needn't show every extreme that they name: `lengths`: each row sums to 512; its largest entry is exactly 256.
All inputs are finite; a program needn't handle non-finite values.
Results may differ from the reference program's by a relative error of at most 0.015.
Values may be sent and summed in bfloat16 or wider, within the bound.
No kernel may reach another device: no remote copies, remote signals or barrier semaphores. Data moves between devices by JAX's collectives and lax.ppermute only.
A program may use at most 128 MiB of HBM per device.

```python
import math
import jax
import jax.numpy as jnp
import numpy as np
from jax import lax

D = 640
HEADS = 4
HD = 256
FF = 2048
GROUP = 256
NSEQ = 4
STREAM = 512
TOKENS = 2048
N_FSDP = 4
N_CONTEXT = 2


def draw_tokens(key, part):
    noise = jnp.clip(jax.random.normal(jax.random.fold_in(key, 3), (TOKENS, D), jnp.float32), -6.0, 6.0)
    return noise.astype(jnp.bfloat16)


def query_matrix(key):
    fresh = jnp.clip(jax.random.normal(jax.random.fold_in(key, 11), (D, HEADS * HD), jnp.float32), -6.0, 6.0)
    return fresh * D ** (-0.5)


def draw_weight_query(key, part):
    return query_matrix(key).astype(jnp.bfloat16)


def draw_weight_key(key, part):
    return (jnp.clip(jax.random.normal(jax.random.fold_in(key, 12), (D, HD), jnp.float32), -6.0, 6.0) * D ** (-0.5)).astype(jnp.bfloat16)


def draw_gain_query(key, part):
    return jnp.clip(1.25 + 0.3 * jax.random.normal(jax.random.fold_in(key, 21), (HD,), jnp.float32), 0.5, 2.0).astype(jnp.bfloat16)


def draw_gain_key(key, part):
    return jnp.clip(1.25 + 0.3 * jax.random.normal(jax.random.fold_in(key, 22), (HD,), jnp.float32), 0.5, 2.0).astype(jnp.bfloat16)


def shard_levels(stream_key, shape, split, least, high):
    factor_of, own = 1.0, jax.random.fold_in(stream_key, 6)
    for dim, shards_of in split:
        steps = jnp.exp(jax.random.uniform(jax.random.fold_in(own, dim), (shards_of,), jnp.float32, least / len(split), high / len(split)))
        factor_of = factor_of * jnp.repeat(steps, shape[dim] // shards_of).reshape([-1 if axis == dim else 1 for axis in range(len(shape))])
    return factor_of


def profile(count, total, most, lean):
    weights = [(1 << 20) // math.isqrt(standing ** lean) + 1 for standing in range(2, count + 1)]
    surplus, counts = total - most - (count - 1), [1] * (count - 1)
    while surplus > 0:
        free = [i for i in range(count - 1) if counts[i] < most]
        whole, budget = sum([weights[i] for i in free]), surplus
        for i in free:
            more = min(most - counts[i], max(1, budget * weights[i] // whole), surplus)
            counts[i] = counts[i] + more
            surplus = surplus - more
    return np.array([most] + counts)


def ragged_sizes(key, number_of, total, reach, lean):
    if number_of == 2:
        one = jax.random.randint(key, (), max(1, total - reach), min(reach, total - 1) + 1)
        return jnp.stack([one, total - one])
    sizes = jnp.asarray(profile(number_of, total, reach, lean), jnp.int32)
    couples = (number_of - 1) // 2
    donor, sink = sizes[1:1 + 2 * couples:2], sizes[2:2 + 2 * couples:2]
    room = jnp.minimum(donor - 1, reach - sink)
    moved = jax.random.randint(jax.random.fold_in(key, 1), (couples,), 0, 1 << 20) % (room + 1)
    sizes = sizes.at[1:1 + 2 * couples:2].set(donor - moved).at[2:2 + 2 * couples:2].set(sink + moved)
    return sizes[jax.random.permutation(jax.random.fold_in(key, 2), number_of)]


def centred(stream_key, shape, scale, reach, split=(), kind=jnp.bfloat16):
    gain = shard_levels(stream_key, shape, split, -0.22, 0.18) if split else 1.0
    entries = jax.random.normal(stream_key, shape, jnp.float32) * scale * gain
    return jnp.minimum(jnp.maximum(entries, -reach), reach).astype(kind)


def setup_inputs(seed: int = 0) -> dict:
    key_of = jax.random.split(jax.random.key(seed), 17)
    tokens = draw_tokens(jax.random.fold_in(key_of[16], 71), 0)
    lengths = jax.vmap(lambda own: ragged_sizes(own, NSEQ, STREAM, STREAM // 2, 2))(jax.random.split(key_of[1], N_FSDP)).reshape((N_FSDP, NSEQ)).astype(jnp.int32)
    weight_query = draw_weight_query(jax.random.fold_in(key_of[16], 71), 0)
    weight_key = draw_weight_key(jax.random.fold_in(key_of[16], 71), 0)
    weight_value = centred(key_of[4], (D, HD), D ** -0.5, 0.25, ((0, 4),))
    weight_out = centred(key_of[5], (HEADS * HD, D), (HEADS * HD) ** -0.5, 0.1875, ((0, 4), (1, 4)))
    weight_gate = centred(key_of[6], (D, FF), D ** -0.5, 0.25, ((0, 4), (1, 4)))
    weight_up = centred(key_of[7], (D, FF), D ** -0.5, 0.25, ((0, 4), (1, 4)))
    weight_down = centred(key_of[8], (FF, D), FF ** -0.5, 0.125, ((0, 4), (1, 4)))
    gain_attn_in = jnp.clip(1.0 + 0.18 * jax.random.normal(key_of[9], (D,), jnp.float32), 0.099609375, 1.8984375).astype(jnp.bfloat16)
    gain_attn_out = jnp.clip(1.0 + 0.18 * jax.random.normal(key_of[10], (D,), jnp.float32), 0.099609375, 1.8984375).astype(jnp.bfloat16)
    gain_ffn_in = jnp.clip(1.0 + 0.18 * jax.random.normal(key_of[11], (D,), jnp.float32), 0.099609375, 1.8984375).astype(jnp.bfloat16)
    gain_ffn_out = jnp.clip(1.0 + 0.18 * jax.random.normal(key_of[12], (D,), jnp.float32), 0.099609375, 1.8984375).astype(jnp.bfloat16)
    gain_query = draw_gain_query(jax.random.fold_in(key_of[16], 71), 0)
    gain_key = draw_gain_key(jax.random.fold_in(key_of[16], 71), 0)
    cotangent = centred(key_of[15], (TOKENS, D), 1.0, 6.0, ((0, 8),))
    return {"tokens": tokens, "lengths": lengths, "weight_query": weight_query, "weight_key": weight_key, "weight_value": weight_value, "weight_out": weight_out, "weight_gate": weight_gate, "weight_up": weight_up, "weight_down": weight_down, "gain_attn_in": gain_attn_in, "gain_attn_out": gain_attn_out, "gain_ffn_in": gain_ffn_in, "gain_ffn_out": gain_ffn_out, "gain_query": gain_query, "gain_key": gain_key, "cotangent": cotangent}


EPSILON = 1e-06
ROPE_BASE = 1000000.0
GELU_COEF = math.sqrt(2.0 / math.pi)
NEG_LARGE = -1e+30

def to_bf16(values):
    return lax.optimization_barrier(values.astype(jnp.bfloat16))

def rms_forward(values, gain_vec):
    inverse = lax.rsqrt(lax.optimization_barrier(jnp.mean(values * values, axis=-1, keepdims=True)) + EPSILON)
    normed = values * inverse
    return (normed * gain_vec, normed, inverse)

def rms_backward(grad_out, gain_vec, normed, inverse):
    gain_grad = lax.optimization_barrier(jnp.sum(grad_out * normed, axis=tuple(range(grad_out.ndim - 1))))
    inner = grad_out * gain_vec
    grad_in = inverse * (inner - normed * lax.optimization_barrier(jnp.mean(inner * normed, axis=-1, keepdims=True)))
    return (grad_in, gain_grad)

def rope_tables(positions, width):
    half_width = width // 2
    freqs = ROPE_BASE ** (-jnp.arange(half_width, dtype=jnp.float32) * 2.0 / width)
    angles = positions.astype(jnp.float32)[:, None] * freqs[None, :]
    return (jnp.cos(angles)[:, None, :], jnp.sin(angles)[:, None, :])

def rotate(values, cosine, sine):
    half_width = values.shape[-1] // 2
    first_half = values[..., :half_width]
    second_half = values[..., half_width:]
    return jnp.concatenate([first_half * cosine - second_half * sine, second_half * cosine + first_half * sine], axis=-1)

def rotate_back(values, cosine, sine):
    half_width = values.shape[-1] // 2
    first_half = values[..., :half_width]
    second_half = values[..., half_width:]
    return jnp.concatenate([first_half * cosine + second_half * sine, second_half * cosine - first_half * sine], axis=-1)

def gelu_parts(pre_act):
    cubic = pre_act + 0.044715 * pre_act * pre_act * pre_act
    tangent = jnp.tanh(GELU_COEF * cubic)
    gelu_val = 0.5 * pre_act * (1.0 + tangent)
    slope = 0.5 * (1.0 + tangent) + 0.5 * pre_act * (1.0 - tangent * tangent) * GELU_COEF * (1.0 + 3.0 * 0.044715 * pre_act * pre_act)
    return (gelu_val, slope)

def doc_info(positions, doc_lengths):
    doc_ends = jnp.cumsum(doc_lengths)
    passed = positions[:, None] >= doc_ends[None, :]
    segment = lax.optimization_barrier(jnp.sum(passed.astype(jnp.int32), axis=1))
    doc_start = lax.optimization_barrier(jnp.sum(jnp.where(passed, doc_lengths[None, :], 0), axis=1))
    return (segment, positions - doc_start)

def attention_forward(query_rot, key_rot, value_own, segment, token_index):
    total_rows = key_rot.shape[0]
    blk_rows = math.gcd(total_rows, 512)
    key_float = key_rot.astype(jnp.float32)
    value_float = value_own.astype(jnp.float32)

    def one_block(block_num):
        row_begin = block_num * blk_rows
        query_blk = lax.dynamic_slice_in_dim(query_rot, row_begin, blk_rows, 0).astype(jnp.float32)
        seg_blk = lax.dynamic_slice_in_dim(segment, row_begin, blk_rows, 0)
        idx_blk = lax.dynamic_slice_in_dim(token_index, row_begin, blk_rows, 0)
        allowed = (seg_blk[:, None] == segment[None, :]) & (idx_blk[:, None] >= token_index[None, :])
        scores = jnp.einsum('qhd,kd->hqk', query_blk, key_float)
        scores = jnp.where(allowed[None], scores, NEG_LARGE)
        row_max = lax.optimization_barrier(jnp.max(scores, axis=2))
        weights = jnp.where(allowed[None], jnp.exp(scores - row_max[:, :, None]), 0.0)
        totals = lax.optimization_barrier(jnp.sum(weights, axis=2))
        rounded = to_bf16(weights).astype(jnp.float32)
        summed = jnp.einsum('hqk,kd->qhd', rounded, value_float)
        return (summed / totals.T[:, :, None], (row_max + jnp.log(totals)).T)
    results, log_totals = lax.map(one_block, jnp.arange(total_rows // blk_rows, dtype=jnp.int32))
    return (results.reshape(total_rows, HEADS, HD), log_totals.reshape(total_rows, HEADS))

def attention_backward(query_rot, key_rot, value_own, grad_heads, log_total, delta, segment, token_index):
    total_rows = key_rot.shape[0]
    blk_rows = math.gcd(total_rows, 512)
    key_float = key_rot.astype(jnp.float32)
    value_float = value_own.astype(jnp.float32)

    def one_block(carry, block_num):
        key_acc, value_acc = carry
        row_begin = block_num * blk_rows
        query_blk = lax.dynamic_slice_in_dim(query_rot, row_begin, blk_rows, 0).astype(jnp.float32)
        grad_blk = lax.dynamic_slice_in_dim(grad_heads, row_begin, blk_rows, 0).astype(jnp.float32)
        lse_blk = lax.dynamic_slice_in_dim(log_total, row_begin, blk_rows, 0)
        delta_blk = lax.dynamic_slice_in_dim(delta, row_begin, blk_rows, 0)
        seg_blk = lax.dynamic_slice_in_dim(segment, row_begin, blk_rows, 0)
        idx_blk = lax.dynamic_slice_in_dim(token_index, row_begin, blk_rows, 0)
        allowed = (seg_blk[:, None] == segment[None, :]) & (idx_blk[:, None] >= token_index[None, :])
        scores = jnp.einsum('qhd,kd->hqk', query_blk, key_float)
        probs = jnp.where(allowed[None], jnp.exp(scores - lse_blk.T[:, :, None]), 0.0)
        grad_probs = jnp.einsum('qhd,kd->hqk', grad_blk, value_float)
        grad_scores = probs * (grad_probs - delta_blk.T[:, :, None])
        scores_round = to_bf16(grad_scores).astype(jnp.float32)
        probs_round = to_bf16(probs).astype(jnp.float32)
        grad_query = jnp.einsum('hqk,kd->qhd', scores_round, key_float)
        key_acc = key_acc + jnp.einsum('hqk,qhd->kd', scores_round, query_blk)
        value_acc = value_acc + jnp.einsum('hqk,qhd->kd', probs_round, grad_blk)
        return ((key_acc, value_acc), grad_query)
    zero_rows = jnp.zeros((total_rows, HD), jnp.float32)
    (key_grad, value_grad), grad_query = lax.scan(one_block, (zero_rows, zero_rows), jnp.arange(total_rows // blk_rows, dtype=jnp.int32))
    return (grad_query.reshape(total_rows, HEADS, HD), key_grad, value_grad)

def dot32(mat_left, mat_right):
    return jnp.dot(mat_left, mat_right, preferred_element_type=jnp.float32)

def layer_stream(tok_stream, doc_lengths, cot_stream, weights, gains):
    weight_query, weight_key, weight_value, weight_out, weight_gate, weight_up, weight_down = weights
    scale_ai, scale_ao, scale_fi, scale_fo, scale_q, scale_k = gains
    total_rows = tok_stream.shape[0]
    token_index = jnp.arange(total_rows, dtype=jnp.int32)
    segment, position = doc_info(token_index, doc_lengths)
    cosine, sine = rope_tables(position, HD)
    att_scale = HD ** (-0.5)
    inputs_f = tok_stream.astype(jnp.float32)
    normed_one, hat_one, inv_one = rms_forward(inputs_f, scale_ai)
    act_one = to_bf16(normed_one)
    query_pre = dot32(act_one, weight_query).reshape(total_rows, HEADS, HD)
    query_norm, query_hat, query_inv = rms_forward(query_pre, scale_q)
    query_rot = to_bf16(rotate(query_norm, cosine, sine) * att_scale)
    key_pre = dot32(act_one, weight_key).reshape(total_rows, 1, HD)
    key_norm, key_hat, key_inv = rms_forward(key_pre, scale_k)
    key_rot = to_bf16(rotate(key_norm, cosine, sine).reshape(total_rows, HD))
    value_own = to_bf16(dot32(act_one, weight_value))
    attn_float, log_total = attention_forward(query_rot, key_rot, value_own, segment, token_index)
    attn_heads = to_bf16(attn_float)
    attn_cat = attn_heads.reshape(total_rows, HEADS * HD)
    attn_total = dot32(attn_cat, weight_out)
    normed_two, hat_two, inv_two = rms_forward(attn_total, scale_ao)
    hidden_res = inputs_f + normed_two
    normed_three, hat_three, inv_three = rms_forward(hidden_res, scale_fi)
    act_three = to_bf16(normed_three)
    gate_pre = dot32(act_three, weight_gate)
    up_pre = dot32(act_three, weight_up)
    gelu_val, gelu_slope = gelu_parts(gate_pre)
    inner_act = to_bf16(gelu_val * up_pre)
    ffn_total = dot32(inner_act, weight_down)
    normed_four, hat_four, inv_four = rms_forward(ffn_total, scale_fo)
    layer_out = hidden_res + normed_four
    grad_final = cot_stream.astype(jnp.float32)
    grad_ffn, dscale_fo = rms_backward(grad_final, scale_fo, hat_four, inv_four)
    grad_ffn_b = to_bf16(grad_ffn)
    dweight_down = dot32(inner_act.T, grad_ffn_b)
    grad_inner = dot32(grad_ffn_b, weight_down.T)
    grad_gate_b = to_bf16(grad_inner * up_pre * gelu_slope)
    grad_up_b = to_bf16(grad_inner * gelu_val)
    dweight_gate = dot32(act_three.T, grad_gate_b)
    dweight_up = dot32(act_three.T, grad_up_b)
    grad_act_three = dot32(grad_gate_b, weight_gate.T) + dot32(grad_up_b, weight_up.T)
    grad_three, dscale_fi = rms_backward(grad_act_three, scale_fi, hat_three, inv_three)
    grad_hidden = grad_final + grad_three
    grad_attn, dscale_ao = rms_backward(grad_hidden, scale_ao, hat_two, inv_two)
    grad_attn_b = to_bf16(grad_attn)
    dweight_out = dot32(attn_cat.T, grad_attn_b)
    grad_heads = to_bf16(dot32(grad_attn_b, weight_out.T)).reshape(total_rows, HEADS, HD)
    delta = lax.optimization_barrier(jnp.sum(grad_heads.astype(jnp.float32) * attn_heads.astype(jnp.float32), axis=2))
    grad_query_rot, grad_key_rot, grad_value = attention_backward(query_rot, key_rot, value_own, grad_heads, log_total, delta, segment, token_index)
    grad_qnorm = rotate_back(grad_query_rot * att_scale, cosine, sine)
    grad_qpre, dscale_q = rms_backward(grad_qnorm, scale_q, query_hat, query_inv)
    grad_qpre_b = to_bf16(grad_qpre.reshape(total_rows, HEADS * HD))
    grad_knorm = rotate_back(grad_key_rot.reshape(total_rows, 1, HD), cosine, sine)
    grad_kpre, dscale_k = rms_backward(grad_knorm, scale_k, key_hat, key_inv)
    grad_kpre_b = to_bf16(grad_kpre.reshape(total_rows, HD))
    grad_value_b = to_bf16(grad_value)
    dweight_query = dot32(act_one.T, grad_qpre_b)
    dweight_key = dot32(act_one.T, grad_kpre_b)
    dweight_value = dot32(act_one.T, grad_value_b)
    grad_act_one = dot32(grad_qpre_b, weight_query.T) + dot32(grad_kpre_b, weight_key.T) + dot32(grad_value_b, weight_value.T)
    grad_one, dscale_ai = rms_backward(grad_act_one, scale_ai, hat_one, inv_one)
    grad_tokens = grad_hidden + grad_one
    outputs = (layer_out, grad_tokens)
    grads = (dweight_query, dweight_key, dweight_value, dweight_out, dweight_gate, dweight_up, dweight_down, dscale_ai, dscale_ao, dscale_fi, dscale_fo, dscale_q, dscale_k)
    return (outputs, grads)

def reference(tokens, lengths, weight_query, weight_key, weight_value, weight_out, weight_gate, weight_up, weight_down, gain_attn_in, gain_attn_out, gain_ffn_in, gain_ffn_out, gain_query, gain_key, cotangent):
    weights = (weight_query, weight_key, weight_value, weight_out, weight_gate, weight_up, weight_down)
    gain_list = (gain_attn_in, gain_attn_out, gain_ffn_in, gain_ffn_out, gain_query, gain_key)
    gains = tuple((gain_item.astype(jnp.float32) for gain_item in gain_list))
    stream_len = GROUP * N_CONTEXT

    def per_stream(carry, stream_inputs):
        tok_stream, doc_lengths, cot_stream = stream_inputs
        outputs, grads = layer_stream(tok_stream, doc_lengths, cot_stream, weights, gains)
        return (tuple((acc_item + grad_item for acc_item, grad_item in zip(carry, grads))), outputs)
    start_grads = tuple((jnp.zeros(param.shape, jnp.float32) for param in weights + gain_list))
    grads, (outputs, grad_tokens) = lax.scan(per_stream, start_grads, (tokens.reshape(N_FSDP, stream_len, D), lengths, cotangent.reshape(N_FSDP, stream_len, D)))
    return (outputs.reshape(N_FSDP * stream_len, D), grad_tokens.reshape(N_FSDP * stream_len, D), grads[0], grads[1], grads[2], grads[3], grads[4], grads[5], grads[6], grads[7], grads[8], grads[9], grads[10], grads[11], grads[12])
```

```python
import math

import jax
import jax.numpy as jnp
from jax import lax
from jax.sharding import PartitionSpec as P

HD = 256

EPSILON = 1e-06
ROPE_BASE = 1000000.0
GELU_COEF = math.sqrt(2.0 / math.pi)
NEG_LARGE = -1e30
BF = jnp.bfloat16
F32 = jnp.float32


def rms_stats(values):
    inverse = lax.rsqrt(jnp.mean(values * values, axis=-1, keepdims=True) + EPSILON)
    return values * inverse, inverse


def rms_back(grad_out, gain_vec, normed, inverse):
    inner = grad_out * gain_vec
    return inverse * (inner - normed * jnp.mean(inner * normed, axis=-1, keepdims=True))


def rope_tables(positions):
    half_width = HD // 2
    freqs = ROPE_BASE ** (-jnp.arange(half_width, dtype=F32) * 2.0 / HD)
    angles = positions.astype(F32)[:, None] * freqs[None, :]
    return jnp.cos(angles), jnp.sin(angles)


def rotate(values, cosine, sine):
    half = values.shape[-1] // 2
    first, second = values[:, :half], values[:, half:]
    return jnp.concatenate(
        [first * cosine - second * sine, second * cosine + first * sine], axis=-1
    )


def gelu_parts(pre_act):
    cubic = pre_act + 0.044715 * pre_act * pre_act * pre_act
    tangent = jnp.tanh(GELU_COEF * cubic)
    gelu_val = 0.5 * pre_act * (1.0 + tangent)
    slope = 0.5 * (1.0 + tangent) + 0.5 * pre_act * (1.0 - tangent * tangent) * GELU_COEF * (
        1.0 + 3.0 * 0.044715 * pre_act * pre_act
    )
    return gelu_val, slope


def doc_info(index, lengths):
    ends = jnp.cumsum(lengths)
    passed = index[:, None] >= ends[None, :]
    segment = jnp.sum(passed.astype(jnp.int32), axis=1)
    start = jnp.sum(jnp.where(passed, lengths[None, :], 0), axis=1)
    return segment, index - start


def dot32(left, right):
    return jnp.dot(left, right, preferred_element_type=F32)


def dot_nt(left, right):
    return lax.dot_general(left, right, (((1,), (1,)), ((), ())), preferred_element_type=F32)


def dot_tn(left, right):
    return lax.dot_general(left, right, (((0,), (0,)), ((), ())), preferred_element_type=F32)


def make_program(n_fsdp, n_context, n_tensor):
    def core_swap(value):
        return lax.ppermute(value, "context", [(i, i ^ 1) for i in range(n_context)])

    def z_near(value):
        return lax.ppermute(value, "tensor", [(i, i ^ 1) for i in range(n_tensor)])

    def z_far(value):
        return lax.ppermute(value, "tensor", [(i, i ^ 2) for i in range(n_tensor)])

    def z_one_way(value, from_owner):
        pairs = []
        for ctx in range(n_context):
            for pos in range(n_tensor):
                owner = (pos // 2) == (ctx % 2)
                if owner == from_owner:
                    pairs.append((ctx * n_tensor + pos, ctx * n_tensor + (pos ^ 2)))
        return lax.ppermute(value, ("context", "tensor"), pairs)

    def fsdp_hop(value, step):
        return lax.ppermute(value, "fsdp", [(i, i ^ step) for i in range(n_fsdp)])

    def gather_blocks(value):
        return [value] + [fsdp_hop(value, step) for step in range(1, n_fsdp)]

    def across_pairs(value):
        step = 2
        while step < n_context:
            value = value.astype(F32) + lax.ppermute(
                value.astype(BF), "context", [(i, i ^ step) for i in range(n_context)]
            ).astype(F32)
            step *= 2
        return value

    def on_device(
        tokens, lengths, weight_query, weight_key, weight_value, weight_out, weight_gate,
        weight_up, weight_down, gain_attn_in, gain_attn_out, gain_ffn_in, gain_ffn_out,
        gain_query, gain_key, cotangent,
    ):
        own_f = lax.axis_index("fsdp")
        ctx = lax.axis_index("context")
        pos_z = lax.axis_index("tensor")
        group = pos_z // 2
        is_owner = group == (ctx % 2)
        rows, width = tokens.shape
        half = rows // 2
        stream = rows * n_context
        block = weight_query.shape[0]
        gain_block = gain_query.shape[0]
        att_scale = HD ** (-0.5)
        order = jnp.arange(n_fsdp) ^ own_f

        def in_order(blocks):
            stacked = jnp.take(jnp.stack(blocks), order, axis=0)
            return stacked.reshape((-1,) + stacked.shape[2:])

        gains = jnp.concatenate(
            [gain_attn_in, gain_attn_out, gain_ffn_in, gain_ffn_out, gain_query, gain_key]
        )
        gain_all = jnp.take(jnp.stack(gather_blocks(gains)), order, axis=0).astype(F32)
        scales = []
        for i in range(4):
            scales.append(gain_all[:, i * block : (i + 1) * block].reshape(-1))
        for i in range(2):
            first = 4 * block + i * gain_block
            scales.append(gain_all[:, first : first + gain_block].reshape(-1))
        scale_ai, scale_ao, scale_fi, scale_fo, scale_q, scale_k = scales

        tokens_other = core_swap(tokens)
        pack_kv = jnp.concatenate([weight_key, weight_value], axis=1)
        pack_qo = jnp.concatenate([weight_query, weight_out.T], axis=1)
        pack_ffn = jnp.concatenate([weight_gate, weight_up, weight_down.T], axis=1)
        full_kv = in_order(gather_blocks(pack_kv))
        pack_qo = jnp.where(is_owner, pack_qo, z_one_way(pack_qo, True))
        full_qo = in_order(gather_blocks(pack_qo))
        pack_ffn = jnp.where(is_owner, pack_ffn, z_one_way(pack_ffn, True))
        hidden = weight_gate.shape[1]
        full_gu = in_order(gather_blocks(pack_ffn[:, : 2 * hidden]))
        full_dt = in_order(gather_blocks(pack_ffn[:, 2 * hidden :]))
        full_q, full_ot = full_qo[:, :HD], full_qo[:, HD:]

        span = jnp.arange(rows, dtype=jnp.int32)
        if n_context == 2:
            tok_all = jnp.concatenate([tokens, tokens_other], axis=0)
            key_index = jnp.concatenate([ctx * rows + span, (ctx ^ 1) * rows + span])
            place = (group * half, rows + group * half)
        else:
            tok_all = lax.all_gather(tokens, "context", axis=0, tiled=True)
            key_index = jnp.arange(stream, dtype=jnp.int32)
            place = (ctx * rows + group * half, (ctx ^ 1) * rows + group * half)

        def pick(value):
            return jnp.concatenate(
                [lax.dynamic_slice_in_dim(value, start, half, 0) for start in place], axis=0
            )

        doc_lengths = lengths[0]
        key_segment, key_position = doc_info(key_index, doc_lengths)
        cos_k, sin_k = rope_tables(key_position)
        row_index, row_segment = pick(key_index), pick(key_segment)
        cos_q, sin_q = pick(cos_k), pick(sin_k)
        allowed = (row_segment[:, None] == key_segment[None, :]) & (
            row_index[:, None] >= key_index[None, :]
        )

        hat_one, inv_one = rms_stats(tok_all.astype(F32))
        act_all = (hat_one * scale_ai).astype(BF)
        act_q = pick(act_all)
        q_hat, q_inv = rms_stats(dot32(act_q, full_q))
        q_rot = (rotate(q_hat * scale_q, cos_q, sin_q) * att_scale).astype(BF)
        kv_pre = dot32(act_all, full_kv)
        k_hat, k_inv = rms_stats(kv_pre[:, :HD])
        k_rot = rotate(k_hat * scale_k, cos_k, sin_k).astype(BF)
        value_all = kv_pre[:, HD:].astype(BF)

        scores = jnp.where(allowed, dot_nt(q_rot, k_rot), NEG_LARGE)
        row_max = jnp.max(scores, axis=1, keepdims=True)
        weights = jnp.where(allowed, jnp.exp(scores - row_max), 0.0)
        total = jnp.sum(weights, axis=1, keepdims=True)
        log_total = row_max + jnp.log(total)
        attn = (dot32(weights.astype(BF), value_all) / total).astype(BF)

        def row_sum(partial):
            pair = partial[:half] + core_swap(partial[half:].astype(BF)).astype(F32)
            pair = pair.astype(BF)
            return pair.astype(F32) + z_near(pair).astype(F32)

        def both_halves(value):
            return jnp.concatenate([value, core_swap(value)], axis=0)

        own_tok = lax.dynamic_slice_in_dim(tokens, group * half, half, 0).astype(F32)
        own_cot = lax.dynamic_slice_in_dim(cotangent, group * half, half, 0).astype(F32)

        attn_total = row_sum(dot_nt(attn, full_ot))
        hat_two, inv_two = rms_stats(attn_total)
        hidden_res = own_tok + hat_two * scale_ao
        hat_three, inv_three = rms_stats(hidden_res)
        act_three = both_halves((hat_three * scale_fi).astype(BF))
        gate_up = dot32(act_three, full_gu)
        gate_pre, up_pre = gate_up[:, :hidden], gate_up[:, hidden:]
        gelu_val, gelu_slope = gelu_parts(gate_pre)
        inner_act = (gelu_val * up_pre).astype(BF)
        ffn_total = row_sum(dot_nt(inner_act, full_dt))
        hat_four, inv_four = rms_stats(ffn_total)
        layer_half = hidden_res + hat_four * scale_fo
        dscale_fo = jnp.sum(own_cot * hat_four, axis=0)
        grad_ffn = both_halves(rms_back(own_cot, scale_fo, hat_four, inv_four).astype(BF))
        grad_dt = dot_tn(grad_ffn, inner_act)
        grad_inner = dot32(grad_ffn, full_dt)
        grad_gu = jnp.concatenate(
            [(grad_inner * up_pre * gelu_slope).astype(BF), (grad_inner * gelu_val).astype(BF)],
            axis=1,
        )
        grad_wgu = dot_tn(act_three, grad_gu)
        grad_three = row_sum(dot_nt(grad_gu, full_gu))
        dscale_fi = jnp.sum(grad_three * hat_three, axis=0)
        grad_hidden = own_cot + rms_back(grad_three, scale_fi, hat_three, inv_three)
        dscale_ao = jnp.sum(grad_hidden * hat_two, axis=0)
        grad_attn = both_halves(rms_back(grad_hidden, scale_ao, hat_two, inv_two).astype(BF))
        grad_wot = dot_tn(grad_attn, attn)
        grad_heads = dot32(grad_attn, full_ot).astype(BF)
        delta = jnp.sum(grad_heads.astype(F32) * attn.astype(F32), axis=1, keepdims=True)
        probs = jnp.where(allowed, jnp.exp(dot_nt(q_rot, k_rot) - log_total), 0.0)
        grad_s = (probs * (dot_nt(grad_heads, value_all) - delta)).astype(BF)
        grad_qrot = dot32(grad_s, k_rot)
        grad_krot = dot_tn(grad_s, q_rot)
        grad_v = dot_tn(probs.astype(BF), grad_heads).astype(BF)
        grad_qn = rotate(grad_qrot * att_scale, cos_q, -sin_q)
        dscale_q = jnp.sum(grad_qn * q_hat, axis=0)
        grad_q = rms_back(grad_qn, scale_q, q_hat, q_inv).astype(BF)
        grad_kn = rotate(grad_krot, cos_k, -sin_k)
        dscale_k = jnp.sum(grad_kn * k_hat, axis=0)
        grad_k = rms_back(grad_kn, scale_k, k_hat, k_inv).astype(BF)
        grad_kv = jnp.concatenate([grad_k, grad_v], axis=1)
        grad_wq = dot_tn(act_q, grad_q)
        grad_wkv = dot_tn(act_all, grad_kv)
        part = dot_nt(grad_kv, full_kv)
        part_q = dot_nt(grad_q, full_q)
        for i, start in enumerate(place):
            piece = lax.dynamic_slice_in_dim(part, start, half, 0)
            piece = piece + part_q[i * half : (i + 1) * half]
            part = lax.dynamic_update_slice_in_dim(part, piece, start, 0)
        dscale_ai = jnp.sum(part * hat_one, axis=0)

        part = part.astype(BF)
        if n_context == 2:
            mine = part[:rows].astype(F32) + core_swap(part[rows:]).astype(F32)
        else:
            mine = lax.psum_scatter(
                part.astype(F32), "context", scatter_dimension=0, tiled=True
            )
        mine = mine.astype(BF)
        keep = lax.dynamic_slice_in_dim(mine, group * half, half, 0)
        give = lax.dynamic_slice_in_dim(mine, (1 - group) * half, half, 0)
        keep = (keep.astype(F32) + z_far(give).astype(F32)).astype(BF)
        grad_one = keep.astype(F32) + z_near(keep).astype(F32)
        own_hat, own_inv = rms_stats(own_tok)
        grad_half = grad_hidden + rms_back(grad_one, scale_ai, own_hat, own_inv)

        def both_groups(value):
            value = value.astype(BF)
            other = z_far(value)
            low = jnp.where(group == 0, value, other)
            high = jnp.where(group == 0, other, value)
            return jnp.concatenate([low, high], axis=0).astype(F32)

        def scatter_blocks(value):
            pieces = value.astype(BF).reshape((n_fsdp, -1) + value.shape[1:])
            total_piece = 0.0
            for step in range(n_fsdp):
                piece = lax.dynamic_index_in_dim(pieces, own_f ^ step, 0, keepdims=False)
                if step:
                    piece = fsdp_hop(piece, step)
                total_piece = total_piece + piece.astype(F32)
            return total_piece

        def to_owner(value):
            value = across_pairs(value).astype(BF)
            final = (value.astype(F32) + z_one_way(value, False).astype(F32)).astype(BF)
            return jnp.where(is_owner, final, core_swap(final)).astype(F32)

        def to_all(value):
            value = across_pairs(value).astype(BF)
            value = (value.astype(F32) + core_swap(value).astype(F32)).astype(BF)
            value = (value.astype(F32) + z_near(value).astype(F32)).astype(BF)
            return value.astype(F32) + z_far(value).astype(F32)

        ffn_sum = to_owner(scatter_blocks(jnp.concatenate([grad_wgu, grad_dt], axis=1)))
        qo_sum = to_owner(scatter_blocks(jnp.concatenate([grad_wq, grad_wot], axis=1)))
        wide = [x.reshape(n_fsdp, block) for x in (dscale_ai, dscale_ao * 0.5, dscale_fi * 0.5, dscale_fo * 0.5)]
        slim = [x.reshape(n_fsdp, gain_block) for x in (dscale_q, dscale_k)]
        small = jnp.concatenate(wide + slim, axis=1)
        extra_rows = 16
        small = jnp.pad(small, ((0, 0), (0, extra_rows * 2 * HD - small.shape[1])))
        small = small.reshape(n_fsdp, extra_rows, 2 * HD)
        kv_ext = jnp.concatenate([grad_wkv.reshape(n_fsdp, block, 2 * HD), small], axis=1)
        kv_sum = to_all(scatter_blocks(kv_ext.reshape(-1, 2 * HD)))
        small_sum = kv_sum[block:].reshape(-1)
        gain_outs = []
        for i in range(4):
            gain_outs.append(small_sum[i * block : (i + 1) * block])
        for i in range(2):
            first = 4 * block + i * gain_block
            gain_outs.append(small_sum[first : first + gain_block])
        return (
            both_groups(layer_half),
            both_groups(grad_half),
            qo_sum[:, :HD],
            kv_sum[:block, :HD],
            kv_sum[:block, HD:],
            qo_sum[:, HD:].T,
            ffn_sum[:, :hidden],
            ffn_sum[:, hidden : 2 * hidden],
            ffn_sum[:, 2 * hidden :].T,
            *gain_outs,
        )

    return on_device


def solution(mesh):
    in_specs = (
        P(("fsdp", "context"), None),
        P("fsdp", None),
        P("fsdp", "tensor"),
        P("fsdp", None),
        P("fsdp", None),
        P("tensor", "fsdp"),
        P("fsdp", "tensor"),
        P("fsdp", "tensor"),
        P("tensor", "fsdp"),
        P("fsdp"),
        P("fsdp"),
        P("fsdp"),
        P("fsdp"),
        P("fsdp"),
        P("fsdp"),
        P(("fsdp", "context"), None),
    )
    out_specs = (
        P(("fsdp", "context"), None),
        P(("fsdp", "context"), None),
        P("fsdp", "tensor"),
        P("fsdp", None),
        P("fsdp", None),
        P("tensor", "fsdp"),
        P("fsdp", "tensor"),
        P("fsdp", "tensor"),
        P("tensor", "fsdp"),
        P("fsdp"),
        P("fsdp"),
        P("fsdp"),
        P("fsdp"),
        P("fsdp"),
        P("fsdp"),
    )
    on_device = make_program(mesh.shape["fsdp"], mesh.shape["context"], mesh.shape["tensor"])
    return jax.shard_map(
        on_device, mesh=mesh, in_specs=in_specs, out_specs=out_specs, check_vma=False
    )
```

```python
import math

import jax
import jax.numpy as jnp
from jax import lax
from jax.experimental import pallas as pl
from jax.experimental.pallas import tpu as pltpu
from jax.sharding import PartitionSpec as P

HD = 256

EPSILON = 1e-06
ROPE_BASE = 1000000.0
GELU_COEF = math.sqrt(2.0 / math.pi)
NEG_LARGE = -1e30
BF = jnp.bfloat16
F32 = jnp.float32
EXTRA = 16
SMALL_VMEM = 16 * 2**20
LARGE_VMEM = 48 * 2**20


def rms_stats(values):
    inverse = lax.rsqrt(jnp.mean(values * values, axis=-1, keepdims=True) + EPSILON)
    return values * inverse, inverse


def rms_back(grad_out, gain_vec, normed, inverse):
    inner = grad_out * gain_vec
    return inverse * (inner - normed * jnp.mean(inner * normed, axis=-1, keepdims=True))


def rotate(values, cosine, sine):
    half = values.shape[-1] // 2
    first, second = values[:, :half], values[:, half:]
    return jnp.concatenate(
        [first * cosine - second * sine, second * cosine + first * sine], axis=-1
    )


def gelu_parts(pre_act):
    cubic = pre_act + 0.044715 * pre_act * pre_act * pre_act
    tangent = jnp.tanh(GELU_COEF * cubic)
    gelu_val = 0.5 * pre_act * (1.0 + tangent)
    slope = 0.5 * (1.0 + tangent) + 0.5 * pre_act * (1.0 - tangent * tangent) * GELU_COEF * (
        1.0 + 3.0 * 0.044715 * pre_act * pre_act
    )
    return gelu_val, slope


def dot32(left, right):
    return jnp.dot(left, right, preferred_element_type=F32)


def dot_nt(left, right):
    return lax.dot_general(left, right, (((1,), (1,)), ((), ())), preferred_element_type=F32)


def dot_tn(left, right):
    return lax.dot_general(left, right, (((0,), (0,)), ((), ())), preferred_element_type=F32)


def shape(dims, dtype):
    return jax.ShapeDtypeStruct(dims, dtype)


def call(
    body, name, outs, args, scalars=(), raw=(), hold=(), scratch=(), flops=0, limit=SMALL_VMEM
):
    vmem = pl.BlockSpec(memory_space=pltpu.VMEM)
    smem = pl.BlockSpec(memory_space=pltpu.SMEM)
    size = sum(x.size * x.dtype.itemsize for x in list(args) + list(outs))
    n_used = len(scalars) + len(raw) + len(args)
    n_hold = len(hold)

    def wrapped(*refs):
        body(*refs[:n_used], *refs[n_used + n_hold :])

    return pl.pallas_call(
        wrapped,
        name=name,
        out_shape=tuple(outs),
        in_specs=[smem] * len(scalars)
        + [pl.BlockSpec(memory_space=pltpu.HBM)] * len(raw)
        + [vmem] * len(args)
        + [pl.BlockSpec(memory_space=pl.ANY)] * n_hold,
        out_specs=tuple(vmem for _ in outs),
        scratch_shapes=list(scratch),
        compiler_params=pltpu.CompilerParams(vmem_limit_bytes=limit),
        cost_estimate=pl.CostEstimate(flops=flops, bytes_accessed=size, transcendentals=0),
    )(*scalars, *[pltpu.with_memory_space_constraint(x, pltpu.HBM) for x in raw], *args, *hold)


def tie(value, *others):
    return lax.optimization_barrier((value,) + others)[0]


def make_program(n_fsdp, n_context, n_tensor):
    def core_swap(value):
        return lax.ppermute(value, "context", [(i, i ^ 1) for i in range(n_context)])

    def z_near(value):
        return lax.ppermute(value, "tensor", [(i, i ^ 1) for i in range(n_tensor)])

    def z_far(value):
        return lax.ppermute(value, "tensor", [(i, i ^ 2) for i in range(n_tensor)])

    def cross(value):
        pairs = []
        for ctx in range(n_context):
            for pos in range(n_tensor):
                stay = (pos // 2) == (ctx % 2)
                to = ctx * n_tensor + pos if stay else (ctx ^ 1) * n_tensor + (pos ^ 2)
                pairs.append((ctx * n_tensor + pos, to))
        return lax.ppermute(value, ("context", "tensor"), pairs)

    def fsdp_hop(value, step):
        return lax.ppermute(value, "fsdp", [(i, i ^ step) for i in range(n_fsdp)])

    def gather_blocks(value, first):
        second = 3 - first
        near = fsdp_hop(value, first)
        far = fsdp_hop(value, second)
        both = fsdp_hop(near, second)
        return [value, near, far, both] if first == 1 else [value, far, near, both]

    def across_pairs(value):
        step = 2
        while step < n_context:
            value = value.astype(F32) + lax.ppermute(
                value.astype(BF), "context", [(i, i ^ step) for i in range(n_context)]
            ).astype(F32)
            step *= 2
        return value

    def on_device(
        tokens, lengths, weight_query, weight_key, weight_value, weight_out, weight_gate,
        weight_up, weight_down, gain_attn_in, gain_attn_out, gain_ffn_in, gain_ffn_out,
        gain_query, gain_key, cotangent,
    ):
        rows, width = tokens.shape
        half = rows // 2
        stream = rows * n_context
        block = weight_query.shape[0]
        gblock = gain_query.shape[0]
        hidden = weight_gate.shape[1]
        kvw = 2 * HD
        att_scale = HD ** (-0.5)
        n_doc = lengths.shape[1]
        two = n_context == 2
        limit = SMALL_VMEM if two else LARGE_VMEM
        blk_ext = block + EXTRA

        def own_f():
            return lax.axis_index("fsdp")

        def group_start():
            return pl.multiple_of((lax.axis_index("tensor") // 2) * half, half)

        def other_start():
            return pl.multiple_of((1 - lax.axis_index("tensor") // 2) * half, half)

        def bases():
            ctx = lax.axis_index("context")
            if two:
                return ctx * rows, (ctx ^ 1) * rows
            return 0, rows

        def places():
            ctx = lax.axis_index("context")
            if two:
                return group_start(), pl.multiple_of(rows + group_start(), half)
            return (
                pl.multiple_of(ctx * rows + group_start(), half),
                pl.multiple_of((ctx ^ 1) * rows + group_start(), half),
            )

        def key_index(dims, axis):
            base0, base1 = bases()
            at = lax.broadcasted_iota(jnp.int32, dims, axis)
            return at + jnp.where(at < rows, base0, base1 - rows)

        def query_index(dims):
            ctx = lax.axis_index("context")
            at = lax.broadcasted_iota(jnp.int32, dims, 0)
            first = ctx * rows + group_start()
            second = (ctx ^ 1) * rows + group_start()
            return at + jnp.where(at < half, first, second - half)

        def doc_of(index, lens):
            segment = jnp.zeros(index.shape, jnp.int32)
            start = jnp.zeros(index.shape, jnp.int32)
            end = jnp.int32(0)
            for i in range(n_doc):
                end = end + lens[0, i]
                passed = index >= end
                segment = segment + passed.astype(jnp.int32)
                start = jnp.where(passed, end, start)
            return segment, start

        def mask_of(lens):
            key_at = key_index((1, stream), 1)
            row_at = query_index((2 * half, 1))
            key_seg, _ = doc_of(key_at, lens)
            row_seg, _ = doc_of(row_at, lens)
            return (row_seg == key_seg) & (row_at >= key_at)

        def put_blocks(dest, blocks, columns=None):
            for step in range(n_fsdp):
                at = pl.multiple_of((own_f() ^ step) * block, EXTRA)
                dest[pl.ds(at, block), :] = blocks[step][:block, :]

        def take_block(source, step, size):
            at = pl.multiple_of((own_f() ^ step) * size, EXTRA)
            return source[pl.ds(at, size), :]

        ffn_cols = 3 * hidden // 2
        split = ffn_cols - hidden

        def pack(lens, k_in, v_in, q_in, o_in, g_in, u_in, d_in, *refs):
            gains = refs[:6]
            kv_out, qo_out, f1_out, f2_out, cos_out, sin_out = refs[6:12]
            held, sems = refs[12:18], refs[18]
            moves = [
                (k_in, kv_out.at[:block, :HD]),
                (v_in, kv_out.at[:block, HD:]),
                (q_in, qo_out.at[:, :HD]),
                (o_in, qo_out.at[:, HD:]),
                (g_in, f1_out.at[:, :hidden]),
                (u_in.at[:, :split], f1_out.at[:, hidden:]),
                (u_in.at[:, split:], f2_out.at[:, : hidden - split]),
                (d_in, f2_out.at[:, hidden - split :]),
            ] + list(zip(gains, held))
            copies = [
                pltpu.make_async_copy(src, dst, sems.at[i]) for i, (src, dst) in enumerate(moves)
            ]
            for copy in copies:
                copy.start()
            at = key_index((stream, 1), 0)
            _, start = doc_of(at, lens)
            lane = lax.broadcasted_iota(jnp.int32, (1, HD // 2), 1).astype(F32)
            freqs = jnp.exp(lane * (-2.0 * math.log(ROPE_BASE) / HD))
            angles = (at - start).astype(F32) * freqs
            cos_out[...] = jnp.cos(angles)
            sin_out[...] = jnp.sin(angles)
            for copy in copies:
                copy.wait()
            row = lax.broadcasted_iota(jnp.int32, (EXTRA, block), 0)
            tile = jnp.zeros((EXTRA, block), F32)
            for i in range(4):
                tile = jnp.where(row == i, held[i][...].astype(F32)[None, :], tile)
            kv_out[block:, :] = jnp.zeros((EXTRA, kvw), BF)
            kv_out[block:, :block] = tile.astype(BF)
            row = lax.broadcasted_iota(jnp.int32, (EXTRA, gblock), 0)
            tile = jnp.zeros((EXTRA, gblock), F32)
            for i in range(2):
                tile = jnp.where(row == i, held[4 + i][...].astype(F32)[None, :], tile)
            kv_out[block:, HD : HD + gblock] = tile.astype(BF)

        pack_kv, pack_qo, pack_f1, pack_f2, cos_t, sin_t = call(
            pack, "pack",
            [
                shape((blk_ext, kvw), BF), shape((block, kvw), BF), shape((block, ffn_cols), BF),
                shape((block, ffn_cols), BF), shape((stream, HD // 2), F32),
                shape((stream, HD // 2), F32),
            ],
            [], scalars=[lengths],
            raw=[
                weight_key, weight_value, weight_query, weight_out.T, weight_gate, weight_up,
                weight_down.T, gain_attn_in, gain_attn_out, gain_ffn_in, gain_ffn_out,
                gain_query, gain_key,
            ],
            scratch=[pltpu.VMEM((block,), BF)] * 4 + [pltpu.VMEM((gblock,), BF)] * 2
            + [pltpu.SemaphoreType.DMA((14,))],
        )
        tok_parts = [tokens, core_swap(tokens)] if two else [
            lax.all_gather(tokens, "context", axis=0, tiled=True)
        ]
        cross_qo = cross(pack_qo)
        cross_f1, cross_f2 = cross(pack_f1), cross(pack_f2)
        kv_blocks = gather_blocks(pack_kv, 1)
        qo_blocks = gather_blocks(cross_qo, 2)
        f1_blocks = gather_blocks(cross_f1, 1)
        f2_blocks = gather_blocks(cross_f2, 2)

        n_tok = len(tok_parts)

        def front(lens, *refs):
            toks = refs[:n_tok]
            kvb = refs[n_tok : n_tok + 4]
            qob = refs[n_tok + 4 : n_tok + 8]
            cos_ref, sin_ref = refs[n_tok + 8 : n_tok + 10]
            (act, q_rot, k_rot, val, q_pre, k_pre, attn, logt, keep, send, gw, gs, wkv, wqo) = (
                refs[n_tok + 10 :]
            )
            put_blocks(wkv, kvb)
            put_blocks(wqo, qob)
            f = own_f()
            tiles = [b[block:, :].astype(F32) for b in kvb]
            chunks = []
            for p in range(n_fsdp):
                tile = tiles[3]
                for step in range(3):
                    tile = jnp.where(f == (p ^ step), tiles[step], tile)
                chunks.append(tile)
            wide = jnp.concatenate([t[:8, :block] for t in chunks], axis=1)
            slim = jnp.concatenate([t[:8, HD : HD + gblock] for t in chunks], axis=1)
            gw[...] = wide
            gs[...] = slim
            scale_ai, scale_q, scale_k = wide[0:1], slim[0:1], slim[1:2]
            at = 0
            for tok in toks:
                hat, _ = rms_stats(tok[...].astype(F32))
                act[at : at + tok.shape[0], :] = (hat * scale_ai).astype(BF)
                at += tok.shape[0]
            kv = dot32(act[...], wkv[...])
            k_pre[...] = kv[:, :HD]
            val[...] = kv[:, HD:].astype(BF)
            k_hat, _ = rms_stats(kv[:, :HD])
            k_rot[...] = rotate(k_hat * scale_k, cos_ref[...], sin_ref[...]).astype(BF)
            for i, place in enumerate(places()):
                mine = slice(i * half, (i + 1) * half)
                pre = dot32(act[pl.ds(place, half), :], wqo[:, :HD])
                q_pre[mine, :] = pre
                hat, _ = rms_stats(pre)
                turned = rotate(
                    hat * scale_q, cos_ref[pl.ds(place, half), :], sin_ref[pl.ds(place, half), :]
                )
                q_rot[mine, :] = (turned * att_scale).astype(BF)
            allowed = mask_of(lens)
            scores = jnp.where(allowed, dot_nt(q_rot[...], k_rot[...]), NEG_LARGE)
            row_max = jnp.max(scores, axis=1, keepdims=True)
            weights = jnp.where(allowed, jnp.exp(scores - row_max), 0.0)
            total = jnp.sum(weights, axis=1, keepdims=True)
            logt[...] = row_max + jnp.log(total)
            heads = (dot32(weights.astype(BF), val[...]) / total).astype(BF)
            attn[...] = heads
            partial = dot_nt(heads, wqo[:, HD:])
            keep[...] = partial[:half]
            send[...] = partial[half:].astype(BF)

        n_q = 2 * half
        wide_f, wide_b = shape((half, width), F32), shape((half, width), BF)
        row_f = shape((1, width), F32)
        cos_t = tie(cos_t, cross_f1, cross_f2)
        (act, q_rot, k_rot, val, q_pre, k_pre, attn, logt, keep, send, gw, gs) = call(
            front, "front",
            [
                shape((stream, width), BF), shape((n_q, HD), BF), shape((stream, HD), BF),
                shape((stream, HD), BF), shape((n_q, HD), F32), shape((stream, HD), F32),
                shape((n_q, HD), BF), shape((n_q, 1), F32), wide_f, wide_b,
                shape((8, width), F32), shape((8, HD), F32),
            ],
            tok_parts + kv_blocks + qo_blocks + [cos_t, sin_t],
            scalars=[lengths],
            scratch=[pltpu.VMEM((width, kvw), BF), pltpu.VMEM((width, kvw), BF)],
            flops=2 * stream * width * kvw + 4 * n_q * stream * HD,
            limit=limit,
        )
        saved = [q_rot, k_rot, val, q_pre, k_pre, attn, logt, gs, cos_t, sin_t, act]
        saved = (saved + [gw] + kv_blocks + qo_blocks) if two else []

        def pair_sum(kept, sent):
            return (kept + core_swap(sent).astype(F32)).astype(BF)

        def mid_one(pair, near, tok, gains, total_out, res_out, act_out):
            total = pair[...].astype(F32) + near[...].astype(F32)
            total_out[...] = total
            hat, _ = rms_stats(total)
            res = tok[pl.ds(group_start(), half), :].astype(F32) + hat * gains[1:2, :]
            res_out[...] = res
            hat, _ = rms_stats(res)
            act_out[...] = (hat * gains[2:3, :]).astype(BF)

        pair = pair_sum(keep, send)
        attn_total, hidden_res, act_own = call(
            mid_one, "mid_one", [wide_f, wide_f, wide_b], [pair, z_near(pair), tokens, gw],
            hold=saved,
        )
        act_oth = core_swap(act_own)

        def put_ffn(wgu, wd, f1, f2):
            for step in range(n_fsdp):
                at = pl.ds(pl.multiple_of((own_f() ^ step) * block, EXTRA), block)
                wgu[at, :ffn_cols] = f1[step][...]
                wgu[at, ffn_cols:] = f2[step][:, : hidden - split]
                wd[at, :] = f2[step][:, hidden - split :]

        def ffn(a0, a1, *refs):
            gu_out, inner_out, keep, send, wgu, wd = refs[8:]
            put_ffn(wgu, wd, refs[:4], refs[4:8])
            for i, a in enumerate((a0, a1)):
                mine = slice(i * half, (i + 1) * half)
                gu = dot32(a[...], wgu[...])
                gu_out[mine, :] = gu
                gelu_val, _ = gelu_parts(gu[:, :hidden])
                inner = (gelu_val * gu[:, hidden:]).astype(BF)
                inner_out[mine, :] = inner
                partial = dot_nt(inner, wd[...])
                if i == 0:
                    keep[...] = partial
                else:
                    send[...] = partial.astype(BF)

        ffn_scratch = [pltpu.VMEM((width, 2 * hidden), BF), pltpu.VMEM((width, hidden), BF)]
        ffn_flops = 6 * n_q * width * hidden
        gate_up, inner_act, keep, send = call(
            ffn, "ffn",
            [shape((n_q, 2 * hidden), F32), shape((n_q, hidden), BF), wide_f, wide_b],
            [act_own, act_oth] + f1_blocks + f2_blocks, scratch=ffn_scratch, flops=ffn_flops,
            hold=saved + ([hidden_res, attn_total] if two else []),
        )

        def mid_two(pair, near, res, cot, gains, out_ref, grad_out, ds_out):
            hat, inv = rms_stats(pair[...].astype(F32) + near[...].astype(F32))
            out_ref[...] = (res[...] + hat * gains[3:4, :]).astype(BF)
            grad = cot[pl.ds(group_start(), half), :].astype(F32)
            ds_out[...] = jnp.sum(grad * hat, axis=0, keepdims=True)
            grad_out[...] = rms_back(grad, gains[3:4, :], hat, inv).astype(BF)

        pair = pair_sum(keep, send)
        layer_own, gf_own, ds_fo = call(
            mid_two, "mid_two", [wide_b, wide_b, row_f],
            [pair, z_near(pair), hidden_res, cotangent, gw],
            hold=saved + ([attn_total, act_own, act_oth] + f1_blocks + f2_blocks if two else []),
        )
        layer_oth = z_far(layer_own)
        gf_oth = core_swap(gf_own)

        def ffn_back(f0, f1, gu_ref, *refs):
            ggu_out, keep, send, wgu, wd = refs[8:]
            put_ffn(wgu, wd, refs[:4], refs[4:8])
            for i, g in enumerate((f0, f1)):
                mine = slice(i * half, (i + 1) * half)
                grad_inner = dot32(g[...], wd[...])
                gelu_val, slope = gelu_parts(gu_ref[mine, :hidden])
                up = gu_ref[mine, hidden:]
                ggu_out[mine, :hidden] = (grad_inner * up * slope).astype(BF)
                ggu_out[mine, hidden:] = (grad_inner * gelu_val).astype(BF)
                partial = dot_nt(ggu_out[mine, :], wgu[...])
                if i == 0:
                    keep[...] = partial
                else:
                    send[...] = partial.astype(BF)

        grad_gu, keep, send = call(
            ffn_back, "ffn_back", [shape((n_q, 2 * hidden), BF), wide_f, wide_b],
            [gf_own, gf_oth, gate_up] + f1_blocks + f2_blocks,
            scratch=ffn_scratch, flops=ffn_flops,
            hold=saved + ([hidden_res, attn_total, act_own, act_oth] if two else []),
        )
        pair = pair_sum(keep, send)

        def put_grads(full, first, mine_out, give_out, size, lanes=slice(None)):
            second = 3 - first
            for i, step in enumerate((0, second)):
                mine_out[i * size : (i + 1) * size, lanes] = take_block(full, step, size)
            for i, step in enumerate((first, 3)):
                give_out[i * size : (i + 1) * size, lanes] = take_block(full, step, size)

        def ffn_weights(a0, a1, f0, f1, ggu, inner, m1, s1, m2, s2, full1, full2):
            low, high = slice(0, half), slice(half, 2 * half)
            cut = ffn_cols
            full1[...] = (
                dot_tn(a0[...], ggu[low, :cut]) + dot_tn(a1[...], ggu[high, :cut])
            ).astype(BF)
            full2[:, : hidden - split] = (
                dot_tn(a0[...], ggu[low, cut:]) + dot_tn(a1[...], ggu[high, cut:])
            ).astype(BF)
            full2[:, hidden - split :] = (
                dot_tn(f0[...], inner[low, :]) + dot_tn(f1[...], inner[high, :])
            ).astype(BF)
            put_grads(full1, 1, m1, s1, block)
            put_grads(full2, 2, m2, s2, block)

        ffn_m1, ffn_s1, ffn_m2, ffn_s2 = call(
            ffn_weights, "ffn_weights", [shape((2 * block, ffn_cols), BF)] * 4,
            [act_own, act_oth, gf_own, gf_oth, tie(grad_gu, pair), inner_act],
            scratch=[pltpu.VMEM((width, ffn_cols), BF)] * 2, flops=ffn_flops,
        )

        def mid_three(pair, near, res, tot, cot, gains, hid_out, grad_out, fi_out, ao_out):
            total = pair[...].astype(F32) + near[...].astype(F32)
            hat, inv = rms_stats(res[...])
            fi_out[...] = jnp.sum(total * hat, axis=0, keepdims=True)
            grad = cot[pl.ds(group_start(), half), :].astype(F32)
            grad = grad + rms_back(total, gains[2:3, :], hat, inv)
            hid_out[...] = grad
            hat, inv = rms_stats(tot[...])
            ao_out[...] = jnp.sum(grad * hat, axis=0, keepdims=True)
            grad_out[...] = rms_back(grad, gains[1:2, :], hat, inv).astype(BF)

        grad_hidden, ga_own, ds_fi, ds_ao = call(
            mid_three, "mid_three", [wide_f, wide_b, row_f, row_f],
            [pair, z_near(pair), hidden_res, attn_total, cotangent, gw],
            hold=saved,
        )
        ga_oth = tie(core_swap(ga_own), layer_oth)

        def attn_back(lens, *refs):
            (a0, a1, attn_r, logt_r, q_r, k_r, v_r, qp, kp, cos_ref, sin_ref, gains) = refs[:12]
            kvb, qob = refs[12:16], refs[16:20]
            gq_out, gkv_out, part_keep, part_send, dsq, dsk, wkv, wqo, part = refs[20:]
            put_blocks(wkv, kvb)
            put_blocks(wqo, qob)
            scale_q, scale_k = gains[0:1, :], gains[1:2, :]
            grad_attn = jnp.concatenate([a0[...], a1[...]], axis=0)
            grad_heads = dot32(grad_attn, wqo[:, HD:]).astype(BF)
            delta = jnp.sum(
                grad_heads.astype(F32) * attn_r[...].astype(F32), axis=1, keepdims=True
            )
            allowed = mask_of(lens)
            scores = dot_nt(q_r[...], k_r[...])
            probs = jnp.where(allowed, jnp.exp(scores - logt_r[...]), 0.0)
            grad_s = (probs * (dot_nt(grad_heads, v_r[...]) - delta)).astype(BF)
            grad_kn = rotate(dot_tn(grad_s, q_r[...]), cos_ref[...], -sin_ref[...])
            hat, inv = rms_stats(kp[...])
            dsk[...] = jnp.sum(grad_kn * hat, axis=0, keepdims=True)
            gkv_out[:, :HD] = rms_back(grad_kn, scale_k, hat, inv).astype(BF)
            gkv_out[:, HD:] = dot_tn(probs.astype(BF), grad_heads).astype(BF)
            part[...] = dot_nt(gkv_out[...], wkv[...])
            grad_qr = dot32(grad_s, k_r[...]) * att_scale
            total_q = jnp.zeros((1, HD), F32)
            for i, place in enumerate(places()):
                mine = slice(i * half, (i + 1) * half)
                grad_qn = rotate(
                    grad_qr[mine], cos_ref[pl.ds(place, half), :], -sin_ref[pl.ds(place, half), :]
                )
                hat, inv = rms_stats(qp[mine, :])
                total_q = total_q + jnp.sum(grad_qn * hat, axis=0, keepdims=True)
                gq_out[mine, :] = rms_back(grad_qn, scale_q, hat, inv).astype(BF)
                part[pl.ds(place, half), :] += dot_nt(gq_out[mine, :], wqo[:, :HD])
            dsq[...] = total_q
            part_keep[...] = part[:rows, :]
            part_send[...] = part[rows:, :].astype(BF)

        n_rest = stream - rows
        grad_q, grad_kv, part_keep, part_send, ds_q, ds_k = call(
            attn_back, "attn_back",
            [
                shape((n_q, HD), BF), shape((stream, kvw), BF), shape((rows, width), F32),
                shape((n_rest, width), BF), shape((1, HD), F32), shape((1, HD), F32),
            ],
            [ga_own, ga_oth, attn, logt, q_rot, k_rot, val, q_pre, k_pre, cos_t, sin_t, gs]
            + kv_blocks + qo_blocks,
            scalars=[lengths],
            scratch=[
                pltpu.VMEM((width, kvw), BF), pltpu.VMEM((width, kvw), BF),
                pltpu.VMEM((stream, width), F32),
            ],
            flops=2 * stream * width * kvw + 10 * n_q * stream * HD, limit=limit,
        )

        def attn_weights(*refs):
            toks = refs[:n_tok]
            (act_r, gq, gkv, a0, a1, attn_r, pk, ps, dfo, dfi, dao, dq, dk) = (
                refs[n_tok : n_tok + 13]
            )
            kv_m, kv_s, qo_m, qo_s, full, ext = refs[n_tok + 13 :]
            low, high = slice(0, half), slice(half, 2 * half)
            dai = jnp.zeros((1, width), F32)
            at = 0
            for tok in toks:
                hat, _ = rms_stats(tok[...].astype(F32))
                size = tok.shape[0]
                if size > rows:
                    dai = dai + jnp.sum(hat[:rows] * pk[...], axis=0, keepdims=True)
                    dai = dai + jnp.sum(hat[rows:] * ps[...].astype(F32), axis=0, keepdims=True)
                else:
                    piece = (pk if at == 0 else ps)[...].astype(F32)
                    dai = dai + jnp.sum(hat * piece, axis=0, keepdims=True)
                at += size
            wide = [dai, dao[...] * 0.5, dfi[...] * 0.5, dfo[...] * 0.5]
            slim = [dq[...], dk[...]]
            ext[...] = jnp.zeros(ext.shape, BF)
            row_w = lax.broadcasted_iota(jnp.int32, (EXTRA, block), 0)
            row_s = lax.broadcasted_iota(jnp.int32, (EXTRA, gblock), 0)
            for p in range(n_fsdp):
                tile = jnp.zeros((EXTRA, block), F32)
                for i, vec in enumerate(wide):
                    tile = jnp.where(row_w == i, vec[:, p * block : (p + 1) * block], tile)
                ext[p * EXTRA : (p + 1) * EXTRA, :block] = tile.astype(BF)
                tile = jnp.zeros((EXTRA, gblock), F32)
                for i, vec in enumerate(slim):
                    tile = jnp.where(row_s == i, vec[:, p * gblock : (p + 1) * gblock], tile)
                ext[p * EXTRA : (p + 1) * EXTRA, HD : HD + gblock] = tile.astype(BF)
            full[...] = dot_tn(act_r[...], gkv[...]).astype(BF)
            for out, steps in ((kv_m, (0, 2)), (kv_s, (1, 3))):
                for i, step in enumerate(steps):
                    at = i * blk_ext
                    out[at : at + block, :] = take_block(full, step, block)
                    out[at + block : at + blk_ext, :] = take_block(ext, step, EXTRA)
            place0, place1 = places()
            full[:, :HD] = (
                dot_tn(act_r[pl.ds(place0, half), :], gq[low, :])
                + dot_tn(act_r[pl.ds(place1, half), :], gq[high, :])
            ).astype(BF)
            full[:, HD:] = (
                dot_tn(a0[...], attn_r[low, :]) + dot_tn(a1[...], attn_r[high, :])
            ).astype(BF)
            put_grads(full, 2, qo_m, qo_s, block)

        kv_m, kv_s, qo_m, qo_s = call(
            attn_weights, "attn_weights",
            [shape((2 * blk_ext, kvw), BF)] * 2 + [shape((2 * block, kvw), BF)] * 2,
            tok_parts
            + [act, grad_q, grad_kv, ga_own, ga_oth, attn, part_keep, part_send]
            + [ds_fo, ds_fi, ds_ao, ds_q, ds_k],
            scratch=[pltpu.VMEM((width, kvw), BF), pltpu.VMEM((n_fsdp * EXTRA, kvw), BF)],
            flops=2 * stream * width * kvw + 4 * n_q * width * HD, limit=limit,
        )

        if two:
            mine = part_keep + core_swap(part_send).astype(F32)
        else:
            mine = lax.psum_scatter(
                jnp.concatenate([part_keep, part_send.astype(F32)], axis=0),
                "context", scatter_dimension=0, tiled=True,
            )
        mine = mine.astype(BF)
        start = (lax.axis_index("tensor") // 2) * half
        kept = lax.dynamic_slice_in_dim(mine, start, half, 0)
        give = lax.dynamic_slice_in_dim(mine, half - start, half, 0)
        kept = (kept.astype(F32) + z_far(give).astype(F32)).astype(BF)

        def last_norm(kept, near, tok, hid, gains, out):
            grad = kept[...].astype(F32) + near[...].astype(F32)
            hat, inv = rms_stats(tok[pl.ds(group_start(), half), :].astype(F32))
            out[...] = (hid[...] + rms_back(grad, gains[0:1, :], hat, inv)).astype(BF)

        (input_own,) = call(
            last_norm, "last_norm", [wide_b], [kept, z_near(kept), tokens, grad_hidden, gw]
        )

        def join(own, oth, out):
            out[pl.ds(group_start(), half), :] = own[...].astype(F32)
            out[pl.ds(other_start(), half), :] = oth[...].astype(F32)

        def both_groups(own, other, name):
            return call(join, name, [shape((rows, width), F32)], [own, other])[0]

        layer_output = both_groups(layer_own, layer_oth, "join_output")
        grad_input = both_groups(input_own, z_far(input_own), "join_grad")

        def scatter(kept, sent, first):
            size = kept.shape[0] // 2
            both = (kept.astype(F32) + fsdp_hop(sent, first).astype(F32)).astype(BF)
            last = fsdp_hop(both[size:], 3 - first)
            return across_pairs(both[:size].astype(F32) + last.astype(F32)).astype(BF)

        def finish_ffn(x1, y1, x2, y2, g_out, u_out, d_out):
            both = x1[...].astype(F32) + y1[...].astype(F32)
            g_out[...] = both[:, :hidden]
            u_out[:, :split] = both[:, hidden:]
            both = x2[...].astype(F32) + y2[...].astype(F32)
            u_out[:, split:] = both[:, : hidden - split]
            d_out[...] = both[:, hidden - split :]

        ffn_c1 = cross(scatter(ffn_m1, ffn_s1, 1))
        ffn_c2 = cross(scatter(ffn_m2, ffn_s2, 2))
        grad_gate, grad_up, grad_down = call(
            finish_ffn, "finish_ffn",
            [shape((block, hidden), F32)] * 3,
            [ffn_c1, core_swap(ffn_c1), ffn_c2, core_swap(ffn_c2)],
        )

        kv_sum = scatter(kv_m, kv_s, 1)
        qo_mine = cross(scatter(qo_m, qo_s, 2))
        for move in (core_swap, z_near):
            kv_sum = (kv_sum.astype(F32) + move(kv_sum).astype(F32)).astype(BF)

        def finish_qo(x_ref, y_ref, q_out, o_out):
            both = x_ref[...].astype(F32) + y_ref[...].astype(F32)
            q_out[...] = both[:, :HD]
            o_out[...] = both[:, HD:]

        grad_wq, grad_wo = call(
            finish_qo, "finish_qo", [shape((block, HD), F32)] * 2,
            [qo_mine, core_swap(qo_mine)],
        )

        def finish_kv(x_ref, y_ref, k_out, v_out, *gain_outs):
            both = x_ref[...].astype(F32) + y_ref[...].astype(F32)
            k_out[...] = both[:block, :HD]
            v_out[...] = both[:block, HD:]
            for i in range(4):
                gain_outs[i][...] = both[block + i : block + i + 1, :block]
            for i in range(2):
                gain_outs[4 + i][...] = both[block + i : block + i + 1, HD : HD + gblock]

        grad_wk, grad_wv, *gain_grads = call(
            finish_kv, "finish_kv",
            [shape((block, HD), F32)] * 2 + [shape((1, block), F32)] * 4 + [shape((1, gblock), F32)] * 2,
            [kv_sum, z_far(kv_sum)],
        )
        return (
            layer_output, grad_input, grad_wq, grad_wk, grad_wv, grad_wo.T,
            grad_gate, grad_up, grad_down.T, *[g.reshape(-1) for g in gain_grads],
        )

    return on_device


def solution(mesh):
    in_specs = (
        P(("fsdp", "context"), None),
        P("fsdp", None),
        P("fsdp", "tensor"),
        P("fsdp", None),
        P("fsdp", None),
        P("tensor", "fsdp"),
        P("fsdp", "tensor"),
        P("fsdp", "tensor"),
        P("tensor", "fsdp"),
        P("fsdp"),
        P("fsdp"),
        P("fsdp"),
        P("fsdp"),
        P("fsdp"),
        P("fsdp"),
        P(("fsdp", "context"), None),
    )
    out_specs = (
        P(("fsdp", "context"), None),
        P(("fsdp", "context"), None),
        P("fsdp", "tensor"),
        P("fsdp", None),
        P("fsdp", None),
        P("tensor", "fsdp"),
        P("fsdp", "tensor"),
        P("fsdp", "tensor"),
        P("tensor", "fsdp"),
        P("fsdp"),
        P("fsdp"),
        P("fsdp"),
        P("fsdp"),
        P("fsdp"),
        P("fsdp"),
    )
    on_device = make_program(mesh.shape["fsdp"], mesh.shape["context"], mesh.shape["tensor"])
    return jax.shard_map(
        on_device, mesh=mesh, in_specs=in_specs, out_specs=out_specs, check_vma=False
    )
```

```python
import math

import jax
import jax.numpy as jnp
from jax import lax
from jax.experimental import pallas as pl
from jax.experimental.pallas import tpu as pltpu
from jax.sharding import PartitionSpec as P

HD = 256

EPSILON = 1e-06
ROPE_BASE = 1000000.0
GELU_COEF = math.sqrt(2.0 / math.pi)
NEG_LARGE = -1e30
BF = jnp.bfloat16
F32 = jnp.float32
EXTRA = 16
SMALL_VMEM = 16 * 2**20
LARGE_VMEM = 48 * 2**20


def rms_stats(values):
    inverse = lax.rsqrt(jnp.mean(values * values, axis=-1, keepdims=True) + EPSILON)
    return values * inverse, inverse


def rms_back(grad_out, gain_vec, normed, inverse):
    inner = grad_out * gain_vec
    return inverse * (inner - normed * jnp.mean(inner * normed, axis=-1, keepdims=True))


def rotate(values, cosine, sine):
    half = values.shape[-1] // 2
    first, second = values[:, :half], values[:, half:]
    return jnp.concatenate(
        [first * cosine - second * sine, second * cosine + first * sine], axis=-1
    )


def gelu_parts(pre_act):
    cubic = pre_act + 0.044715 * pre_act * pre_act * pre_act
    tangent = jnp.tanh(GELU_COEF * cubic)
    gelu_val = 0.5 * pre_act * (1.0 + tangent)
    slope = 0.5 * (1.0 + tangent) + 0.5 * pre_act * (1.0 - tangent * tangent) * GELU_COEF * (
        1.0 + 3.0 * 0.044715 * pre_act * pre_act
    )
    return gelu_val, slope


def dot32(left, right):
    return jnp.dot(left, right, preferred_element_type=F32)


def dot_nt(left, right):
    return lax.dot_general(left, right, (((1,), (1,)), ((), ())), preferred_element_type=F32)


def dot_tn(left, right):
    return lax.dot_general(left, right, (((0,), (0,)), ((), ())), preferred_element_type=F32)


def shape(dims, dtype):
    return jax.ShapeDtypeStruct(dims, dtype)


def call(
    body, name, outs, args, scalars=(), raw=(), hold=(), scratch=(), flops=0, limit=SMALL_VMEM
):
    vmem = pl.BlockSpec(memory_space=pltpu.VMEM)
    smem = pl.BlockSpec(memory_space=pltpu.SMEM)
    size = sum(x.size * x.dtype.itemsize for x in list(args) + list(outs))
    n_used = len(scalars) + len(raw) + len(args)
    n_hold = len(hold)

    def wrapped(*refs):
        body(*refs[:n_used], *refs[n_used + n_hold :])

    return pl.pallas_call(
        wrapped,
        name=name,
        out_shape=tuple(outs),
        in_specs=[smem] * len(scalars)
        + [pl.BlockSpec(memory_space=pltpu.HBM)] * len(raw)
        + [vmem] * len(args)
        + [pl.BlockSpec(memory_space=pl.ANY)] * n_hold,
        out_specs=tuple(vmem for _ in outs),
        scratch_shapes=list(scratch),
        compiler_params=pltpu.CompilerParams(vmem_limit_bytes=limit),
        cost_estimate=pl.CostEstimate(flops=flops, bytes_accessed=size, transcendentals=0),
    )(*scalars, *[pltpu.with_memory_space_constraint(x, pltpu.HBM) for x in raw], *args, *hold)


def tie(value, *others):
    return lax.optimization_barrier((value,) + others)[0]


def together(*values):
    return lax.optimization_barrier(values)


def make_program(n_fsdp, n_context, n_tensor):
    def core_swap(value):
        return lax.ppermute(value, "context", [(i, i ^ 1) for i in range(n_context)])

    def z_near(value):
        return lax.ppermute(value, "tensor", [(i, i ^ 1) for i in range(n_tensor)])

    def z_far(value):
        return lax.ppermute(value, "tensor", [(i, i ^ 2) for i in range(n_tensor)])

    def cross(value):
        pairs = []
        for ctx in range(n_context):
            for pos in range(n_tensor):
                stay = (pos // 2) == (ctx % 2)
                to = ctx * n_tensor + pos if stay else (ctx ^ 1) * n_tensor + (pos ^ 2)
                pairs.append((ctx * n_tensor + pos, to))
        return lax.ppermute(value, ("context", "tensor"), pairs)

    def fsdp_hop(value, step):
        return lax.ppermute(value, "fsdp", [(i, i ^ step) for i in range(n_fsdp)])

    def gather_blocks(value, first):
        second = 3 - first
        near = fsdp_hop(value, first)
        far = fsdp_hop(value, second)
        both = fsdp_hop(near, second)
        return [value, near, far, both] if first == 1 else [value, far, near, both]

    def across_pairs(value):
        step = 2
        while step < n_context:
            value = value.astype(F32) + lax.ppermute(
                value.astype(BF), "context", [(i, i ^ step) for i in range(n_context)]
            ).astype(F32)
            step *= 2
        return value

    def on_device(
        tokens, lengths, weight_query, weight_key, weight_value, weight_out, weight_gate,
        weight_up, weight_down, gain_attn_in, gain_attn_out, gain_ffn_in, gain_ffn_out,
        gain_query, gain_key, cotangent,
    ):
        rows, width = tokens.shape
        half = rows // 2
        stream = rows * n_context
        block = weight_query.shape[0]
        gblock = gain_query.shape[0]
        hidden = weight_gate.shape[1]
        kvw = 2 * HD
        att_scale = HD ** (-0.5)
        n_doc = lengths.shape[1]
        two = n_context == 2
        limit = SMALL_VMEM if two else LARGE_VMEM
        blk_ext = block + EXTRA

        def own_f():
            return lax.axis_index("fsdp")

        def group_start():
            return pl.multiple_of((lax.axis_index("tensor") // 2) * half, half)

        def other_start():
            return pl.multiple_of((1 - lax.axis_index("tensor") // 2) * half, half)

        def bases():
            ctx = lax.axis_index("context")
            if two:
                return ctx * rows, (ctx ^ 1) * rows
            return 0, rows

        def places():
            ctx = lax.axis_index("context")
            if two:
                return group_start(), pl.multiple_of(rows + group_start(), half)
            return (
                pl.multiple_of(ctx * rows + group_start(), half),
                pl.multiple_of((ctx ^ 1) * rows + group_start(), half),
            )

        def key_index(dims, axis):
            base0, base1 = bases()
            at = lax.broadcasted_iota(jnp.int32, dims, axis)
            return at + jnp.where(at < rows, base0, base1 - rows)

        def query_index(dims):
            ctx = lax.axis_index("context")
            at = lax.broadcasted_iota(jnp.int32, dims, 0)
            first = ctx * rows + group_start()
            second = (ctx ^ 1) * rows + group_start()
            return at + jnp.where(at < half, first, second - half)

        def doc_of(index, lens):
            segment = jnp.zeros(index.shape, jnp.int32)
            start = jnp.zeros(index.shape, jnp.int32)
            end = jnp.int32(0)
            for i in range(n_doc):
                end = end + lens[0, i]
                passed = index >= end
                segment = segment + passed.astype(jnp.int32)
                start = jnp.where(passed, end, start)
            return segment, start

        def mask_of(lens):
            key_at = key_index((1, stream), 1)
            row_at = query_index((2 * half, 1))
            key_seg, _ = doc_of(key_at, lens)
            row_seg, _ = doc_of(row_at, lens)
            return (row_seg == key_seg) & (row_at >= key_at)

        def put_blocks(dest, blocks, columns=None):
            for step in range(n_fsdp):
                at = pl.multiple_of((own_f() ^ step) * block, EXTRA)
                dest[pl.ds(at, block), :] = blocks[step][:block, :]

        def take_block(source, step, size):
            at = pl.multiple_of((own_f() ^ step) * size, EXTRA)
            return source[pl.ds(at, size), :]

        ffn_cols = 3 * hidden // 2
        split = ffn_cols - hidden

        def pack(lens, k_in, v_in, q_in, o_in, g_in, u_in, d_in, *refs):
            gains = refs[:6]
            kv_out, qo_out, f1_out, f2_out, cos_out, sin_out = refs[6:12]
            held, sems = refs[12:18], refs[18]
            moves = [
                (k_in, kv_out.at[:block, :HD]),
                (v_in, kv_out.at[:block, HD:]),
                (q_in, qo_out.at[:, :HD]),
                (o_in, qo_out.at[:, HD:]),
                (g_in, f1_out.at[:, :hidden]),
                (u_in.at[:, :split], f1_out.at[:, hidden:]),
                (u_in.at[:, split:], f2_out.at[:, : hidden - split]),
                (d_in, f2_out.at[:, hidden - split :]),
            ] + list(zip(gains, held))
            copies = [
                pltpu.make_async_copy(src, dst, sems.at[i]) for i, (src, dst) in enumerate(moves)
            ]
            for copy in copies:
                copy.start()
            at = key_index((stream, 1), 0)
            _, start = doc_of(at, lens)
            lane = lax.broadcasted_iota(jnp.int32, (1, HD // 2), 1).astype(F32)
            freqs = jnp.exp(lane * (-2.0 * math.log(ROPE_BASE) / HD))
            angles = (at - start).astype(F32) * freqs
            cos_out[...] = jnp.cos(angles)
            sin_out[...] = jnp.sin(angles)
            for copy in copies:
                copy.wait()
            row = lax.broadcasted_iota(jnp.int32, (EXTRA, block), 0)
            tile = jnp.zeros((EXTRA, block), F32)
            for i in range(4):
                tile = jnp.where(row == i, held[i][...].astype(F32)[None, :], tile)
            kv_out[block:, :] = jnp.zeros((EXTRA, kvw), BF)
            kv_out[block:, :block] = tile.astype(BF)
            row = lax.broadcasted_iota(jnp.int32, (EXTRA, gblock), 0)
            tile = jnp.zeros((EXTRA, gblock), F32)
            for i in range(2):
                tile = jnp.where(row == i, held[4 + i][...].astype(F32)[None, :], tile)
            kv_out[block:, HD : HD + gblock] = tile.astype(BF)

        tok_parts = [tokens, core_swap(tokens)] if two else [
            lax.all_gather(tokens, "context", axis=0, tiled=True)
        ]
        pack_kv, pack_qo, pack_f1, pack_f2, cos_t, sin_t = call(
            pack, "pack",
            [
                shape((blk_ext, kvw), BF), shape((block, kvw), BF), shape((block, ffn_cols), BF),
                shape((block, ffn_cols), BF), shape((stream, HD // 2), F32),
                shape((stream, HD // 2), F32),
            ],
            [], scalars=[lengths],
            raw=[
                weight_key, weight_value, weight_query, weight_out.T, weight_gate, weight_up,
                weight_down.T, gain_attn_in, gain_attn_out, gain_ffn_in, gain_ffn_out,
                gain_query, gain_key,
            ],
            scratch=[pltpu.VMEM((block,), BF)] * 4 + [pltpu.VMEM((gblock,), BF)] * 2
            + [pltpu.SemaphoreType.DMA((14,))],
        )
        pack_kv, pack_qo, pack_f1, pack_f2, tok_other = together(
            pack_kv, pack_qo, pack_f1, pack_f2, tok_parts[-1]
        )
        tok_parts = tok_parts[:-1] + [tok_other]
        cross_qo = cross(pack_qo)
        cross_f1, cross_f2 = cross(pack_f1), cross(pack_f2)
        kv_blocks = gather_blocks(pack_kv, 1)
        qo_blocks = gather_blocks(cross_qo, 2)
        f1_blocks = gather_blocks(cross_f1, 1)
        f2_blocks = gather_blocks(cross_f2, 2)

        n_tok = len(tok_parts)

        n_q = 2 * half
        at_q, at_o = slice(0, n_q), slice(n_q, 2 * n_q)
        at_k = slice(2 * n_q, 2 * n_q + stream)
        at_v = slice(2 * n_q + stream, 2 * n_q + 2 * stream)
        at_g = 2 * n_q + stream

        def front(lens, *refs):
            toks = refs[:n_tok]
            kvb = refs[n_tok : n_tok + 4]
            qob = refs[n_tok + 4 : n_tok + 8]
            cos_ref, sin_ref = refs[n_tok + 8 : n_tok + 10]
            act, att_b, att_f, w_att, keep, send, gw = refs[n_tok + 10 :]
            f = own_f()
            for step in range(n_fsdp):
                at = pl.ds(pl.multiple_of((f ^ step) * block, EXTRA), block)
                w_att[at, :kvw] = kvb[step][:block, :]
                w_att[at, kvw:] = qob[step][...]
            tiles = [b[block:, :].astype(F32) for b in kvb]
            chunks = []
            for p in range(n_fsdp):
                tile = tiles[3]
                for step in range(3):
                    tile = jnp.where(f == (p ^ step), tiles[step], tile)
                chunks.append(tile)
            wide = jnp.concatenate([t[:8, :block] for t in chunks], axis=1)
            slim = jnp.concatenate([t[:8, HD : HD + gblock] for t in chunks], axis=1)
            gw[...] = wide
            att_f[at_g:, :] = slim
            scale_ai, scale_q, scale_k = wide[0:1], slim[0:1], slim[1:2]
            at = 0
            for tok in toks:
                hat, _ = rms_stats(tok[...].astype(F32))
                act[at : at + tok.shape[0], :] = (hat * scale_ai).astype(BF)
                at += tok.shape[0]
            kv = dot32(act[...], w_att[:, :kvw])
            att_f[at_k, :] = kv[:, :HD]
            att_b[at_v, :] = kv[:, HD:].astype(BF)
            k_hat, _ = rms_stats(kv[:, :HD])
            att_b[at_k, :] = rotate(k_hat * scale_k, cos_ref[...], sin_ref[...]).astype(BF)
            for i, place in enumerate(places()):
                mine = slice(i * half, (i + 1) * half)
                pre = dot32(act[pl.ds(place, half), :], w_att[:, kvw : kvw + HD])
                att_f[mine, :] = pre
                hat, _ = rms_stats(pre)
                turned = rotate(
                    hat * scale_q, cos_ref[pl.ds(place, half), :], sin_ref[pl.ds(place, half), :]
                )
                att_b[mine, :] = (turned * att_scale).astype(BF)
            allowed = mask_of(lens)
            scores = jnp.where(allowed, dot_nt(att_b[at_q, :], att_b[at_k, :]), NEG_LARGE)
            row_max = jnp.max(scores, axis=1, keepdims=True)
            weights = jnp.where(allowed, jnp.exp(scores - row_max), 0.0)
            total = jnp.sum(weights, axis=1, keepdims=True)
            att_f[at_o, :] = jnp.broadcast_to(row_max + jnp.log(total), (n_q, HD))
            heads = (dot32(weights.astype(BF), att_b[at_v, :]) / total).astype(BF)
            att_b[at_o, :] = heads
            partial = dot_nt(heads, w_att[:, kvw + HD :])
            keep[...] = partial[:half]
            send[...] = partial[half:].astype(BF)

        wide_f, wide_b = shape((half, width), F32), shape((half, width), BF)
        row_f = shape((1, width), F32)
        cos_t = tie(cos_t, cross_f1, cross_f2)
        act, att_b, att_f, w_att, keep, send, gw = call(
            front, "front",
            [
                shape((stream, width), BF), shape((2 * n_q + 2 * stream, HD), BF),
                shape((at_g + 8, HD), F32), shape((width, 2 * kvw), BF), wide_f, wide_b,
                shape((8, width), F32),
            ],
            tok_parts + kv_blocks + qo_blocks + [cos_t, sin_t],
            scalars=[lengths],
            flops=2 * stream * width * kvw + 4 * n_q * stream * HD,
            limit=limit,
        )
        saved = [att_b, att_f, cos_t, sin_t, act, gw, w_att] + tok_parts if two else []

        def pair_sum(kept, sent):
            return (kept + core_swap(sent).astype(F32)).astype(BF)

        def mid_one(pair, near, tok, gains, total_out, res_out, act_out):
            total = pair[...].astype(F32) + near[...].astype(F32)
            total_out[...] = total
            hat, _ = rms_stats(total)
            res = tok[pl.ds(group_start(), half), :].astype(F32) + hat * gains[1:2, :]
            res_out[...] = res
            hat, _ = rms_stats(res)
            act_out[...] = (hat * gains[2:3, :]).astype(BF)

        pair = pair_sum(keep, send)
        attn_total, hidden_res, act_own = call(
            mid_one, "mid_one", [wide_f, wide_f, wide_b], [pair, z_near(pair), tokens, gw],
            hold=saved,
        )
        act_oth = core_swap(act_own)

        def put_ffn(wgu, wd, f1, f2):
            for step in range(n_fsdp):
                at = pl.ds(pl.multiple_of((own_f() ^ step) * block, EXTRA), block)
                wgu[at, :ffn_cols] = f1[step][...]
                wgu[at, ffn_cols:] = f2[step][:, : hidden - split]
                wd[at, :] = f2[step][:, hidden - split :]

        def ffn(a0, a1, *refs):
            gu_out, inner_out, keep, send, wgu, wd = refs[8:]
            put_ffn(wgu, wd, refs[:4], refs[4:8])
            for i, a in enumerate((a0, a1)):
                mine = slice(i * half, (i + 1) * half)
                gu = dot32(a[...], wgu[...])
                gu_out[mine, :] = gu
                gelu_val, _ = gelu_parts(gu[:, :hidden])
                inner = (gelu_val * gu[:, hidden:]).astype(BF)
                inner_out[mine, :] = inner
                partial = dot_nt(inner, wd[...])
                if i == 0:
                    keep[...] = partial
                else:
                    send[...] = partial.astype(BF)

        ffn_flops = 6 * n_q * width * hidden
        gate_up, inner_act, keep, send, w_gu, w_d = call(
            ffn, "ffn",
            [
                shape((n_q, 2 * hidden), F32), shape((n_q, hidden), BF), wide_f, wide_b,
                shape((width, 2 * hidden), BF), shape((width, hidden), BF),
            ],
            [act_own, act_oth] + f1_blocks + f2_blocks, flops=ffn_flops,
            hold=saved + ([hidden_res, attn_total] if two else []),
        )
        kept_ffn = [attn_total, act_own, act_oth, inner_act] if two else []

        def mid_two(pair, near, res, cot, gains, out_ref, grad_out, ds_out):
            hat, inv = rms_stats(pair[...].astype(F32) + near[...].astype(F32))
            out_ref[...] = (res[...] + hat * gains[3:4, :]).astype(BF)
            grad = cot[pl.ds(group_start(), half), :].astype(F32)
            ds_out[...] = jnp.sum(grad * hat, axis=0, keepdims=True)
            grad_out[...] = rms_back(grad, gains[3:4, :], hat, inv).astype(BF)

        pair = pair_sum(keep, send)
        layer_own, gf_own, ds_fo = call(
            mid_two, "mid_two", [wide_b, wide_b, row_f],
            [pair, z_near(pair), hidden_res, cotangent, gw],
            hold=saved + kept_ffn + ([gate_up, w_gu, w_d] if two else []),
        )
        layer_oth = z_far(layer_own)
        gf_oth = core_swap(gf_own)

        def ffn_back(f0, f1, gu_ref, wgu, wd, ggu_out, keep, send):
            for i, g in enumerate((f0, f1)):
                mine = slice(i * half, (i + 1) * half)
                grad_inner = dot32(g[...], wd[...])
                gelu_val, slope = gelu_parts(gu_ref[mine, :hidden])
                up = gu_ref[mine, hidden:]
                ggu_out[mine, :hidden] = (grad_inner * up * slope).astype(BF)
                ggu_out[mine, hidden:] = (grad_inner * gelu_val).astype(BF)
                partial = dot_nt(ggu_out[mine, :], wgu[...])
                if i == 0:
                    keep[...] = partial
                else:
                    send[...] = partial.astype(BF)

        grad_gu, keep, send = call(
            ffn_back, "ffn_back", [shape((n_q, 2 * hidden), BF), wide_f, wide_b],
            [gf_own, gf_oth, gate_up, w_gu, w_d], flops=ffn_flops,
            hold=saved + kept_ffn + ([hidden_res] if two else []),
        )
        pair = pair_sum(keep, send)

        all_cols = 3 * hidden

        def ffn_weights(a0, a1, f0, f1, ggu, inner, o0, o1, o2, o3, full):
            low, high = slice(0, half), slice(half, 2 * half)
            cut = 2 * hidden
            full[:, :cut] = (dot_tn(a0[...], ggu[low, :]) + dot_tn(a1[...], ggu[high, :])).astype(BF)
            full[:, cut:] = (
                dot_tn(f0[...], inner[low, :]) + dot_tn(f1[...], inner[high, :])
            ).astype(BF)
            for step, out in enumerate((o0, o1, o2, o3)):
                out[...] = take_block(full, step, block)

        def sum_blocks(blocks):
            total = blocks[0].astype(F32)
            for piece in blocks[1:]:
                total = total + piece.astype(F32)
            return across_pairs(total).astype(BF)

        ffn_parts = call(
            ffn_weights, "ffn_weights", [shape((block, all_cols), BF)] * 4,
            [act_own, act_oth, gf_own, gf_oth, tie(grad_gu, pair), inner_act],
            scratch=[pltpu.VMEM((width, all_cols), BF)], flops=ffn_flops,
        )
        ffn_hops = [fsdp_hop(ffn_parts[step], step) for step in (1, 2, 3)]

        def mid_three(pair, near, res, tot, cot, gains, fo, hid_out, grad_out):
            total = pair[...].astype(F32) + near[...].astype(F32)
            hat, inv = rms_stats(res[...])
            hid_out[half : half + 1, :] = fo[...]
            hid_out[half + 1 : half + 2, :] = jnp.sum(total * hat, axis=0, keepdims=True)
            grad = cot[pl.ds(group_start(), half), :].astype(F32)
            grad = grad + rms_back(total, gains[2:3, :], hat, inv)
            hid_out[:half, :] = grad
            hat, inv = rms_stats(tot[...])
            hid_out[half + 2 : half + 3, :] = jnp.sum(grad * hat, axis=0, keepdims=True)
            hid_out[half + 3 : half + 8, :] = gains[0:5, :]
            grad_out[...] = rms_back(grad, gains[1:2, :], hat, inv).astype(BF)

        grad_hidden, ga_own = call(
            mid_three, "mid_three", [shape((half + 8, width), F32), wide_b],
            [pair, z_near(pair), hidden_res, attn_total, cotangent, gw, ds_fo],
            hold=saved,
        )
        ga_oth = tie(core_swap(ga_own), ffn_parts[1])

        def attn_back(lens, *refs):
            a0, a1, att_r, pre_r, cos_ref, sin_ref, w_r = refs[:7]
            gq_out, gkv_out, part_keep, part_send, dsq, dsk, part = refs[7:]
            attn_r, q_r, k_r, v_r = (att_r.at[x, :] for x in (at_o, at_q, at_k, at_v))
            qp, kp, logt_r = (pre_r.at[x, :] for x in (at_q, at_k, at_o))
            scale_q, scale_k = pre_r[at_g : at_g + 1, :], pre_r[at_g + 1 : at_g + 2, :]
            grad_attn = jnp.concatenate([a0[...], a1[...]], axis=0)
            grad_heads = dot32(grad_attn, w_r[:, kvw + HD :]).astype(BF)
            delta = jnp.sum(
                grad_heads.astype(F32) * attn_r[...].astype(F32), axis=1, keepdims=True
            )
            allowed = mask_of(lens)
            scores = dot_nt(q_r[...], k_r[...])
            probs = jnp.where(allowed, jnp.exp(scores - logt_r[:, :1]), 0.0)
            grad_s = (probs * (dot_nt(grad_heads, v_r[...]) - delta)).astype(BF)
            grad_kn = rotate(dot_tn(grad_s, q_r[...]), cos_ref[...], -sin_ref[...])
            hat, inv = rms_stats(kp[...])
            dsk[...] = jnp.sum(grad_kn * hat, axis=0, keepdims=True)
            gkv_out[:, :HD] = rms_back(grad_kn, scale_k, hat, inv).astype(BF)
            gkv_out[:, HD:] = dot_tn(probs.astype(BF), grad_heads).astype(BF)
            part[...] = dot_nt(gkv_out[...], w_r[:, :kvw])
            grad_qr = dot32(grad_s, k_r[...]) * att_scale
            total_q = jnp.zeros((1, HD), F32)
            for i, place in enumerate(places()):
                mine = slice(i * half, (i + 1) * half)
                grad_qn = rotate(
                    grad_qr[mine], cos_ref[pl.ds(place, half), :], -sin_ref[pl.ds(place, half), :]
                )
                hat, inv = rms_stats(qp[mine, :])
                total_q = total_q + jnp.sum(grad_qn * hat, axis=0, keepdims=True)
                gq_out[mine, :] = rms_back(grad_qn, scale_q, hat, inv).astype(BF)
                part[pl.ds(place, half), :] += dot_nt(gq_out[mine, :], w_r[:, kvw : kvw + HD])
            dsq[...] = total_q
            part_keep[...] = part[:rows, :]
            part_send[...] = part[rows:, :].astype(BF)

        n_rest = stream - rows
        grad_q, grad_kv, part_keep, part_send, ds_q, ds_k = call(
            attn_back, "attn_back",
            [
                shape((n_q, HD), BF), shape((stream, kvw), BF), shape((rows, width), F32),
                shape((n_rest, width), BF), shape((1, HD), F32), shape((1, HD), F32),
            ],
            [ga_own, ga_oth, att_b, att_f, cos_t, sin_t, w_att],
            scalars=[lengths],
            scratch=[pltpu.VMEM((stream, width), F32)],
            hold=[act, grad_hidden] + tok_parts if two else [],
            flops=2 * stream * width * kvw + 10 * n_q * stream * HD, limit=limit,
        )

        quarter = half // 2

        def near_at():
            return lax.axis_index("tensor") % 2

        def share(kept, recv, keep_out, give_out):
            for g in range(2):
                to = slice(g * quarter, (g + 1) * quarter)
                for out, which in ((keep_out, near_at()), (give_out, 1 - near_at())):
                    at = pl.ds(pl.multiple_of(g * half + which * quarter, quarter), quarter)
                    out[to, :] = (kept[at, :] + recv[at, :].astype(F32)).astype(BF)

        if two:
            part_recv = core_swap(part_send)
            part_mine = part_keep
        else:
            part_mine = lax.psum_scatter(
                jnp.concatenate([part_keep, part_send.astype(F32)], axis=0),
                "context", scatter_dimension=0, tiled=True,
            )
            part_recv = jnp.zeros((rows, width), BF)
        row_keep, row_give = call(share, "share_rows", [wide_b, wide_b], [part_mine, part_recv])

        def attn_weights(*refs):
            toks = refs[:n_tok]
            act_r, gq, gkv, a0, a1, att_r, pk, ps, hid, dq, dk = refs[n_tok : n_tok + 11]
            kv_k, kv_s, qo_m, qo_s, full, ext = refs[n_tok + 11 :]
            attn_r = att_r.at[at_o, :]
            low, high = slice(0, half), slice(half, 2 * half)
            dai = jnp.zeros((1, width), F32)
            at = 0
            for tok in toks:
                hat, _ = rms_stats(tok[...].astype(F32))
                size = tok.shape[0]
                if size > rows:
                    dai = dai + jnp.sum(hat[:rows] * pk[...], axis=0, keepdims=True)
                    dai = dai + jnp.sum(hat[rows:] * ps[...].astype(F32), axis=0, keepdims=True)
                else:
                    piece = (pk if at == 0 else ps)[...].astype(F32)
                    dai = dai + jnp.sum(hat * piece, axis=0, keepdims=True)
                at += size
            wide = [dai] + [hid[half + i : half + i + 1, :] * 0.5 for i in (2, 1, 0)]
            slim = [dq[...], dk[...]]
            ext[...] = jnp.zeros(ext.shape, BF)
            row_w = lax.broadcasted_iota(jnp.int32, (EXTRA, block), 0)
            row_s = lax.broadcasted_iota(jnp.int32, (EXTRA, gblock), 0)
            for p in range(n_fsdp):
                tile = jnp.zeros((EXTRA, block), F32)
                for i, vec in enumerate(wide):
                    tile = jnp.where(row_w == i, vec[:, p * block : (p + 1) * block], tile)
                ext[p * EXTRA : (p + 1) * EXTRA, :block] = tile.astype(BF)
                tile = jnp.zeros((EXTRA, gblock), F32)
                for i, vec in enumerate(slim):
                    tile = jnp.where(row_s == i, vec[:, p * gblock : (p + 1) * gblock], tile)
                ext[p * EXTRA : (p + 1) * EXTRA, HD : HD + gblock] = tile.astype(BF)
            full[...] = dot_tn(act_r[...], gkv[...]).astype(BF)
            core = lax.axis_index("context") % 2
            for out, side in ((kv_k, core), (kv_s, 1 - core)):
                lanes = pl.ds(pl.multiple_of(side * HD, HD), HD)
                for i, step in enumerate((0, 2, 1, 3)):
                    at = i * blk_ext
                    from_row = pl.multiple_of((own_f() ^ step) * block, EXTRA)
                    out[at : at + block, :] = full[pl.ds(from_row, block), lanes]
                    from_row = pl.multiple_of((own_f() ^ step) * EXTRA, EXTRA)
                    out[at + block : at + blk_ext, :] = ext[pl.ds(from_row, EXTRA), lanes]
            place0, place1 = places()
            full[:, :HD] = (
                dot_tn(act_r[pl.ds(place0, half), :], gq[low, :])
                + dot_tn(act_r[pl.ds(place1, half), :], gq[high, :])
            ).astype(BF)
            full[:, HD:] = (
                dot_tn(a0[...], attn_r[low, :]) + dot_tn(a1[...], attn_r[high, :])
            ).astype(BF)
            for out, steps in ((qo_m, (0, 1)), (qo_s, (2, 3))):
                for i, step in enumerate(steps):
                    out[i * block : (i + 1) * block, :] = take_block(full, step, block)

        kv_k, kv_s, qo_m, qo_s = call(
            attn_weights, "attn_weights",
            [shape((4 * blk_ext, HD), BF)] * 2 + [shape((2 * block, kvw), BF)] * 2,
            tok_parts
            + [act, tie(grad_q, row_keep), grad_kv, ga_own, ga_oth, att_b]
            + [part_keep, part_send, grad_hidden, ds_q, ds_k],
            scratch=[pltpu.VMEM((width, kvw), BF), pltpu.VMEM((n_fsdp * EXTRA, kvw), BF)],
            flops=2 * stream * width * kvw + 4 * n_q * width * HD, limit=limit,
        )

        def add(x, y):
            return (x.astype(F32) + y.astype(F32)).astype(BF)

        def last_add(both, hop):
            size = both.shape[0] // 2
            return across_pairs(both[:size].astype(F32) + hop.astype(F32)).astype(BF)

        row_near = z_near(row_give)
        kv_recv = core_swap(kv_s)
        row_near, kv_recv = together(row_near, kv_recv)
        kv_both = add(kv_k[: 2 * blk_ext], kv_recv[: 2 * blk_ext])
        kv_h1 = fsdp_hop(add(kv_k[2 * blk_ext :], kv_recv[2 * blk_ext :]), 1)
        qo_h1 = fsdp_hop(qo_s, 2)

        def halve(kept, recv, keep_out, give_out):
            group = lax.axis_index("tensor") // 2
            for out, which in ((keep_out, group), (give_out, 1 - group)):
                at = pl.ds(pl.multiple_of(which * quarter, quarter), quarter)
                out[...] = (kept[at, :].astype(F32) + recv[at, :].astype(F32)).astype(BF)

        small_b = shape((quarter, width), BF)
        row_mine, row_far = call(halve, "halve_rows", [small_b, small_b], [row_keep, row_near])
        row_far = z_far(row_far)
        row_far, kv_h1, qo_h1, layer_oth, *ffn_hops = together(
            row_far, kv_h1, qo_h1, layer_oth, *ffn_hops
        )
        ffn_mine = cross(sum_blocks([ffn_parts[0]] + ffn_hops))
        kv_both = add(kv_both, kv_h1)
        kv_h2 = fsdp_hop(kv_both[blk_ext:], 2)
        qo_both = add(qo_m, qo_h1)
        qo_h2 = fsdp_hop(qo_both[block:], 1)

        def last_norm(kept, recv, tok, hid, out):
            grad = kept[...].astype(F32) + recv[...].astype(F32)
            inner = pl.multiple_of(near_at() * quarter, quarter)
            at = pl.multiple_of(group_start() + inner, quarter)
            hat, inv = rms_stats(tok[pl.ds(at, quarter), :].astype(F32))
            hidden_part = hid[pl.ds(inner, quarter), :]
            gain = hid[half + 3 : half + 4, :]
            out[...] = (hidden_part + rms_back(grad, gain, hat, inv)).astype(BF)

        (row_done,) = call(
            last_norm, "last_norm", [small_b], [row_mine, row_far, tokens, grad_hidden]
        )
        row_fars, row_nears = z_far(row_done), z_near(row_done)
        row_fars, row_nears, kv_h2, qo_h2 = together(row_fars, row_nears, kv_h2, qo_h2)
        row_both = z_near(row_fars)
        kv_sum = last_add(kv_both, kv_h2)
        kv_n = z_near(kv_sum)
        qo_c = cross(last_add(qo_both, qo_h2))
        row_both, kv_n, ffn_mine = together(row_both, kv_n, ffn_mine)
        kv_sum = add(kv_sum, kv_n)
        kv_sum = add(kv_sum, z_far(kv_sum))
        kv_other = core_swap(kv_sum)

        qo_x, ffn_x = core_swap(qo_c), core_swap(ffn_mine)

        def finish(
            l0, l1, r0, r1, r2, r3, qx, qy, fx, fy, kx, ky,
            layer_out, in_out, q_out, k_out, v_out, o_out, g_out, u_out, d_out, *gain_outs,
        ):
            layer_out[pl.ds(group_start(), half), :] = l0[...].astype(F32)
            layer_out[pl.ds(other_start(), half), :] = l1[...].astype(F32)
            group, near = lax.axis_index("tensor") // 2, near_at()
            for ref, g, n in (
                (r0, group, near), (r1, group, 1 - near),
                (r2, 1 - group, near), (r3, 1 - group, 1 - near),
            ):
                at = pl.multiple_of(g * half + n * quarter, quarter)
                in_out[pl.ds(at, quarter), :] = ref[...].astype(F32)
            q_out[...] = qx[:, :HD].astype(F32) + qy[:, :HD].astype(F32)
            o_out[...] = qx[:, HD:].astype(F32) + qy[:, HD:].astype(F32)
            for i, out in enumerate((g_out, u_out, d_out)):
                cols = slice(i * hidden, (i + 1) * hidden)
                out[...] = fx[:, cols].astype(F32) + fy[:, cols].astype(F32)
            first = lax.axis_index("context") % 2 == 0
            mine, other = kx[...].astype(F32), ky[...].astype(F32)
            left = jnp.where(first, mine, other)
            right = jnp.where(first, other, mine)
            k_out[...] = left[:block]
            v_out[...] = right[:block]
            for i in range(4):
                gain_outs[i][...] = left[block + i : block + i + 1, :block]
            for i in range(2):
                gain_outs[4 + i][...] = right[block + i : block + i + 1, :gblock]

        (
            layer_output, grad_input, grad_wq, grad_wk, grad_wv, grad_wo,
            grad_gate, grad_up, grad_down, *gain_grads,
        ) = call(
            finish, "finish",
            [shape((rows, width), F32)] * 2 + [shape((block, HD), F32)] * 4
            + [shape((block, hidden), F32)] * 3 + [shape((1, block), F32)] * 4
            + [shape((1, gblock), F32)] * 2,
            [
                layer_own, layer_oth, row_done, row_nears, row_fars, row_both,
                qo_c, qo_x, ffn_mine, ffn_x, kv_sum, kv_other,
            ],
        )
        return (
            layer_output, grad_input, grad_wq, grad_wk, grad_wv, grad_wo.T,
            grad_gate, grad_up, grad_down.T, *[g.reshape(-1) for g in gain_grads],
        )

    return on_device


def solution(mesh):
    in_specs = (
        P(("fsdp", "context"), None),
        P("fsdp", None),
        P("fsdp", "tensor"),
        P("fsdp", None),
        P("fsdp", None),
        P("tensor", "fsdp"),
        P("fsdp", "tensor"),
        P("fsdp", "tensor"),
        P("tensor", "fsdp"),
        P("fsdp"),
        P("fsdp"),
        P("fsdp"),
        P("fsdp"),
        P("fsdp"),
        P("fsdp"),
        P(("fsdp", "context"), None),
    )
    out_specs = (
        P(("fsdp", "context"), None),
        P(("fsdp", "context"), None),
        P("fsdp", "tensor"),
        P("fsdp", None),
        P("fsdp", None),
        P("tensor", "fsdp"),
        P("fsdp", "tensor"),
        P("fsdp", "tensor"),
        P("tensor", "fsdp"),
        P("fsdp"),
        P("fsdp"),
        P("fsdp"),
        P("fsdp"),
        P("fsdp"),
        P("fsdp"),
    )
    on_device = make_program(mesh.shape["fsdp"], mesh.shape["context"], mesh.shape["tensor"])
    return jax.shard_map(
        on_device, mesh=mesh, in_specs=in_specs, out_specs=out_specs, check_vma=False
    )
```

```python
import math

import jax
import jax.numpy as jnp
from jax import lax
from jax.experimental import pallas as pl
from jax.experimental.pallas import tpu as pltpu
from jax.sharding import PartitionSpec as P

HD = 256

EPSILON = 1e-06
ROPE_BASE = 1000000.0
GELU_COEF = math.sqrt(2.0 / math.pi)
NEG_LARGE = -1e30
BF = jnp.bfloat16
F32 = jnp.float32
EXTRA = 16
SMALL_VMEM = 16 * 2**20
LARGE_VMEM = 48 * 2**20


def rms_stats(values):
    inverse = lax.rsqrt(jnp.mean(values * values, axis=-1, keepdims=True) + EPSILON)
    return values * inverse, inverse


def rms_back(grad_out, gain_vec, normed, inverse):
    inner = grad_out * gain_vec
    return inverse * (inner - normed * jnp.mean(inner * normed, axis=-1, keepdims=True))


def rotate(values, cosine, sine):
    half = values.shape[-1] // 2
    first, second = values[:, :half], values[:, half:]
    return jnp.concatenate(
        [first * cosine - second * sine, second * cosine + first * sine], axis=-1
    )


def gelu_parts(pre_act):
    cubic = pre_act + 0.044715 * pre_act * pre_act * pre_act
    tangent = jnp.tanh(GELU_COEF * cubic)
    gelu_val = 0.5 * pre_act * (1.0 + tangent)
    slope = 0.5 * (1.0 + tangent) + 0.5 * pre_act * (1.0 - tangent * tangent) * GELU_COEF * (
        1.0 + 3.0 * 0.044715 * pre_act * pre_act
    )
    return gelu_val, slope


def dot32(left, right):
    return jnp.dot(left, right, preferred_element_type=F32)


def dot_nt(left, right):
    return lax.dot_general(left, right, (((1,), (1,)), ((), ())), preferred_element_type=F32)


def dot_tn(left, right):
    return lax.dot_general(left, right, (((0,), (0,)), ((), ())), preferred_element_type=F32)


def shape(dims, dtype):
    return jax.ShapeDtypeStruct(dims, dtype)


def call(
    body, name, outs, args, scalars=(), raw=(), hold=(), scratch=(), flops=0, limit=SMALL_VMEM
):
    vmem = pl.BlockSpec(memory_space=pltpu.VMEM)
    smem = pl.BlockSpec(memory_space=pltpu.SMEM)
    size = sum(x.size * x.dtype.itemsize for x in list(args) + list(outs))
    n_used = len(scalars) + len(raw) + len(args)
    n_hold = len(hold)

    def wrapped(*refs):
        body(*refs[:n_used], *refs[n_used + n_hold :])

    return pl.pallas_call(
        wrapped,
        name=name,
        out_shape=tuple(outs),
        in_specs=[smem] * len(scalars)
        + [pl.BlockSpec(memory_space=pltpu.HBM)] * len(raw)
        + [vmem] * len(args)
        + [pl.BlockSpec(memory_space=pl.ANY)] * n_hold,
        out_specs=tuple(vmem for _ in outs),
        scratch_shapes=list(scratch),
        compiler_params=pltpu.CompilerParams(vmem_limit_bytes=limit),
        cost_estimate=pl.CostEstimate(flops=flops, bytes_accessed=size, transcendentals=0),
    )(*scalars, *[pltpu.with_memory_space_constraint(x, pltpu.HBM) for x in raw], *args, *hold)


def tie(value, *others):
    return lax.optimization_barrier((value,) + others)[0]


def together(*values):
    return lax.optimization_barrier(values)


def make_program(n_fsdp, n_context, n_tensor):
    def core_swap(value):
        return lax.ppermute(value, "context", [(i, i ^ 1) for i in range(n_context)])

    def z_near(value):
        return lax.ppermute(value, "tensor", [(i, i ^ 1) for i in range(n_tensor)])

    def z_far(value):
        return lax.ppermute(value, "tensor", [(i, i ^ 2) for i in range(n_tensor)])

    def cross(value):
        pairs = []
        for ctx in range(n_context):
            for pos in range(n_tensor):
                stay = (pos // 2) == (ctx % 2)
                to = ctx * n_tensor + pos if stay else (ctx ^ 1) * n_tensor + (pos ^ 2)
                pairs.append((ctx * n_tensor + pos, to))
        return lax.ppermute(value, ("context", "tensor"), pairs)

    def fsdp_hop(value, step):
        return lax.ppermute(value, "fsdp", [(i, i ^ step) for i in range(n_fsdp)])

    def gather_blocks(value, first):
        second = 3 - first
        near = fsdp_hop(value, first)
        far = fsdp_hop(value, second)
        both = fsdp_hop(near, second)
        return [value, near, far, both] if first == 1 else [value, far, near, both]

    def across_pairs(value):
        step = 2
        while step < n_context:
            value = value.astype(F32) + lax.ppermute(
                value.astype(BF), "context", [(i, i ^ step) for i in range(n_context)]
            ).astype(F32)
            step *= 2
        return value

    def on_device(
        tokens, lengths, weight_query, weight_key, weight_value, weight_out, weight_gate,
        weight_up, weight_down, gain_attn_in, gain_attn_out, gain_ffn_in, gain_ffn_out,
        gain_query, gain_key, cotangent,
    ):
        rows, width = tokens.shape
        half = rows // 2
        stream = rows * n_context
        block = weight_query.shape[0]
        gblock = gain_query.shape[0]
        hidden = weight_gate.shape[1]
        kvw = 2 * HD
        att_scale = HD ** (-0.5)
        n_doc = lengths.shape[1]
        two = n_context == 2
        limit = SMALL_VMEM if two else LARGE_VMEM
        blk_ext = block + EXTRA

        def own_f():
            return lax.axis_index("fsdp")

        def group_start():
            return pl.multiple_of((lax.axis_index("tensor") // 2) * half, half)

        def other_start():
            return pl.multiple_of((1 - lax.axis_index("tensor") // 2) * half, half)

        def bases():
            ctx = lax.axis_index("context")
            if two:
                return ctx * rows, (ctx ^ 1) * rows
            return 0, rows

        def places():
            ctx = lax.axis_index("context")
            if two:
                return group_start(), pl.multiple_of(rows + group_start(), half)
            return (
                pl.multiple_of(ctx * rows + group_start(), half),
                pl.multiple_of((ctx ^ 1) * rows + group_start(), half),
            )

        def key_index(dims, axis):
            base0, base1 = bases()
            at = lax.broadcasted_iota(jnp.int32, dims, axis)
            return at + jnp.where(at < rows, base0, base1 - rows)

        def query_index(dims):
            ctx = lax.axis_index("context")
            at = lax.broadcasted_iota(jnp.int32, dims, 0)
            first = ctx * rows + group_start()
            second = (ctx ^ 1) * rows + group_start()
            return at + jnp.where(at < half, first, second - half)

        def doc_of(index, lens):
            segment = jnp.zeros(index.shape, jnp.int32)
            start = jnp.zeros(index.shape, jnp.int32)
            end = jnp.int32(0)
            for i in range(n_doc):
                end = end + lens[0, i]
                passed = index >= end
                segment = segment + passed.astype(jnp.int32)
                start = jnp.where(passed, end, start)
            return segment, start

        def mask_of(lens):
            key_at = key_index((1, stream), 1)
            row_at = query_index((2 * half, 1))
            key_seg, _ = doc_of(key_at, lens)
            row_seg, _ = doc_of(row_at, lens)
            return (row_seg == key_seg) & (row_at >= key_at)

        def put_blocks(dest, blocks, columns=None):
            for step in range(n_fsdp):
                at = pl.multiple_of((own_f() ^ step) * block, EXTRA)
                dest[pl.ds(at, block), :] = blocks[step][:block, :]

        def take_block(source, step, size):
            at = pl.multiple_of((own_f() ^ step) * size, EXTRA)
            return source[pl.ds(at, size), :]

        ffn_cols = 3 * hidden // 2
        split = ffn_cols - hidden

        def pack(lens, k_in, v_in, q_in, o_in, g_in, u_in, d_in, *refs):
            gains = refs[:6]
            kv_out, qo_out, f1_out, f2_out, cos_out, sin_out = refs[6:12]
            held, sems = refs[12:18], refs[18]
            moves = [
                (k_in, kv_out.at[:block, :HD]),
                (v_in, kv_out.at[:block, HD:]),
                (q_in, qo_out.at[:, :HD]),
                (o_in, qo_out.at[:, HD:]),
                (g_in, f1_out.at[:, :hidden]),
                (u_in.at[:, :split], f1_out.at[:, hidden:]),
                (u_in.at[:, split:], f2_out.at[:, : hidden - split]),
                (d_in, f2_out.at[:, hidden - split :]),
            ] + list(zip(gains, held))
            copies = [
                pltpu.make_async_copy(src, dst, sems.at[i]) for i, (src, dst) in enumerate(moves)
            ]
            for copy in copies:
                copy.start()
            at = key_index((stream, 1), 0)
            _, start = doc_of(at, lens)
            lane = lax.broadcasted_iota(jnp.int32, (1, HD // 2), 1).astype(F32)
            freqs = jnp.exp(lane * (-2.0 * math.log(ROPE_BASE) / HD))
            angles = (at - start).astype(F32) * freqs
            cos_out[...] = jnp.cos(angles)
            sin_out[...] = jnp.sin(angles)
            for copy in copies:
                copy.wait()
            row = lax.broadcasted_iota(jnp.int32, (EXTRA, block), 0)
            tile = jnp.zeros((EXTRA, block), F32)
            for i in range(4):
                tile = jnp.where(row == i, held[i][...].astype(F32)[None, :], tile)
            kv_out[block:, :] = jnp.zeros((EXTRA, kvw), BF)
            kv_out[block:, :block] = tile.astype(BF)
            row = lax.broadcasted_iota(jnp.int32, (EXTRA, gblock), 0)
            tile = jnp.zeros((EXTRA, gblock), F32)
            for i in range(2):
                tile = jnp.where(row == i, held[4 + i][...].astype(F32)[None, :], tile)
            kv_out[block:, HD : HD + gblock] = tile.astype(BF)

        tok_parts = [tokens, core_swap(tokens)] if two else [
            lax.all_gather(tokens, "context", axis=0, tiled=True)
        ]
        pack_kv, pack_qo, pack_f1, pack_f2, cos_t, sin_t = call(
            pack, "pack",
            [
                shape((blk_ext, kvw), BF), shape((block, kvw), BF), shape((block, ffn_cols), BF),
                shape((block, ffn_cols), BF), shape((stream, HD // 2), F32),
                shape((stream, HD // 2), F32),
            ],
            [], scalars=[lengths],
            raw=[
                weight_key, weight_value, weight_query, weight_out.T, weight_gate, weight_up,
                weight_down.T, gain_attn_in, gain_attn_out, gain_ffn_in, gain_ffn_out,
                gain_query, gain_key,
            ],
            scratch=[pltpu.VMEM((block,), BF)] * 4 + [pltpu.VMEM((gblock,), BF)] * 2
            + [pltpu.SemaphoreType.DMA((14,))],
        )
        pack_kv, pack_qo, pack_f1, pack_f2, tok_other = together(
            pack_kv, pack_qo, pack_f1, pack_f2, tok_parts[-1]
        )
        tok_parts = tok_parts[:-1] + [tok_other]
        cross_qo = cross(pack_qo)
        cross_f1, cross_f2 = cross(pack_f1), cross(pack_f2)
        kv_blocks = gather_blocks(pack_kv, 1)
        qo_blocks = gather_blocks(cross_qo, 2)
        f1_blocks = gather_blocks(cross_f1, 1)
        f2_blocks = gather_blocks(cross_f2, 2)

        n_tok = len(tok_parts)

        n_q = 2 * half
        at_q, at_o = slice(0, n_q), slice(n_q, 2 * n_q)
        at_k = slice(2 * n_q, 2 * n_q + stream)
        at_v = slice(2 * n_q + stream, 2 * n_q + 2 * stream)
        at_g = 2 * n_q + stream

        def front(lens, *refs):
            toks = refs[:n_tok]
            kvb = refs[n_tok : n_tok + 4]
            qob = refs[n_tok + 4 : n_tok + 8]
            cos_ref, sin_ref = refs[n_tok + 8 : n_tok + 10]
            act, att_b, att_f, w_att, keep, send, gw = refs[n_tok + 10 :]
            f = own_f()
            for step in range(n_fsdp):
                at = pl.ds(pl.multiple_of((f ^ step) * block, EXTRA), block)
                w_att[at, :kvw] = kvb[step][:block, :]
                w_att[at, kvw:] = qob[step][...]
            tiles = [b[block:, :].astype(F32) for b in kvb]
            chunks = []
            for p in range(n_fsdp):
                tile = tiles[3]
                for step in range(3):
                    tile = jnp.where(f == (p ^ step), tiles[step], tile)
                chunks.append(tile)
            wide = jnp.concatenate([t[:8, :block] for t in chunks], axis=1)
            slim = jnp.concatenate([t[:8, HD : HD + gblock] for t in chunks], axis=1)
            gw[...] = wide
            att_f[at_g:, :] = slim
            scale_ai, scale_q, scale_k = wide[0:1], slim[0:1], slim[1:2]
            at = 0
            for tok in toks:
                hat, _ = rms_stats(tok[...].astype(F32))
                act[at : at + tok.shape[0], :] = (hat * scale_ai).astype(BF)
                at += tok.shape[0]
            kv = dot32(act[...], w_att[:, :kvw])
            att_f[at_k, :] = kv[:, :HD]
            att_b[at_v, :] = kv[:, HD:].astype(BF)
            k_hat, _ = rms_stats(kv[:, :HD])
            att_b[at_k, :] = rotate(k_hat * scale_k, cos_ref[...], sin_ref[...]).astype(BF)
            for i, place in enumerate(places()):
                mine = slice(i * half, (i + 1) * half)
                pre = dot32(act[pl.ds(place, half), :], w_att[:, kvw : kvw + HD])
                att_f[mine, :] = pre
                hat, _ = rms_stats(pre)
                turned = rotate(
                    hat * scale_q, cos_ref[pl.ds(place, half), :], sin_ref[pl.ds(place, half), :]
                )
                att_b[mine, :] = (turned * att_scale).astype(BF)
            allowed = mask_of(lens)
            scores = jnp.where(allowed, dot_nt(att_b[at_q, :], att_b[at_k, :]), NEG_LARGE)
            row_max = jnp.max(scores, axis=1, keepdims=True)
            weights = jnp.where(allowed, jnp.exp(scores - row_max), 0.0)
            total = jnp.sum(weights, axis=1, keepdims=True)
            att_f[at_o, :] = jnp.broadcast_to(row_max + jnp.log(total), (n_q, HD))
            heads = (dot32(weights.astype(BF), att_b[at_v, :]) / total).astype(BF)
            att_b[at_o, :] = heads
            partial = dot_nt(heads, w_att[:, kvw + HD :])
            keep[...] = partial[:half]
            send[...] = partial[half:].astype(BF)

        wide_f, wide_b = shape((half, width), F32), shape((half, width), BF)
        row_f = shape((1, width), F32)
        act, att_b, att_f, w_att, keep, send, gw = call(
            front, "front",
            [
                shape((stream, width), BF), shape((2 * n_q + 2 * stream, HD), BF),
                shape((at_g + 8, HD), F32), shape((width, 2 * kvw), BF), wide_f, wide_b,
                shape((8, width), F32),
            ],
            tok_parts + kv_blocks + qo_blocks + [cos_t, sin_t],
            scalars=[lengths],
            flops=2 * stream * width * kvw + 4 * n_q * stream * HD,
            limit=limit,
        )
        saved = [att_b, att_f, cos_t, sin_t, act, gw, w_att] + tok_parts if two else []

        def pair_sum(kept, sent):
            return (kept + core_swap(sent).astype(F32)).astype(BF)

        def mid_one(pair, near, tok, gains, total_out, res_out, act_out):
            total = pair[...].astype(F32) + near[...].astype(F32)
            total_out[...] = total
            hat, _ = rms_stats(total)
            res = tok[pl.ds(group_start(), half), :].astype(F32) + hat * gains[1:2, :]
            res_out[...] = res
            hat, _ = rms_stats(res)
            act_out[...] = (hat * gains[2:3, :]).astype(BF)

        pair = pair_sum(keep, send)
        attn_total, hidden_res, act_own = call(
            mid_one, "mid_one", [wide_f, wide_f, wide_b], [pair, z_near(pair), tokens, gw],
            hold=saved,
        )
        act_oth = core_swap(act_own)

        def put_ffn(wgu, wd, f1, f2):
            for step in range(n_fsdp):
                at = pl.ds(pl.multiple_of((own_f() ^ step) * block, EXTRA), block)
                wgu[at, :ffn_cols] = f1[step][...]
                wgu[at, ffn_cols:] = f2[step][:, : hidden - split]
                wd[at, :] = f2[step][:, hidden - split :]

        def ffn(a0, a1, *refs):
            gu_out, inner_out, keep, send, wgu, wd = refs[8:]
            put_ffn(wgu, wd, refs[:4], refs[4:8])
            for i, a in enumerate((a0, a1)):
                mine = slice(i * half, (i + 1) * half)
                gu = dot32(a[...], wgu[...])
                gu_out[mine, :] = gu
                gelu_val, _ = gelu_parts(gu[:, :hidden])
                inner = (gelu_val * gu[:, hidden:]).astype(BF)
                inner_out[mine, :] = inner
                partial = dot_nt(inner, wd[...])
                if i == 0:
                    keep[...] = partial
                else:
                    send[...] = partial.astype(BF)

        ffn_flops = 6 * n_q * width * hidden
        gate_up, inner_act, keep, send, w_gu, w_d = call(
            ffn, "ffn",
            [
                shape((n_q, 2 * hidden), F32), shape((n_q, hidden), BF), wide_f, wide_b,
                shape((width, 2 * hidden), BF), shape((width, hidden), BF),
            ],
            [act_own, act_oth] + f1_blocks + f2_blocks, flops=ffn_flops,
            hold=saved + ([hidden_res, attn_total] if two else []),
        )
        kept_ffn = [attn_total, act_own, act_oth, inner_act] if two else []

        def mid_two(pair, near, res, cot, gains, out_ref, grad_out, ds_out):
            hat, inv = rms_stats(pair[...].astype(F32) + near[...].astype(F32))
            out_ref[...] = (res[...] + hat * gains[3:4, :]).astype(BF)
            grad = cot[pl.ds(group_start(), half), :].astype(F32)
            ds_out[...] = jnp.sum(grad * hat, axis=0, keepdims=True)
            grad_out[...] = rms_back(grad, gains[3:4, :], hat, inv).astype(BF)

        pair = pair_sum(keep, send)
        layer_own, gf_own, ds_fo = call(
            mid_two, "mid_two", [wide_b, wide_b, row_f],
            [pair, z_near(pair), hidden_res, cotangent, gw],
            hold=saved + kept_ffn + ([gate_up, w_gu, w_d] if two else []),
        )
        layer_oth = z_far(layer_own)
        gf_oth = core_swap(gf_own)

        def ffn_back(f0, f1, gu_ref, wgu, wd, ggu_out, keep, send):
            for i, g in enumerate((f0, f1)):
                mine = slice(i * half, (i + 1) * half)
                grad_inner = dot32(g[...], wd[...])
                gelu_val, slope = gelu_parts(gu_ref[mine, :hidden])
                up = gu_ref[mine, hidden:]
                ggu_out[mine, :hidden] = (grad_inner * up * slope).astype(BF)
                ggu_out[mine, hidden:] = (grad_inner * gelu_val).astype(BF)
                partial = dot_nt(ggu_out[mine, :], wgu[...])
                if i == 0:
                    keep[...] = partial
                else:
                    send[...] = partial.astype(BF)

        grad_gu, keep, send = call(
            ffn_back, "ffn_back", [shape((n_q, 2 * hidden), BF), wide_f, wide_b],
            [gf_own, gf_oth, gate_up, w_gu, w_d], flops=ffn_flops,
            hold=saved + kept_ffn + ([hidden_res] if two else []),
        )
        pair = pair_sum(keep, send)

        def put_grads(full, first, mine_out, give_out, size, lanes=slice(None)):
            second = 3 - first
            for i, step in enumerate((0, second)):
                mine_out[i * size : (i + 1) * size, lanes] = take_block(full, step, size)
            for i, step in enumerate((first, 3)):
                give_out[i * size : (i + 1) * size, lanes] = take_block(full, step, size)

        def ffn_weights(a0, a1, f0, f1, ggu, inner, m1, s1, m2, s2, full1, full2):
            low, high = slice(0, half), slice(half, 2 * half)
            cut = ffn_cols
            full1[...] = (
                dot_tn(a0[...], ggu[low, :cut]) + dot_tn(a1[...], ggu[high, :cut])
            ).astype(BF)
            full2[:, : hidden - split] = (
                dot_tn(a0[...], ggu[low, cut:]) + dot_tn(a1[...], ggu[high, cut:])
            ).astype(BF)
            full2[:, hidden - split :] = (
                dot_tn(f0[...], inner[low, :]) + dot_tn(f1[...], inner[high, :])
            ).astype(BF)
            put_grads(full1, 1, m1, s1, block)
            put_grads(full2, 2, m2, s2, block)

        ffn_m1, ffn_s1, ffn_m2, ffn_s2 = call(
            ffn_weights, "ffn_weights", [shape((2 * block, ffn_cols), BF)] * 4,
            [act_own, act_oth, gf_own, gf_oth, tie(grad_gu, pair), inner_act],
            scratch=[pltpu.VMEM((width, ffn_cols), BF)] * 2, flops=ffn_flops,
        )

        def hop_add(kept, sent, first):
            return (kept.astype(F32) + fsdp_hop(sent, first).astype(F32)).astype(BF)

        ffn_b1 = hop_add(ffn_m1, ffn_s1, 1)
        ffn_b2 = hop_add(ffn_m2, ffn_s2, 2)

        def mid_three(pair, near, res, tot, cot, gains, fo, hid_out, grad_out):
            total = pair[...].astype(F32) + near[...].astype(F32)
            hat, inv = rms_stats(res[...])
            hid_out[half : half + 1, :] = fo[...]
            hid_out[half + 1 : half + 2, :] = jnp.sum(total * hat, axis=0, keepdims=True)
            grad = cot[pl.ds(group_start(), half), :].astype(F32)
            grad = grad + rms_back(total, gains[2:3, :], hat, inv)
            hid_out[:half, :] = grad
            hat, inv = rms_stats(tot[...])
            hid_out[half + 2 : half + 3, :] = jnp.sum(grad * hat, axis=0, keepdims=True)
            hid_out[half + 3 : half + 8, :] = gains[0:5, :]
            grad_out[...] = rms_back(grad, gains[1:2, :], hat, inv).astype(BF)

        grad_hidden, ga_own = call(
            mid_three, "mid_three", [shape((half + 8, width), F32), wide_b],
            [pair, z_near(pair), hidden_res, attn_total, cotangent, gw, ds_fo],
            hold=saved,
        )
        ga_oth = core_swap(ga_own)

        def attn_back(lens, *refs):
            a0, a1, att_r, pre_r, cos_ref, sin_ref, w_r = refs[:7]
            gq_out, gkv_out, part_keep, part_send, dsq, dsk, part = refs[7:]
            attn_r, q_r, k_r, v_r = (att_r.at[x, :] for x in (at_o, at_q, at_k, at_v))
            qp, kp, logt_r = (pre_r.at[x, :] for x in (at_q, at_k, at_o))
            scale_q, scale_k = pre_r[at_g : at_g + 1, :], pre_r[at_g + 1 : at_g + 2, :]
            grad_attn = jnp.concatenate([a0[...], a1[...]], axis=0)
            grad_heads = dot32(grad_attn, w_r[:, kvw + HD :]).astype(BF)
            delta = jnp.sum(
                grad_heads.astype(F32) * attn_r[...].astype(F32), axis=1, keepdims=True
            )
            allowed = mask_of(lens)
            scores = dot_nt(q_r[...], k_r[...])
            probs = jnp.where(allowed, jnp.exp(scores - logt_r[:, :1]), 0.0)
            grad_s = (probs * (dot_nt(grad_heads, v_r[...]) - delta)).astype(BF)
            grad_kn = rotate(dot_tn(grad_s, q_r[...]), cos_ref[...], -sin_ref[...])
            hat, inv = rms_stats(kp[...])
            dsk[...] = jnp.sum(grad_kn * hat, axis=0, keepdims=True)
            gkv_out[:, :HD] = rms_back(grad_kn, scale_k, hat, inv).astype(BF)
            gkv_out[:, HD:] = dot_tn(probs.astype(BF), grad_heads).astype(BF)
            part[...] = dot_nt(gkv_out[...], w_r[:, :kvw])
            grad_qr = dot32(grad_s, k_r[...]) * att_scale
            total_q = jnp.zeros((1, HD), F32)
            for i, place in enumerate(places()):
                mine = slice(i * half, (i + 1) * half)
                grad_qn = rotate(
                    grad_qr[mine], cos_ref[pl.ds(place, half), :], -sin_ref[pl.ds(place, half), :]
                )
                hat, inv = rms_stats(qp[mine, :])
                total_q = total_q + jnp.sum(grad_qn * hat, axis=0, keepdims=True)
                gq_out[mine, :] = rms_back(grad_qn, scale_q, hat, inv).astype(BF)
                part[pl.ds(place, half), :] += dot_nt(gq_out[mine, :], w_r[:, kvw : kvw + HD])
            dsq[...] = total_q
            part_keep[...] = part[:rows, :]
            part_send[...] = part[rows:, :].astype(BF)

        n_rest = stream - rows
        grad_q, grad_kv, part_keep, part_send, ds_q, ds_k = call(
            attn_back, "attn_back",
            [
                shape((n_q, HD), BF), shape((stream, kvw), BF), shape((rows, width), F32),
                shape((n_rest, width), BF), shape((1, HD), F32), shape((1, HD), F32),
            ],
            [ga_own, ga_oth, att_b, att_f, cos_t, sin_t, w_att],
            scalars=[lengths],
            scratch=[pltpu.VMEM((stream, width), F32)],
            hold=[act, grad_hidden] + tok_parts if two else [],
            flops=2 * stream * width * kvw + 10 * n_q * stream * HD, limit=limit,
        )

        quarter = half // 2

        def near_at():
            return lax.axis_index("tensor") % 2

        def share(kept, recv, keep_out, give_out):
            for g in range(2):
                to = slice(g * quarter, (g + 1) * quarter)
                for out, which in ((keep_out, near_at()), (give_out, 1 - near_at())):
                    at = pl.ds(pl.multiple_of(g * half + which * quarter, quarter), quarter)
                    out[to, :] = (kept[at, :] + recv[at, :].astype(F32)).astype(BF)

        if two:
            part_recv = core_swap(part_send)
            part_mine = part_keep
        else:
            part_mine = lax.psum_scatter(
                jnp.concatenate([part_keep, part_send.astype(F32)], axis=0),
                "context", scatter_dimension=0, tiled=True,
            )
            part_recv = jnp.zeros((rows, width), BF)
        row_keep, row_give = call(share, "share_rows", [wide_b, wide_b], [part_mine, part_recv])

        def attn_weights(*refs):
            toks = refs[:n_tok]
            act_r, gq, gkv, a0, a1, att_r, pk, ps, hid, dq, dk = refs[n_tok : n_tok + 11]
            kv_k, kv_s, qo_m, qo_s, full, ext = refs[n_tok + 11 :]
            attn_r = att_r.at[at_o, :]
            low, high = slice(0, half), slice(half, 2 * half)
            dai = jnp.zeros((1, width), F32)
            at = 0
            for tok in toks:
                hat, _ = rms_stats(tok[...].astype(F32))
                size = tok.shape[0]
                if size > rows:
                    dai = dai + jnp.sum(hat[:rows] * pk[...], axis=0, keepdims=True)
                    dai = dai + jnp.sum(hat[rows:] * ps[...].astype(F32), axis=0, keepdims=True)
                else:
                    piece = (pk if at == 0 else ps)[...].astype(F32)
                    dai = dai + jnp.sum(hat * piece, axis=0, keepdims=True)
                at += size
            wide = [dai] + [hid[half + i : half + i + 1, :] * 0.5 for i in (2, 1, 0)]
            slim = [dq[...], dk[...]]
            ext[...] = jnp.zeros(ext.shape, BF)
            row_w = lax.broadcasted_iota(jnp.int32, (EXTRA, block), 0)
            row_s = lax.broadcasted_iota(jnp.int32, (EXTRA, gblock), 0)
            for p in range(n_fsdp):
                tile = jnp.zeros((EXTRA, block), F32)
                for i, vec in enumerate(wide):
                    tile = jnp.where(row_w == i, vec[:, p * block : (p + 1) * block], tile)
                ext[p * EXTRA : (p + 1) * EXTRA, :block] = tile.astype(BF)
                tile = jnp.zeros((EXTRA, gblock), F32)
                for i, vec in enumerate(slim):
                    tile = jnp.where(row_s == i, vec[:, p * gblock : (p + 1) * gblock], tile)
                ext[p * EXTRA : (p + 1) * EXTRA, HD : HD + gblock] = tile.astype(BF)
            full[...] = dot_tn(act_r[...], gkv[...]).astype(BF)
            core = lax.axis_index("context") % 2
            for out, side in ((kv_k, core), (kv_s, 1 - core)):
                lanes = pl.ds(pl.multiple_of(side * HD, HD), HD)
                for i, step in enumerate((0, 2, 1, 3)):
                    at = i * blk_ext
                    from_row = pl.multiple_of((own_f() ^ step) * block, EXTRA)
                    out[at : at + block, :] = full[pl.ds(from_row, block), lanes]
                    from_row = pl.multiple_of((own_f() ^ step) * EXTRA, EXTRA)
                    out[at + block : at + blk_ext, :] = ext[pl.ds(from_row, EXTRA), lanes]
            place0, place1 = places()
            full[:, :HD] = (
                dot_tn(act_r[pl.ds(place0, half), :], gq[low, :])
                + dot_tn(act_r[pl.ds(place1, half), :], gq[high, :])
            ).astype(BF)
            full[:, HD:] = (
                dot_tn(a0[...], attn_r[low, :]) + dot_tn(a1[...], attn_r[high, :])
            ).astype(BF)
            put_grads(full, 2, qo_m, qo_s, block)

        kv_k, kv_s, qo_m, qo_s = call(
            attn_weights, "attn_weights",
            [shape((4 * blk_ext, HD), BF)] * 2 + [shape((2 * block, kvw), BF)] * 2,
            tok_parts
            + [act, tie(grad_q, row_keep, ffn_b1, ffn_b2), grad_kv, ga_own, ga_oth, att_b]
            + [part_keep, part_send, grad_hidden, ds_q, ds_k],
            scratch=[pltpu.VMEM((width, kvw), BF), pltpu.VMEM((n_fsdp * EXTRA, kvw), BF)],
            flops=2 * stream * width * kvw + 4 * n_q * width * HD, limit=limit,
        )

        def add(x, y):
            return (x.astype(F32) + y.astype(F32)).astype(BF)

        def last_add(both, hop):
            size = both.shape[0] // 2
            return across_pairs(both[:size].astype(F32) + hop.astype(F32)).astype(BF)

        row_near = z_near(row_give)
        kv_recv = core_swap(kv_s)
        ffn_l1 = fsdp_hop(ffn_b1[block:], 2)
        ffn_l2 = fsdp_hop(ffn_b2[block:], 1)
        row_near, kv_recv, ffn_l1, ffn_l2 = together(row_near, kv_recv, ffn_l1, ffn_l2)
        ffn_c1 = cross(last_add(ffn_b1, ffn_l1))
        ffn_c2 = cross(last_add(ffn_b2, ffn_l2))
        kv_both = add(kv_k[: 2 * blk_ext], kv_recv[: 2 * blk_ext])
        kv_h1 = fsdp_hop(add(kv_k[2 * blk_ext :], kv_recv[2 * blk_ext :]), 1)
        qo_h1 = fsdp_hop(qo_s, 2)

        def halve(kept, recv, keep_out, give_out):
            group = lax.axis_index("tensor") // 2
            for out, which in ((keep_out, group), (give_out, 1 - group)):
                at = pl.ds(pl.multiple_of(which * quarter, quarter), quarter)
                out[...] = (kept[at, :].astype(F32) + recv[at, :].astype(F32)).astype(BF)

        small_b = shape((quarter, width), BF)
        row_mine, row_far = call(halve, "halve_rows", [small_b, small_b], [row_keep, row_near])
        row_far = z_far(row_far)
        row_far, kv_h1, qo_h1, layer_oth = together(row_far, kv_h1, qo_h1, layer_oth)
        kv_both = add(kv_both, kv_h1)
        kv_h2 = fsdp_hop(kv_both[blk_ext:], 2)
        qo_both = add(qo_m, qo_h1)
        qo_h2 = fsdp_hop(qo_both[block:], 1)

        def last_norm(kept, recv, tok, hid, out):
            grad = kept[...].astype(F32) + recv[...].astype(F32)
            inner = pl.multiple_of(near_at() * quarter, quarter)
            at = pl.multiple_of(group_start() + inner, quarter)
            hat, inv = rms_stats(tok[pl.ds(at, quarter), :].astype(F32))
            hidden_part = hid[pl.ds(inner, quarter), :]
            gain = hid[half + 3 : half + 4, :]
            out[...] = (hidden_part + rms_back(grad, gain, hat, inv)).astype(BF)

        (row_done,) = call(
            last_norm, "last_norm", [small_b], [row_mine, row_far, tokens, grad_hidden]
        )
        row_fars, row_nears = z_far(row_done), z_near(row_done)
        row_fars, row_nears, kv_h2, qo_h2 = together(row_fars, row_nears, kv_h2, qo_h2)
        row_both = z_near(row_fars)
        kv_sum = last_add(kv_both, kv_h2)
        kv_n = z_near(kv_sum)
        qo_c = cross(last_add(qo_both, qo_h2))
        row_both, kv_n, ffn_c1, ffn_c2 = together(row_both, kv_n, ffn_c1, ffn_c2)
        kv_sum = add(kv_sum, kv_n)
        kv_sum = add(kv_sum, z_far(kv_sum))
        kv_other = core_swap(kv_sum)

        qo_x, ffn_x1, ffn_x2 = core_swap(qo_c), core_swap(ffn_c1), core_swap(ffn_c2)

        def finish(
            l0, l1, r0, r1, r2, r3, qx, qy, fx1, fy1, fx2, fy2, kx, ky,
            layer_out, in_out, q_out, k_out, v_out, o_out, g_out, u_out, d_out, *gain_outs,
        ):
            layer_out[pl.ds(group_start(), half), :] = l0[...].astype(F32)
            layer_out[pl.ds(other_start(), half), :] = l1[...].astype(F32)
            group, near = lax.axis_index("tensor") // 2, near_at()
            for ref, g, n in (
                (r0, group, near), (r1, group, 1 - near),
                (r2, 1 - group, near), (r3, 1 - group, 1 - near),
            ):
                at = pl.multiple_of(g * half + n * quarter, quarter)
                in_out[pl.ds(at, quarter), :] = ref[...].astype(F32)
            q_out[...] = qx[:, :HD].astype(F32) + qy[:, :HD].astype(F32)
            o_out[...] = qx[:, HD:].astype(F32) + qy[:, HD:].astype(F32)
            both = fx1[...].astype(F32) + fy1[...].astype(F32)
            g_out[...] = both[:, :hidden]
            u_out[:, :split] = both[:, hidden:]
            both = fx2[...].astype(F32) + fy2[...].astype(F32)
            u_out[:, split:] = both[:, : hidden - split]
            d_out[...] = both[:, hidden - split :]
            first = lax.axis_index("context") % 2 == 0
            mine, other = kx[...].astype(F32), ky[...].astype(F32)
            left = jnp.where(first, mine, other)
            right = jnp.where(first, other, mine)
            k_out[...] = left[:block]
            v_out[...] = right[:block]
            for i in range(4):
                gain_outs[i][...] = left[block + i : block + i + 1, :block]
            for i in range(2):
                gain_outs[4 + i][...] = right[block + i : block + i + 1, :gblock]

        (
            layer_output, grad_input, grad_wq, grad_wk, grad_wv, grad_wo,
            grad_gate, grad_up, grad_down, *gain_grads,
        ) = call(
            finish, "finish",
            [shape((rows, width), F32)] * 2 + [shape((block, HD), F32)] * 4
            + [shape((block, hidden), F32)] * 3 + [shape((1, block), F32)] * 4
            + [shape((1, gblock), F32)] * 2,
            [
                layer_own, layer_oth, row_done, row_nears, row_fars, row_both,
                qo_c, qo_x, ffn_c1, ffn_x1, ffn_c2, ffn_x2, kv_sum, kv_other,
            ],
        )
        return (
            layer_output, grad_input, grad_wq, grad_wk, grad_wv, grad_wo.T,
            grad_gate, grad_up, grad_down.T, *[g.reshape(-1) for g in gain_grads],
        )

    return on_device


def solution(mesh):
    in_specs = (
        P(("fsdp", "context"), None),
        P("fsdp", None),
        P("fsdp", "tensor"),
        P("fsdp", None),
        P("fsdp", None),
        P("tensor", "fsdp"),
        P("fsdp", "tensor"),
        P("fsdp", "tensor"),
        P("tensor", "fsdp"),
        P("fsdp"),
        P("fsdp"),
        P("fsdp"),
        P("fsdp"),
        P("fsdp"),
        P("fsdp"),
        P(("fsdp", "context"), None),
    )
    out_specs = (
        P(("fsdp", "context"), None),
        P(("fsdp", "context"), None),
        P("fsdp", "tensor"),
        P("fsdp", None),
        P("fsdp", None),
        P("tensor", "fsdp"),
        P("fsdp", "tensor"),
        P("fsdp", "tensor"),
        P("tensor", "fsdp"),
        P("fsdp"),
        P("fsdp"),
        P("fsdp"),
        P("fsdp"),
        P("fsdp"),
        P("fsdp"),
    )
    on_device = make_program(mesh.shape["fsdp"], mesh.shape["context"], mesh.shape["tensor"])
    return jax.shard_map(
        on_device, mesh=mesh, in_specs=in_specs, out_specs=out_specs, check_vma=False
    )
```

```python
import math

import jax
import jax.numpy as jnp
from jax import lax
from jax.experimental import pallas as pl
from jax.experimental.pallas import tpu as pltpu
from jax.sharding import PartitionSpec as P

HD = 256

EPSILON = 1e-06
ROPE_BASE = 1000000.0
GELU_COEF = math.sqrt(2.0 / math.pi)
NEG_LARGE = -1e30
BF = jnp.bfloat16
F32 = jnp.float32
EXTRA = 16
SMALL_VMEM = 16 * 2**20
LARGE_VMEM = 48 * 2**20


def rms_stats(values):
    inverse = lax.rsqrt(jnp.mean(values * values, axis=-1, keepdims=True) + EPSILON)
    return values * inverse, inverse


def rms_back(grad_out, gain_vec, normed, inverse):
    inner = grad_out * gain_vec
    return inverse * (inner - normed * jnp.mean(inner * normed, axis=-1, keepdims=True))


def rotate(values, cosine, sine):
    half = values.shape[-1] // 2
    first, second = values[:, :half], values[:, half:]
    return jnp.concatenate(
        [first * cosine - second * sine, second * cosine + first * sine], axis=-1
    )


def gelu_parts(pre_act):
    cubic = pre_act + 0.044715 * pre_act * pre_act * pre_act
    tangent = jnp.tanh(GELU_COEF * cubic)
    gelu_val = 0.5 * pre_act * (1.0 + tangent)
    slope = 0.5 * (1.0 + tangent) + 0.5 * pre_act * (1.0 - tangent * tangent) * GELU_COEF * (
        1.0 + 3.0 * 0.044715 * pre_act * pre_act
    )
    return gelu_val, slope


def dot32(left, right):
    return jnp.dot(left, right, preferred_element_type=F32)


def dot_nt(left, right):
    return lax.dot_general(left, right, (((1,), (1,)), ((), ())), preferred_element_type=F32)


def dot_tn(left, right):
    return lax.dot_general(left, right, (((0,), (0,)), ((), ())), preferred_element_type=F32)


def shape(dims, dtype):
    return jax.ShapeDtypeStruct(dims, dtype)


def call(
    body, name, outs, args, scalars=(), raw=(), hold=(), scratch=(), flops=0, limit=SMALL_VMEM
):
    vmem = pl.BlockSpec(memory_space=pltpu.VMEM)
    smem = pl.BlockSpec(memory_space=pltpu.SMEM)
    size = sum(x.size * x.dtype.itemsize for x in list(args) + list(outs))
    n_used = len(scalars) + len(raw) + len(args)
    n_hold = len(hold)

    def wrapped(*refs):
        body(*refs[:n_used], *refs[n_used + n_hold :])

    return pl.pallas_call(
        wrapped,
        name=name,
        out_shape=tuple(outs),
        in_specs=[smem] * len(scalars)
        + [pl.BlockSpec(memory_space=pltpu.HBM)] * len(raw)
        + [vmem] * len(args)
        + [pl.BlockSpec(memory_space=pl.ANY)] * n_hold,
        out_specs=tuple(vmem for _ in outs),
        scratch_shapes=list(scratch),
        compiler_params=pltpu.CompilerParams(vmem_limit_bytes=limit),
        cost_estimate=pl.CostEstimate(flops=flops, bytes_accessed=size, transcendentals=0),
    )(*scalars, *[pltpu.with_memory_space_constraint(x, pltpu.HBM) for x in raw], *args, *hold)


def tie(value, *others):
    return lax.optimization_barrier((value,) + others)[0]


def together(*values):
    return lax.optimization_barrier(values)


def make_program(n_fsdp, n_context, n_tensor):
    def core_swap(value):
        return lax.ppermute(value, "context", [(i, i ^ 1) for i in range(n_context)])

    def z_near(value):
        return lax.ppermute(value, "tensor", [(i, i ^ 1) for i in range(n_tensor)])

    def z_far(value):
        return lax.ppermute(value, "tensor", [(i, i ^ 2) for i in range(n_tensor)])

    def cross(value):
        pairs = []
        for ctx in range(n_context):
            for pos in range(n_tensor):
                stay = (pos // 2) == (ctx % 2)
                to = ctx * n_tensor + pos if stay else (ctx ^ 1) * n_tensor + (pos ^ 2)
                pairs.append((ctx * n_tensor + pos, to))
        return lax.ppermute(value, ("context", "tensor"), pairs)

    def fsdp_hop(value, step):
        return lax.ppermute(value, "fsdp", [(i, i ^ step) for i in range(n_fsdp)])

    def gather_blocks(value, first):
        second = 3 - first
        near = fsdp_hop(value, first)
        far = fsdp_hop(value, second)
        both = fsdp_hop(near, second)
        return [value, near, far, both] if first == 1 else [value, far, near, both]

    def gather_direct(value):
        return [value] + [fsdp_hop(value, step) for step in range(1, n_fsdp)]

    def across_pairs(value):
        step = 2
        while step < n_context:
            value = value.astype(F32) + lax.ppermute(
                value.astype(BF), "context", [(i, i ^ step) for i in range(n_context)]
            ).astype(F32)
            step *= 2
        return value

    def on_device(
        tokens, lengths, weight_query, weight_key, weight_value, weight_out, weight_gate,
        weight_up, weight_down, gain_attn_in, gain_attn_out, gain_ffn_in, gain_ffn_out,
        gain_query, gain_key, cotangent,
    ):
        rows, width = tokens.shape
        half = rows // 2
        stream = rows * n_context
        block = weight_query.shape[0]
        gblock = gain_query.shape[0]
        hidden = weight_gate.shape[1]
        kvw = 2 * HD
        att_scale = HD ** (-0.5)
        n_doc = lengths.shape[1]
        two = n_context == 2
        limit = SMALL_VMEM if two else LARGE_VMEM
        blk_ext = block + EXTRA

        def own_f():
            return lax.axis_index("fsdp")

        def group_start():
            return pl.multiple_of((lax.axis_index("tensor") // 2) * half, half)

        def other_start():
            return pl.multiple_of((1 - lax.axis_index("tensor") // 2) * half, half)

        def bases():
            ctx = lax.axis_index("context")
            if two:
                return ctx * rows, (ctx ^ 1) * rows
            return 0, rows

        def places():
            ctx = lax.axis_index("context")
            if two:
                return group_start(), pl.multiple_of(rows + group_start(), half)
            return (
                pl.multiple_of(ctx * rows + group_start(), half),
                pl.multiple_of((ctx ^ 1) * rows + group_start(), half),
            )

        def key_index(dims, axis):
            base0, base1 = bases()
            at = lax.broadcasted_iota(jnp.int32, dims, axis)
            return at + jnp.where(at < rows, base0, base1 - rows)

        def query_index(dims):
            ctx = lax.axis_index("context")
            at = lax.broadcasted_iota(jnp.int32, dims, 0)
            first = ctx * rows + group_start()
            second = (ctx ^ 1) * rows + group_start()
            return at + jnp.where(at < half, first, second - half)

        def doc_of(index, lens):
            segment = jnp.zeros(index.shape, jnp.int32)
            start = jnp.zeros(index.shape, jnp.int32)
            end = jnp.int32(0)
            for i in range(n_doc):
                end = end + lens[0, i]
                passed = index >= end
                segment = segment + passed.astype(jnp.int32)
                start = jnp.where(passed, end, start)
            return segment, start

        def mask_of(lens):
            key_at = key_index((1, stream), 1)
            row_at = query_index((2 * half, 1))
            key_seg, _ = doc_of(key_at, lens)
            row_seg, _ = doc_of(row_at, lens)
            return (row_seg == key_seg) & (row_at >= key_at)

        def put_blocks(dest, blocks, columns=None):
            for step in range(n_fsdp):
                at = pl.multiple_of((own_f() ^ step) * block, EXTRA)
                dest[pl.ds(at, block), :] = blocks[step][:block, :]

        def take_block(source, step, size):
            at = pl.multiple_of((own_f() ^ step) * size, EXTRA)
            return source[pl.ds(at, size), :]

        ffn_cols = 3 * hidden // 2
        split = ffn_cols - hidden

        def pack(lens, k_in, v_in, q_in, o_in, g_in, u_in, d_in, *refs):
            gains = refs[:6]
            kv_out, qo_out, f1_out, f2_out, cos_out, sin_out = refs[6:12]
            held, sems = refs[12:18], refs[18]
            moves = [
                (k_in, kv_out.at[:block, :HD]),
                (v_in, kv_out.at[:block, HD:]),
                (q_in, qo_out.at[:, :HD]),
                (o_in, qo_out.at[:, HD:]),
                (g_in, f1_out.at[:, :hidden]),
                (u_in.at[:, :split], f1_out.at[:, hidden:]),
                (u_in.at[:, split:], f2_out.at[:, : hidden - split]),
                (d_in, f2_out.at[:, hidden - split :]),
            ] + list(zip(gains, held))
            copies = [
                pltpu.make_async_copy(src, dst, sems.at[i]) for i, (src, dst) in enumerate(moves)
            ]
            for copy in copies:
                copy.start()
            at = key_index((stream, 1), 0)
            _, start = doc_of(at, lens)
            lane = lax.broadcasted_iota(jnp.int32, (1, HD // 2), 1).astype(F32)
            freqs = jnp.exp(lane * (-2.0 * math.log(ROPE_BASE) / HD))
            angles = (at - start).astype(F32) * freqs
            cos_out[...] = jnp.cos(angles)
            sin_out[...] = jnp.sin(angles)
            for copy in copies:
                copy.wait()
            row = lax.broadcasted_iota(jnp.int32, (EXTRA, block), 0)
            tile = jnp.zeros((EXTRA, block), F32)
            for i in range(4):
                tile = jnp.where(row == i, held[i][...].astype(F32)[None, :], tile)
            kv_out[block:, :] = jnp.zeros((EXTRA, kvw), BF)
            kv_out[block:, :block] = tile.astype(BF)
            row = lax.broadcasted_iota(jnp.int32, (EXTRA, gblock), 0)
            tile = jnp.zeros((EXTRA, gblock), F32)
            for i in range(2):
                tile = jnp.where(row == i, held[4 + i][...].astype(F32)[None, :], tile)
            kv_out[block:, HD : HD + gblock] = tile.astype(BF)

        tok_parts = [tokens, core_swap(tokens)] if two else [
            lax.all_gather(tokens, "context", axis=0, tiled=True)
        ]
        pack_kv, pack_qo, pack_f1, pack_f2, cos_t, sin_t = call(
            pack, "pack",
            [
                shape((blk_ext, kvw), BF), shape((block, kvw), BF), shape((block, ffn_cols), BF),
                shape((block, ffn_cols), BF), shape((stream, HD // 2), F32),
                shape((stream, HD // 2), F32),
            ],
            [], scalars=[lengths],
            raw=[
                weight_key, weight_value, weight_query, weight_out.T, weight_gate, weight_up,
                weight_down.T, gain_attn_in, gain_attn_out, gain_ffn_in, gain_ffn_out,
                gain_query, gain_key,
            ],
            scratch=[pltpu.VMEM((block,), BF)] * 4 + [pltpu.VMEM((gblock,), BF)] * 2
            + [pltpu.SemaphoreType.DMA((14,))],
        )
        pack_kv, pack_qo, pack_f1, pack_f2, tok_other = together(
            pack_kv, pack_qo, pack_f1, pack_f2, tok_parts[-1]
        )
        tok_parts = tok_parts[:-1] + [tok_other]
        cross_qo = cross(pack_qo)
        cross_f1, cross_f2 = cross(pack_f1), cross(pack_f2)
        kv_blocks = gather_blocks(pack_kv, 1)
        qo_blocks = gather_direct(cross_qo)
        f1_blocks = gather_blocks(cross_f1, 1)
        f2_blocks = gather_blocks(cross_f2, 2)

        n_tok = len(tok_parts)

        n_q = 2 * half
        at_q, at_o = slice(0, n_q), slice(n_q, 2 * n_q)
        at_k = slice(2 * n_q, 2 * n_q + stream)
        at_v = slice(2 * n_q + stream, 2 * n_q + 2 * stream)
        at_g = 2 * n_q + stream

        def front(lens, *refs):
            toks = refs[:n_tok]
            kvb = refs[n_tok : n_tok + 4]
            qob = refs[n_tok + 4 : n_tok + 8]
            cos_ref, sin_ref = refs[n_tok + 8 : n_tok + 10]
            act, att_b, att_f, w_att, keep, send, gw = refs[n_tok + 10 :]
            f = own_f()
            for step in range(n_fsdp):
                at = pl.ds(pl.multiple_of((f ^ step) * block, EXTRA), block)
                w_att[at, :kvw] = kvb[step][:block, :]
                w_att[at, kvw:] = qob[step][...]
            tiles = [b[block:, :].astype(F32) for b in kvb]
            chunks = []
            for p in range(n_fsdp):
                tile = tiles[3]
                for step in range(3):
                    tile = jnp.where(f == (p ^ step), tiles[step], tile)
                chunks.append(tile)
            wide = jnp.concatenate([t[:8, :block] for t in chunks], axis=1)
            slim = jnp.concatenate([t[:8, HD : HD + gblock] for t in chunks], axis=1)
            gw[...] = wide
            att_f[at_g:, :] = slim
            scale_ai, scale_q, scale_k = wide[0:1], slim[0:1], slim[1:2]
            at = 0
            for tok in toks:
                hat, _ = rms_stats(tok[...].astype(F32))
                act[at : at + tok.shape[0], :] = (hat * scale_ai).astype(BF)
                at += tok.shape[0]
            kv = dot32(act[...], w_att[:, :kvw])
            att_f[at_k, :] = kv[:, :HD]
            att_b[at_v, :] = kv[:, HD:].astype(BF)
            k_hat, _ = rms_stats(kv[:, :HD])
            att_b[at_k, :] = rotate(k_hat * scale_k, cos_ref[...], sin_ref[...]).astype(BF)
            for i, place in enumerate(places()):
                mine = slice(i * half, (i + 1) * half)
                pre = dot32(act[pl.ds(place, half), :], w_att[:, kvw : kvw + HD])
                att_f[mine, :] = pre
                hat, _ = rms_stats(pre)
                turned = rotate(
                    hat * scale_q, cos_ref[pl.ds(place, half), :], sin_ref[pl.ds(place, half), :]
                )
                att_b[mine, :] = (turned * att_scale).astype(BF)
            allowed = mask_of(lens)
            scores = jnp.where(allowed, dot_nt(att_b[at_q, :], att_b[at_k, :]), NEG_LARGE)
            row_max = jnp.max(scores, axis=1, keepdims=True)
            weights = jnp.where(allowed, jnp.exp(scores - row_max), 0.0)
            total = jnp.sum(weights, axis=1, keepdims=True)
            att_f[at_o, :] = jnp.broadcast_to(row_max + jnp.log(total), (n_q, HD))
            heads = (dot32(weights.astype(BF), att_b[at_v, :]) / total).astype(BF)
            att_b[at_o, :] = heads
            partial = dot_nt(heads, w_att[:, kvw + HD :])
            keep[...] = partial[:half]
            send[...] = partial[half:].astype(BF)

        wide_f, wide_b = shape((half, width), F32), shape((half, width), BF)
        row_f = shape((1, width), F32)
        act, att_b, att_f, w_att, keep, send, gw = call(
            front, "front",
            [
                shape((stream, width), BF), shape((2 * n_q + 2 * stream, HD), BF),
                shape((at_g + 8, HD), F32), shape((width, 2 * kvw), BF), wide_f, wide_b,
                shape((8, width), F32),
            ],
            tok_parts + kv_blocks + qo_blocks + [cos_t, sin_t],
            scalars=[lengths],
            flops=2 * stream * width * kvw + 4 * n_q * stream * HD,
            limit=limit,
        )
        saved = [att_b, att_f, cos_t, sin_t, act, gw, w_att] + tok_parts if two else []

        def pair_sum(kept, sent):
            return (kept + core_swap(sent).astype(F32)).astype(BF)

        def mid_one(pair, near, tok, gains, total_out, res_out, act_out):
            total = pair[...].astype(F32) + near[...].astype(F32)
            total_out[...] = total
            hat, _ = rms_stats(total)
            res = tok[pl.ds(group_start(), half), :].astype(F32) + hat * gains[1:2, :]
            res_out[...] = res
            hat, _ = rms_stats(res)
            act_out[...] = (hat * gains[2:3, :]).astype(BF)

        pair = pair_sum(keep, send)
        attn_total, hidden_res, act_own = call(
            mid_one, "mid_one", [wide_f, wide_f, wide_b], [pair, z_near(pair), tokens, gw],
            hold=saved,
        )
        act_oth = core_swap(act_own)

        def put_ffn(wgu, wd, f1, f2):
            for step in range(n_fsdp):
                at = pl.ds(pl.multiple_of((own_f() ^ step) * block, EXTRA), block)
                wgu[at, :ffn_cols] = f1[step][...]
                wgu[at, ffn_cols:] = f2[step][:, : hidden - split]
                wd[at, :] = f2[step][:, hidden - split :]

        def ffn(a0, a1, *refs):
            gu_out, inner_out, keep, send, wgu, wd = refs[8:]
            put_ffn(wgu, wd, refs[:4], refs[4:8])
            for i, a in enumerate((a0, a1)):
                mine = slice(i * half, (i + 1) * half)
                gu = dot32(a[...], wgu[...])
                gu_out[mine, :] = gu
                gelu_val, _ = gelu_parts(gu[:, :hidden])
                inner = (gelu_val * gu[:, hidden:]).astype(BF)
                inner_out[mine, :] = inner
                partial = dot_nt(inner, wd[...])
                if i == 0:
                    keep[...] = partial
                else:
                    send[...] = partial.astype(BF)

        ffn_flops = 6 * n_q * width * hidden
        gate_up, inner_act, keep, send, w_gu, w_d = call(
            ffn, "ffn",
            [
                shape((n_q, 2 * hidden), F32), shape((n_q, hidden), BF), wide_f, wide_b,
                shape((width, 2 * hidden), BF), shape((width, hidden), BF),
            ],
            [act_own, act_oth] + f1_blocks + f2_blocks, flops=ffn_flops,
            hold=saved + ([hidden_res, attn_total] if two else []),
        )
        kept_ffn = [attn_total, act_own, act_oth, inner_act] if two else []

        def mid_two(pair, near, res, cot, gains, out_ref, grad_out, ds_out):
            hat, inv = rms_stats(pair[...].astype(F32) + near[...].astype(F32))
            out_ref[...] = (res[...] + hat * gains[3:4, :]).astype(BF)
            grad = cot[pl.ds(group_start(), half), :].astype(F32)
            ds_out[...] = jnp.sum(grad * hat, axis=0, keepdims=True)
            grad_out[...] = rms_back(grad, gains[3:4, :], hat, inv).astype(BF)

        pair = pair_sum(keep, send)
        layer_own, gf_own, ds_fo = call(
            mid_two, "mid_two", [wide_b, wide_b, row_f],
            [pair, z_near(pair), hidden_res, cotangent, gw],
            hold=saved + kept_ffn + ([gate_up, w_gu, w_d] if two else []),
        )
        layer_oth = z_far(layer_own)
        gf_oth = core_swap(gf_own)

        def ffn_back(f0, f1, gu_ref, wgu, wd, ggu_out, keep, send):
            for i, g in enumerate((f0, f1)):
                mine = slice(i * half, (i + 1) * half)
                grad_inner = dot32(g[...], wd[...])
                gelu_val, slope = gelu_parts(gu_ref[mine, :hidden])
                up = gu_ref[mine, hidden:]
                ggu_out[mine, :hidden] = (grad_inner * up * slope).astype(BF)
                ggu_out[mine, hidden:] = (grad_inner * gelu_val).astype(BF)
                partial = dot_nt(ggu_out[mine, :], wgu[...])
                if i == 0:
                    keep[...] = partial
                else:
                    send[...] = partial.astype(BF)

        grad_gu, keep, send = call(
            ffn_back, "ffn_back", [shape((n_q, 2 * hidden), BF), wide_f, wide_b],
            [gf_own, gf_oth, gate_up, w_gu, w_d], flops=ffn_flops,
            hold=saved + kept_ffn + ([hidden_res] if two else []),
        )
        pair = pair_sum(keep, send)

        def put_grads(full, first, mine_out, give_out, size, lanes=slice(None)):
            second = 3 - first
            for i, step in enumerate((0, second)):
                mine_out[i * size : (i + 1) * size, lanes] = take_block(full, step, size)
            for i, step in enumerate((first, 3)):
                give_out[i * size : (i + 1) * size, lanes] = take_block(full, step, size)

        def ffn_weights(a0, a1, f0, f1, ggu, inner, m1, s1, m2, s2, full1, full2):
            low, high = slice(0, half), slice(half, 2 * half)
            cut = ffn_cols
            full1[...] = (
                dot_tn(a0[...], ggu[low, :cut]) + dot_tn(a1[...], ggu[high, :cut])
            ).astype(BF)
            full2[:, : hidden - split] = (
                dot_tn(a0[...], ggu[low, cut:]) + dot_tn(a1[...], ggu[high, cut:])
            ).astype(BF)
            full2[:, hidden - split :] = (
                dot_tn(f0[...], inner[low, :]) + dot_tn(f1[...], inner[high, :])
            ).astype(BF)
            put_grads(full1, 1, m1, s1, block)
            put_grads(full2, 2, m2, s2, block)

        ffn_m1, ffn_s1, ffn_m2, ffn_s2 = call(
            ffn_weights, "ffn_weights", [shape((2 * block, ffn_cols), BF)] * 4,
            [act_own, act_oth, gf_own, gf_oth, tie(grad_gu, pair), inner_act],
            scratch=[pltpu.VMEM((width, ffn_cols), BF)] * 2, flops=ffn_flops,
        )

        def hop_add(kept, sent, first):
            return (kept.astype(F32) + fsdp_hop(sent, first).astype(F32)).astype(BF)

        ffn_b1 = hop_add(ffn_m1, ffn_s1, 1)
        ffn_b2 = hop_add(ffn_m2, ffn_s2, 2)

        def mid_three(pair, near, res, tot, cot, gains, fo, hid_out, grad_out):
            total = pair[...].astype(F32) + near[...].astype(F32)
            hat, inv = rms_stats(res[...])
            hid_out[half : half + 1, :] = fo[...]
            hid_out[half + 1 : half + 2, :] = jnp.sum(total * hat, axis=0, keepdims=True)
            grad = cot[pl.ds(group_start(), half), :].astype(F32)
            grad = grad + rms_back(total, gains[2:3, :], hat, inv)
            hid_out[:half, :] = grad
            hat, inv = rms_stats(tot[...])
            hid_out[half + 2 : half + 3, :] = jnp.sum(grad * hat, axis=0, keepdims=True)
            hid_out[half + 3 : half + 8, :] = gains[0:5, :]
            grad_out[...] = rms_back(grad, gains[1:2, :], hat, inv).astype(BF)

        grad_hidden, ga_own = call(
            mid_three, "mid_three", [shape((half + 8, width), F32), wide_b],
            [pair, z_near(pair), hidden_res, attn_total, cotangent, gw, ds_fo],
            hold=saved,
        )
        ga_oth = core_swap(ga_own)

        def attn_back(lens, *refs):
            a0, a1, att_r, pre_r, cos_ref, sin_ref, w_r = refs[:7]
            gq_out, gkv_out, part_keep, part_send, dsq, dsk, part = refs[7:]
            attn_r, q_r, k_r, v_r = (att_r.at[x, :] for x in (at_o, at_q, at_k, at_v))
            qp, kp, logt_r = (pre_r.at[x, :] for x in (at_q, at_k, at_o))
            scale_q, scale_k = pre_r[at_g : at_g + 1, :], pre_r[at_g + 1 : at_g + 2, :]
            grad_attn = jnp.concatenate([a0[...], a1[...]], axis=0)
            grad_heads = dot32(grad_attn, w_r[:, kvw + HD :]).astype(BF)
            delta = jnp.sum(
                grad_heads.astype(F32) * attn_r[...].astype(F32), axis=1, keepdims=True
            )
            allowed = mask_of(lens)
            scores = dot_nt(q_r[...], k_r[...])
            probs = jnp.where(allowed, jnp.exp(scores - logt_r[:, :1]), 0.0)
            grad_s = (probs * (dot_nt(grad_heads, v_r[...]) - delta)).astype(BF)
            grad_kn = rotate(dot_tn(grad_s, q_r[...]), cos_ref[...], -sin_ref[...])
            hat, inv = rms_stats(kp[...])
            dsk[...] = jnp.sum(grad_kn * hat, axis=0, keepdims=True)
            gkv_out[:, :HD] = rms_back(grad_kn, scale_k, hat, inv).astype(BF)
            gkv_out[:, HD:] = dot_tn(probs.astype(BF), grad_heads).astype(BF)
            part[...] = dot_nt(gkv_out[...], w_r[:, :kvw])
            grad_qr = dot32(grad_s, k_r[...]) * att_scale
            total_q = jnp.zeros((1, HD), F32)
            for i, place in enumerate(places()):
                mine = slice(i * half, (i + 1) * half)
                grad_qn = rotate(
                    grad_qr[mine], cos_ref[pl.ds(place, half), :], -sin_ref[pl.ds(place, half), :]
                )
                hat, inv = rms_stats(qp[mine, :])
                total_q = total_q + jnp.sum(grad_qn * hat, axis=0, keepdims=True)
                gq_out[mine, :] = rms_back(grad_qn, scale_q, hat, inv).astype(BF)
                part[pl.ds(place, half), :] += dot_nt(gq_out[mine, :], w_r[:, kvw : kvw + HD])
            dsq[...] = total_q
            part_keep[...] = part[:rows, :]
            part_send[...] = part[rows:, :].astype(BF)

        n_rest = stream - rows
        grad_q, grad_kv, part_keep, part_send, ds_q, ds_k = call(
            attn_back, "attn_back",
            [
                shape((n_q, HD), BF), shape((stream, kvw), BF), shape((rows, width), F32),
                shape((n_rest, width), BF), shape((1, HD), F32), shape((1, HD), F32),
            ],
            [ga_own, ga_oth, att_b, att_f, cos_t, sin_t, w_att],
            scalars=[lengths],
            scratch=[pltpu.VMEM((stream, width), F32)],
            hold=[act, grad_hidden] + tok_parts if two else [],
            flops=2 * stream * width * kvw + 10 * n_q * stream * HD, limit=limit,
        )

        quarter = half // 2

        def near_at():
            return lax.axis_index("tensor") % 2

        def share(kept, recv, keep_out, give_out):
            for g in range(2):
                to = slice(g * quarter, (g + 1) * quarter)
                for out, which in ((keep_out, near_at()), (give_out, 1 - near_at())):
                    at = pl.ds(pl.multiple_of(g * half + which * quarter, quarter), quarter)
                    out[to, :] = (kept[at, :] + recv[at, :].astype(F32)).astype(BF)

        if two:
            part_recv = core_swap(part_send)
            part_mine = part_keep
        else:
            part_mine = lax.psum_scatter(
                jnp.concatenate([part_keep, part_send.astype(F32)], axis=0),
                "context", scatter_dimension=0, tiled=True,
            )
            part_recv = jnp.zeros((rows, width), BF)
        row_keep, row_give = call(share, "share_rows", [wide_b, wide_b], [part_mine, part_recv])

        def attn_weights(*refs):
            toks = refs[:n_tok]
            act_r, gq, gkv, a0, a1, att_r, pk, ps, hid, dq, dk = refs[n_tok : n_tok + 11]
            kv_k, kv_s, qo_m, qo_s, full, ext = refs[n_tok + 11 :]
            attn_r = att_r.at[at_o, :]
            low, high = slice(0, half), slice(half, 2 * half)
            dai = jnp.zeros((1, width), F32)
            at = 0
            for tok in toks:
                hat, _ = rms_stats(tok[...].astype(F32))
                size = tok.shape[0]
                if size > rows:
                    dai = dai + jnp.sum(hat[:rows] * pk[...], axis=0, keepdims=True)
                    dai = dai + jnp.sum(hat[rows:] * ps[...].astype(F32), axis=0, keepdims=True)
                else:
                    piece = (pk if at == 0 else ps)[...].astype(F32)
                    dai = dai + jnp.sum(hat * piece, axis=0, keepdims=True)
                at += size
            wide = [dai] + [hid[half + i : half + i + 1, :] * 0.5 for i in (2, 1, 0)]
            slim = [dq[...], dk[...]]
            ext[...] = jnp.zeros(ext.shape, BF)
            row_w = lax.broadcasted_iota(jnp.int32, (EXTRA, block), 0)
            row_s = lax.broadcasted_iota(jnp.int32, (EXTRA, gblock), 0)
            for p in range(n_fsdp):
                tile = jnp.zeros((EXTRA, block), F32)
                for i, vec in enumerate(wide):
                    tile = jnp.where(row_w == i, vec[:, p * block : (p + 1) * block], tile)
                ext[p * EXTRA : (p + 1) * EXTRA, :block] = tile.astype(BF)
                tile = jnp.zeros((EXTRA, gblock), F32)
                for i, vec in enumerate(slim):
                    tile = jnp.where(row_s == i, vec[:, p * gblock : (p + 1) * gblock], tile)
                ext[p * EXTRA : (p + 1) * EXTRA, HD : HD + gblock] = tile.astype(BF)
            full[...] = dot_tn(act_r[...], gkv[...]).astype(BF)
            core = lax.axis_index("context") % 2
            for out, side in ((kv_k, core), (kv_s, 1 - core)):
                lanes = pl.ds(pl.multiple_of(side * HD, HD), HD)
                for i, step in enumerate((0, 2, 1, 3)):
                    at = i * blk_ext
                    from_row = pl.multiple_of((own_f() ^ step) * block, EXTRA)
                    out[at : at + block, :] = full[pl.ds(from_row, block), lanes]
                    from_row = pl.multiple_of((own_f() ^ step) * EXTRA, EXTRA)
                    out[at + block : at + blk_ext, :] = ext[pl.ds(from_row, EXTRA), lanes]
            place0, place1 = places()
            full[:, :HD] = (
                dot_tn(act_r[pl.ds(place0, half), :], gq[low, :])
                + dot_tn(act_r[pl.ds(place1, half), :], gq[high, :])
            ).astype(BF)
            full[:, HD:] = (
                dot_tn(a0[...], attn_r[low, :]) + dot_tn(a1[...], attn_r[high, :])
            ).astype(BF)
            put_grads(full, 2, qo_m, qo_s, block)

        kv_k, kv_s, qo_m, qo_s = call(
            attn_weights, "attn_weights",
            [shape((4 * blk_ext, HD), BF)] * 2 + [shape((2 * block, kvw), BF)] * 2,
            tok_parts
            + [act, tie(grad_q, row_keep, ffn_b1, ffn_b2), grad_kv, ga_own, ga_oth, att_b]
            + [part_keep, part_send, grad_hidden, ds_q, ds_k],
            scratch=[pltpu.VMEM((width, kvw), BF), pltpu.VMEM((n_fsdp * EXTRA, kvw), BF)],
            flops=2 * stream * width * kvw + 4 * n_q * width * HD, limit=limit,
        )

        def add(x, y):
            return (x.astype(F32) + y.astype(F32)).astype(BF)

        def last_add(both, hop):
            size = both.shape[0] // 2
            return across_pairs(both[:size].astype(F32) + hop.astype(F32)).astype(BF)

        row_near = z_near(row_give)
        kv_recv = core_swap(kv_s)
        ffn_l1 = fsdp_hop(ffn_b1[block:], 2)
        ffn_l2 = fsdp_hop(ffn_b2[block:], 1)
        row_near, kv_recv, ffn_l1, ffn_l2 = together(row_near, kv_recv, ffn_l1, ffn_l2)
        ffn_c1 = cross(last_add(ffn_b1, ffn_l1))
        ffn_c2 = cross(last_add(ffn_b2, ffn_l2))
        kv_both = add(kv_k[: 2 * blk_ext], kv_recv[: 2 * blk_ext])
        kv_h1 = fsdp_hop(add(kv_k[2 * blk_ext :], kv_recv[2 * blk_ext :]), 1)
        qo_h1 = fsdp_hop(qo_s, 2)

        def halve(kept, recv, keep_out, give_out):
            group = lax.axis_index("tensor") // 2
            for out, which in ((keep_out, group), (give_out, 1 - group)):
                at = pl.ds(pl.multiple_of(which * quarter, quarter), quarter)
                out[...] = (kept[at, :].astype(F32) + recv[at, :].astype(F32)).astype(BF)

        small_b = shape((quarter, width), BF)
        row_mine, row_far = call(halve, "halve_rows", [small_b, small_b], [row_keep, row_near])
        row_far = z_far(row_far)
        row_far, kv_h1, qo_h1, layer_oth = together(row_far, kv_h1, qo_h1, layer_oth)
        kv_both = add(kv_both, kv_h1)
        kv_h2 = fsdp_hop(kv_both[blk_ext:], 2)
        qo_both = add(qo_m, qo_h1)
        qo_h2 = fsdp_hop(qo_both[block:], 1)

        def last_norm(kept, recv, tok, hid, out):
            grad = kept[...].astype(F32) + recv[...].astype(F32)
            inner = pl.multiple_of(near_at() * quarter, quarter)
            at = pl.multiple_of(group_start() + inner, quarter)
            hat, inv = rms_stats(tok[pl.ds(at, quarter), :].astype(F32))
            hidden_part = hid[pl.ds(inner, quarter), :]
            gain = hid[half + 3 : half + 4, :]
            out[...] = (hidden_part + rms_back(grad, gain, hat, inv)).astype(BF)

        (row_done,) = call(
            last_norm, "last_norm", [small_b], [row_mine, row_far, tokens, grad_hidden]
        )
        row_fars, row_nears = z_far(row_done), z_near(row_done)
        row_fars, row_nears, kv_h2, qo_h2 = together(row_fars, row_nears, kv_h2, qo_h2)
        row_both = z_near(row_fars)
        kv_sum = last_add(kv_both, kv_h2)
        kv_n = z_near(kv_sum)
        qo_c = cross(last_add(qo_both, qo_h2))
        row_both, kv_n = together(row_both, kv_n)
        kv_sum = add(kv_sum, kv_n)
        kv_sum = add(kv_sum, z_far(kv_sum))
        kv_other = core_swap(kv_sum)

        qo_x, ffn_x1, ffn_x2 = core_swap(qo_c), core_swap(ffn_c1), core_swap(ffn_c2)

        def finish(
            l0, l1, r0, r1, r2, r3, qx, qy, fx1, fy1, fx2, fy2, kx, ky,
            layer_out, in_out, q_out, k_out, v_out, o_out, g_out, u_out, d_out, *gain_outs,
        ):
            layer_out[pl.ds(group_start(), half), :] = l0[...].astype(F32)
            layer_out[pl.ds(other_start(), half), :] = l1[...].astype(F32)
            group, near = lax.axis_index("tensor") // 2, near_at()
            for ref, g, n in (
                (r0, group, near), (r1, group, 1 - near),
                (r2, 1 - group, near), (r3, 1 - group, 1 - near),
            ):
                at = pl.multiple_of(g * half + n * quarter, quarter)
                in_out[pl.ds(at, quarter), :] = ref[...].astype(F32)
            q_out[...] = qx[:, :HD].astype(F32) + qy[:, :HD].astype(F32)
            o_out[...] = qx[:, HD:].astype(F32) + qy[:, HD:].astype(F32)
            both = fx1[...].astype(F32) + fy1[...].astype(F32)
            g_out[...] = both[:, :hidden]
            u_out[:, :split] = both[:, hidden:]
            both = fx2[...].astype(F32) + fy2[...].astype(F32)
            u_out[:, split:] = both[:, : hidden - split]
            d_out[...] = both[:, hidden - split :]
            first = lax.axis_index("context") % 2 == 0
            mine, other = kx[...].astype(F32), ky[...].astype(F32)
            left = jnp.where(first, mine, other)
            right = jnp.where(first, other, mine)
            k_out[...] = left[:block]
            v_out[...] = right[:block]
            for i in range(4):
                gain_outs[i][...] = left[block + i : block + i + 1, :block]
            for i in range(2):
                gain_outs[4 + i][...] = right[block + i : block + i + 1, :gblock]

        (
            layer_output, grad_input, grad_wq, grad_wk, grad_wv, grad_wo,
            grad_gate, grad_up, grad_down, *gain_grads,
        ) = call(
            finish, "finish",
            [shape((rows, width), F32)] * 2 + [shape((block, HD), F32)] * 4
            + [shape((block, hidden), F32)] * 3 + [shape((1, block), F32)] * 4
            + [shape((1, gblock), F32)] * 2,
            [
                layer_own, layer_oth, row_done, row_nears, row_fars, row_both,
                qo_c, qo_x, ffn_c1, ffn_x1, ffn_c2, ffn_x2, kv_sum, kv_other,
            ],
        )
        return (
            layer_output, grad_input, grad_wq, grad_wk, grad_wv, grad_wo.T,
            grad_gate, grad_up, grad_down.T, *[g.reshape(-1) for g in gain_grads],
        )

    return on_device


def solution(mesh):
    in_specs = (
        P(("fsdp", "context"), None),
        P("fsdp", None),
        P("fsdp", "tensor"),
        P("fsdp", None),
        P("fsdp", None),
        P("tensor", "fsdp"),
        P("fsdp", "tensor"),
        P("fsdp", "tensor"),
        P("tensor", "fsdp"),
        P("fsdp"),
        P("fsdp"),
        P("fsdp"),
        P("fsdp"),
        P("fsdp"),
        P("fsdp"),
        P(("fsdp", "context"), None),
    )
    out_specs = (
        P(("fsdp", "context"), None),
        P(("fsdp", "context"), None),
        P("fsdp", "tensor"),
        P("fsdp", None),
        P("fsdp", None),
        P("tensor", "fsdp"),
        P("fsdp", "tensor"),
        P("fsdp", "tensor"),
        P("tensor", "fsdp"),
        P("fsdp"),
        P("fsdp"),
        P("fsdp"),
        P("fsdp"),
        P("fsdp"),
        P("fsdp"),
    )
    on_device = make_program(mesh.shape["fsdp"], mesh.shape["context"], mesh.shape["tensor"])
    return jax.shard_map(
        on_device, mesh=mesh, in_specs=in_specs, out_specs=out_specs, check_vma=False
    )
```

```python
import math

import jax
import jax.numpy as jnp
from jax import lax
from jax.experimental import pallas as pl
from jax.experimental.pallas import tpu as pltpu
from jax.sharding import PartitionSpec as P

HD = 256

EPSILON = 1e-06
ROPE_BASE = 1000000.0
GELU_COEF = math.sqrt(2.0 / math.pi)
NEG_LARGE = -1e30
BF = jnp.bfloat16
F32 = jnp.float32
EXTRA = 16
SMALL_VMEM = 16 * 2**20
LARGE_VMEM = 48 * 2**20


def rms_stats(values):
    inverse = lax.rsqrt(jnp.mean(values * values, axis=-1, keepdims=True) + EPSILON)
    return values * inverse, inverse


def rms_back(grad_out, gain_vec, normed, inverse):
    inner = grad_out * gain_vec
    return inverse * (inner - normed * jnp.mean(inner * normed, axis=-1, keepdims=True))


def rotate(values, cosine, sine):
    half = values.shape[-1] // 2
    first, second = values[:, :half], values[:, half:]
    return jnp.concatenate(
        [first * cosine - second * sine, second * cosine + first * sine], axis=-1
    )


def gelu_parts(pre_act):
    cubic = pre_act + 0.044715 * pre_act * pre_act * pre_act
    tangent = jnp.tanh(GELU_COEF * cubic)
    gelu_val = 0.5 * pre_act * (1.0 + tangent)
    slope = 0.5 * (1.0 + tangent) + 0.5 * pre_act * (1.0 - tangent * tangent) * GELU_COEF * (
        1.0 + 3.0 * 0.044715 * pre_act * pre_act
    )
    return gelu_val, slope


def dot32(left, right):
    return jnp.dot(left, right, preferred_element_type=F32)


def dot_nt(left, right):
    return lax.dot_general(left, right, (((1,), (1,)), ((), ())), preferred_element_type=F32)


def dot_tn(left, right):
    return lax.dot_general(left, right, (((0,), (0,)), ((), ())), preferred_element_type=F32)


def shape(dims, dtype):
    return jax.ShapeDtypeStruct(dims, dtype)


def call(
    body, name, outs, args, scalars=(), raw=(), hold=(), scratch=(), flops=0, limit=SMALL_VMEM
):
    vmem = pl.BlockSpec(memory_space=pltpu.VMEM)
    smem = pl.BlockSpec(memory_space=pltpu.SMEM)
    size = sum(x.size * x.dtype.itemsize for x in list(args) + list(outs))
    n_used = len(scalars) + len(raw) + len(args)
    n_hold = len(hold)

    def wrapped(*refs):
        body(*refs[:n_used], *refs[n_used + n_hold :])

    return pl.pallas_call(
        wrapped,
        name=name,
        out_shape=tuple(outs),
        in_specs=[smem] * len(scalars)
        + [pl.BlockSpec(memory_space=pltpu.HBM)] * len(raw)
        + [vmem] * len(args)
        + [pl.BlockSpec(memory_space=pl.ANY)] * n_hold,
        out_specs=tuple(vmem for _ in outs),
        scratch_shapes=list(scratch),
        compiler_params=pltpu.CompilerParams(vmem_limit_bytes=limit),
        cost_estimate=pl.CostEstimate(flops=flops, bytes_accessed=size, transcendentals=0),
    )(*scalars, *[pltpu.with_memory_space_constraint(x, pltpu.HBM) for x in raw], *args, *hold)


def tie(value, *others):
    return lax.optimization_barrier((value,) + others)[0]


def together(*values):
    return lax.optimization_barrier(values)


def make_program(n_fsdp, n_context, n_tensor):
    def core_swap(value):
        return lax.ppermute(value, "context", [(i, i ^ 1) for i in range(n_context)])

    def z_near(value):
        return lax.ppermute(value, "tensor", [(i, i ^ 1) for i in range(n_tensor)])

    def z_far(value):
        return lax.ppermute(value, "tensor", [(i, i ^ 2) for i in range(n_tensor)])

    def cross(value):
        pairs = []
        for ctx in range(n_context):
            for pos in range(n_tensor):
                stay = (pos // 2) == (ctx % 2)
                to = ctx * n_tensor + pos if stay else (ctx ^ 1) * n_tensor + (pos ^ 2)
                pairs.append((ctx * n_tensor + pos, to))
        return lax.ppermute(value, ("context", "tensor"), pairs)

    def fsdp_hop(value, step):
        return lax.ppermute(value, "fsdp", [(i, i ^ step) for i in range(n_fsdp)])

    def gather_blocks(value, first):
        second = 3 - first
        near = fsdp_hop(value, first)
        far = fsdp_hop(value, second)
        both = fsdp_hop(near, second)
        return [value, near, far, both] if first == 1 else [value, far, near, both]

    def gather_direct(value):
        return [value] + [fsdp_hop(value, step) for step in range(1, n_fsdp)]

    def across_pairs(value):
        step = 2
        while step < n_context:
            value = value.astype(F32) + lax.ppermute(
                value.astype(BF), "context", [(i, i ^ step) for i in range(n_context)]
            ).astype(F32)
            step *= 2
        return value

    def on_device(
        tokens, lengths, weight_query, weight_key, weight_value, weight_out, weight_gate,
        weight_up, weight_down, gain_attn_in, gain_attn_out, gain_ffn_in, gain_ffn_out,
        gain_query, gain_key, cotangent,
    ):
        rows, width = tokens.shape
        half = rows // 2
        stream = rows * n_context
        block = weight_query.shape[0]
        gblock = gain_query.shape[0]
        hidden = weight_gate.shape[1]
        kvw = 2 * HD
        att_scale = HD ** (-0.5)
        n_doc = lengths.shape[1]
        two = n_context == 2
        limit = SMALL_VMEM if two else LARGE_VMEM
        blk_ext = block + EXTRA

        def own_f():
            return lax.axis_index("fsdp")

        def group_start():
            return pl.multiple_of((lax.axis_index("tensor") // 2) * half, half)

        def other_start():
            return pl.multiple_of((1 - lax.axis_index("tensor") // 2) * half, half)

        def bases():
            ctx = lax.axis_index("context")
            if two:
                return ctx * rows, (ctx ^ 1) * rows
            return 0, rows

        def places():
            ctx = lax.axis_index("context")
            if two:
                return group_start(), pl.multiple_of(rows + group_start(), half)
            return (
                pl.multiple_of(ctx * rows + group_start(), half),
                pl.multiple_of((ctx ^ 1) * rows + group_start(), half),
            )

        def key_index(dims, axis):
            base0, base1 = bases()
            at = lax.broadcasted_iota(jnp.int32, dims, axis)
            return at + jnp.where(at < rows, base0, base1 - rows)

        def query_index(dims):
            ctx = lax.axis_index("context")
            at = lax.broadcasted_iota(jnp.int32, dims, 0)
            first = ctx * rows + group_start()
            second = (ctx ^ 1) * rows + group_start()
            return at + jnp.where(at < half, first, second - half)

        def doc_of(index, lens):
            segment = jnp.zeros(index.shape, jnp.int32)
            start = jnp.zeros(index.shape, jnp.int32)
            end = jnp.int32(0)
            for i in range(n_doc):
                end = end + lens[0, i]
                passed = index >= end
                segment = segment + passed.astype(jnp.int32)
                start = jnp.where(passed, end, start)
            return segment, start

        def mask_of(lens):
            key_at = key_index((1, stream), 1)
            row_at = query_index((2 * half, 1))
            key_seg, _ = doc_of(key_at, lens)
            row_seg, _ = doc_of(row_at, lens)
            return (row_seg == key_seg) & (row_at >= key_at)

        def put_blocks(dest, blocks, columns=None):
            for step in range(n_fsdp):
                at = pl.multiple_of((own_f() ^ step) * block, EXTRA)
                dest[pl.ds(at, block), :] = blocks[step][:block, :]

        def take_block(source, step, size):
            at = pl.multiple_of((own_f() ^ step) * size, EXTRA)
            return source[pl.ds(at, size), :]

        ffn_cols = 3 * hidden // 2
        split = ffn_cols - hidden

        def pack(lens, k_in, v_in, q_in, o_in, g_in, u_in, d_in, *refs):
            gains = refs[:6]
            kv_out, qo_out, f1_out, f2_out, cos_out, sin_out = refs[6:12]
            held, sems = refs[12:18], refs[18]
            moves = [
                (k_in, kv_out.at[:block, :HD]),
                (v_in, kv_out.at[:block, HD:]),
                (q_in, qo_out.at[:, :HD]),
                (o_in, qo_out.at[:, HD:]),
                (g_in, f1_out.at[:, :hidden]),
                (u_in.at[:, :split], f1_out.at[:, hidden:]),
                (u_in.at[:, split:], f2_out.at[:, : hidden - split]),
                (d_in, f2_out.at[:, hidden - split :]),
            ] + list(zip(gains, held))
            copies = [
                pltpu.make_async_copy(src, dst, sems.at[i]) for i, (src, dst) in enumerate(moves)
            ]
            for copy in copies:
                copy.start()
            at = key_index((stream, 1), 0)
            _, start = doc_of(at, lens)
            lane = lax.broadcasted_iota(jnp.int32, (1, HD // 2), 1).astype(F32)
            freqs = jnp.exp(lane * (-2.0 * math.log(ROPE_BASE) / HD))
            angles = (at - start).astype(F32) * freqs
            cos_out[...] = jnp.cos(angles)
            sin_out[...] = jnp.sin(angles)
            for copy in copies:
                copy.wait()
            row = lax.broadcasted_iota(jnp.int32, (EXTRA, block), 0)
            tile = jnp.zeros((EXTRA, block), F32)
            for i in range(4):
                tile = jnp.where(row == i, held[i][...].astype(F32)[None, :], tile)
            kv_out[block:, :] = jnp.zeros((EXTRA, kvw), BF)
            kv_out[block:, :block] = tile.astype(BF)
            row = lax.broadcasted_iota(jnp.int32, (EXTRA, gblock), 0)
            tile = jnp.zeros((EXTRA, gblock), F32)
            for i in range(2):
                tile = jnp.where(row == i, held[4 + i][...].astype(F32)[None, :], tile)
            kv_out[block:, HD : HD + gblock] = tile.astype(BF)

        tok_parts = [tokens, core_swap(tokens)] if two else [
            lax.all_gather(tokens, "context", axis=0, tiled=True)
        ]
        pack_kv, pack_qo, pack_f1, pack_f2, cos_t, sin_t = call(
            pack, "pack",
            [
                shape((blk_ext, kvw), BF), shape((block, kvw), BF), shape((block, ffn_cols), BF),
                shape((block, ffn_cols), BF), shape((stream, HD // 2), F32),
                shape((stream, HD // 2), F32),
            ],
            [], scalars=[lengths],
            raw=[
                weight_key, weight_value, weight_query, weight_out.T, weight_gate, weight_up,
                weight_down.T, gain_attn_in, gain_attn_out, gain_ffn_in, gain_ffn_out,
                gain_query, gain_key,
            ],
            scratch=[pltpu.VMEM((block,), BF)] * 4 + [pltpu.VMEM((gblock,), BF)] * 2
            + [pltpu.SemaphoreType.DMA((14,))],
        )
        pack_kv, pack_qo, pack_f1, pack_f2, tok_other = together(
            pack_kv, pack_qo, pack_f1, pack_f2, tok_parts[-1]
        )
        tok_parts = tok_parts[:-1] + [tok_other]
        cross_qo = cross(pack_qo)
        cross_f1, cross_f2 = cross(pack_f1), cross(pack_f2)
        kv_blocks = gather_blocks(pack_kv, 1)
        qo_blocks = gather_direct(cross_qo)
        f1_blocks = gather_blocks(cross_f1, 1)
        f2_blocks = gather_blocks(cross_f2, 2)

        n_tok = len(tok_parts)

        n_q = 2 * half
        at_q, at_o = slice(0, n_q), slice(n_q, 2 * n_q)
        at_k = slice(2 * n_q, 2 * n_q + stream)
        at_v = slice(2 * n_q + stream, 2 * n_q + 2 * stream)
        at_g = 2 * n_q + stream

        def front(lens, *refs):
            toks = refs[:n_tok]
            kvb = refs[n_tok : n_tok + 4]
            qob = refs[n_tok + 4 : n_tok + 8]
            cos_ref, sin_ref = refs[n_tok + 8 : n_tok + 10]
            act, att_b, att_f, w_att, keep, send, gw = refs[n_tok + 10 :]
            f = own_f()
            for step in range(n_fsdp):
                at = pl.ds(pl.multiple_of((f ^ step) * block, EXTRA), block)
                w_att[at, :kvw] = kvb[step][:block, :]
                w_att[at, kvw:] = qob[step][...]
            tiles = [b[block:, :].astype(F32) for b in kvb]
            chunks = []
            for p in range(n_fsdp):
                tile = tiles[3]
                for step in range(3):
                    tile = jnp.where(f == (p ^ step), tiles[step], tile)
                chunks.append(tile)
            wide = jnp.concatenate([t[:8, :block] for t in chunks], axis=1)
            slim = jnp.concatenate([t[:8, HD : HD + gblock] for t in chunks], axis=1)
            gw[...] = wide
            att_f[at_g:, :] = slim
            scale_ai, scale_q, scale_k = wide[0:1], slim[0:1], slim[1:2]
            at = 0
            for tok in toks:
                hat, _ = rms_stats(tok[...].astype(F32))
                act[at : at + tok.shape[0], :] = (hat * scale_ai).astype(BF)
                at += tok.shape[0]
            kv = dot32(act[...], w_att[:, :kvw])
            att_f[at_k, :] = kv[:, :HD]
            att_b[at_v, :] = kv[:, HD:].astype(BF)
            k_hat, _ = rms_stats(kv[:, :HD])
            att_b[at_k, :] = rotate(k_hat * scale_k, cos_ref[...], sin_ref[...]).astype(BF)
            for i, place in enumerate(places()):
                mine = slice(i * half, (i + 1) * half)
                pre = dot32(act[pl.ds(place, half), :], w_att[:, kvw : kvw + HD])
                att_f[mine, :] = pre
                hat, _ = rms_stats(pre)
                turned = rotate(
                    hat * scale_q, cos_ref[pl.ds(place, half), :], sin_ref[pl.ds(place, half), :]
                )
                att_b[mine, :] = (turned * att_scale).astype(BF)
            allowed = mask_of(lens)
            scores = jnp.where(allowed, dot_nt(att_b[at_q, :], att_b[at_k, :]), NEG_LARGE)
            row_max = jnp.max(scores, axis=1, keepdims=True)
            weights = jnp.where(allowed, jnp.exp(scores - row_max), 0.0)
            total = jnp.sum(weights, axis=1, keepdims=True)
            att_f[at_o, :] = jnp.broadcast_to(row_max + jnp.log(total), (n_q, HD))
            heads = (dot32(weights.astype(BF), att_b[at_v, :]) / total).astype(BF)
            att_b[at_o, :] = heads
            partial = dot_nt(heads, w_att[:, kvw + HD :])
            keep[...] = partial[:half]
            send[...] = partial[half:].astype(BF)

        wide_f, wide_b = shape((half, width), F32), shape((half, width), BF)
        row_f = shape((1, width), F32)
        act, att_b, att_f, w_att, keep, send, gw = call(
            front, "front",
            [
                shape((stream, width), BF), shape((2 * n_q + 2 * stream, HD), BF),
                shape((at_g + 8, HD), F32), shape((width, 2 * kvw), BF), wide_f, wide_b,
                shape((8, width), F32),
            ],
            tok_parts + kv_blocks + qo_blocks + [cos_t, sin_t],
            scalars=[lengths],
            flops=2 * stream * width * kvw + 4 * n_q * stream * HD,
            limit=limit,
        )
        saved = [att_b, att_f, cos_t, sin_t, act, gw, w_att] + tok_parts if two else []

        def pair_sum(kept, sent):
            return (kept + core_swap(sent).astype(F32)).astype(BF)

        def mid_one(pair, near, tok, gains, total_out, res_out, act_out):
            total = pair[...].astype(F32) + near[...].astype(F32)
            total_out[...] = total
            hat, _ = rms_stats(total)
            res = tok[pl.ds(group_start(), half), :].astype(F32) + hat * gains[1:2, :]
            res_out[...] = res
            hat, _ = rms_stats(res)
            act_out[...] = (hat * gains[2:3, :]).astype(BF)

        pair = pair_sum(keep, send)
        attn_total, hidden_res, act_own = call(
            mid_one, "mid_one", [wide_f, wide_f, wide_b], [pair, z_near(pair), tokens, gw],
            hold=saved,
        )
        act_oth = core_swap(act_own)

        def put_ffn(wgu, wd, f1, f2):
            for step in range(n_fsdp):
                at = pl.ds(pl.multiple_of((own_f() ^ step) * block, EXTRA), block)
                wgu[at, :ffn_cols] = f1[step][...]
                wgu[at, ffn_cols:] = f2[step][:, : hidden - split]
                wd[at, :] = f2[step][:, hidden - split :]

        def ffn(a0, a1, *refs):
            gu_out, inner_out, keep, send, wgu, wd = refs[8:]
            put_ffn(wgu, wd, refs[:4], refs[4:8])
            for i, a in enumerate((a0, a1)):
                mine = slice(i * half, (i + 1) * half)
                gu = dot32(a[...], wgu[...])
                gu_out[mine, :] = gu
                gelu_val, _ = gelu_parts(gu[:, :hidden])
                inner = (gelu_val * gu[:, hidden:]).astype(BF)
                inner_out[mine, :] = inner
                partial = dot_nt(inner, wd[...])
                if i == 0:
                    keep[...] = partial
                else:
                    send[...] = partial.astype(BF)

        ffn_flops = 6 * n_q * width * hidden
        gate_up, inner_act, keep, send, w_gu, w_d = call(
            ffn, "ffn",
            [
                shape((n_q, 2 * hidden), F32), shape((n_q, hidden), BF), wide_f, wide_b,
                shape((width, 2 * hidden), BF), shape((width, hidden), BF),
            ],
            [act_own, act_oth] + f1_blocks + f2_blocks, flops=ffn_flops,
            hold=saved + ([hidden_res, attn_total] if two else []),
        )
        kept_ffn = [attn_total, act_own, act_oth, inner_act] if two else []

        def mid_two(pair, near, res, cot, gains, out_ref, grad_out, ds_out):
            hat, inv = rms_stats(pair[...].astype(F32) + near[...].astype(F32))
            out_ref[...] = (res[...] + hat * gains[3:4, :]).astype(BF)
            grad = cot[pl.ds(group_start(), half), :].astype(F32)
            ds_out[...] = jnp.sum(grad * hat, axis=0, keepdims=True)
            grad_out[...] = rms_back(grad, gains[3:4, :], hat, inv).astype(BF)

        pair = pair_sum(keep, send)
        layer_own, gf_own, ds_fo = call(
            mid_two, "mid_two", [wide_b, wide_b, row_f],
            [pair, z_near(pair), hidden_res, cotangent, gw],
            hold=saved + kept_ffn + ([gate_up, w_gu, w_d] if two else []),
        )
        layer_oth = z_far(layer_own)
        gf_oth = core_swap(gf_own)

        def ffn_back(f0, f1, gu_ref, wgu, wd, ggu_out, keep, send):
            for i, g in enumerate((f0, f1)):
                mine = slice(i * half, (i + 1) * half)
                grad_inner = dot32(g[...], wd[...])
                gelu_val, slope = gelu_parts(gu_ref[mine, :hidden])
                up = gu_ref[mine, hidden:]
                ggu_out[mine, :hidden] = (grad_inner * up * slope).astype(BF)
                ggu_out[mine, hidden:] = (grad_inner * gelu_val).astype(BF)
                partial = dot_nt(ggu_out[mine, :], wgu[...])
                if i == 0:
                    keep[...] = partial
                else:
                    send[...] = partial.astype(BF)

        grad_gu, keep, send = call(
            ffn_back, "ffn_back", [shape((n_q, 2 * hidden), BF), wide_f, wide_b],
            [gf_own, gf_oth, gate_up, w_gu, w_d], flops=ffn_flops,
            hold=saved + kept_ffn + ([hidden_res] if two else []),
        )
        pair = pair_sum(keep, send)

        def put_grads(full, first, mine_out, give_out, size, lanes=slice(None)):
            second = 3 - first
            for i, step in enumerate((0, second)):
                mine_out[i * size : (i + 1) * size, lanes] = take_block(full, step, size)
            for i, step in enumerate((first, 3)):
                give_out[i * size : (i + 1) * size, lanes] = take_block(full, step, size)

        def ffn_weights(a0, a1, f0, f1, ggu, inner, m1, s1, m2, s2, full1, full2):
            low, high = slice(0, half), slice(half, 2 * half)
            cut = ffn_cols
            full1[...] = (
                dot_tn(a0[...], ggu[low, :cut]) + dot_tn(a1[...], ggu[high, :cut])
            ).astype(BF)
            full2[:, : hidden - split] = (
                dot_tn(a0[...], ggu[low, cut:]) + dot_tn(a1[...], ggu[high, cut:])
            ).astype(BF)
            full2[:, hidden - split :] = (
                dot_tn(f0[...], inner[low, :]) + dot_tn(f1[...], inner[high, :])
            ).astype(BF)
            put_grads(full1, 1, m1, s1, block)
            put_grads(full2, 2, m2, s2, block)

        ffn_m1, ffn_s1, ffn_m2, ffn_s2 = call(
            ffn_weights, "ffn_weights", [shape((2 * block, ffn_cols), BF)] * 4,
            [act_own, act_oth, gf_own, gf_oth, tie(grad_gu, pair), inner_act],
            scratch=[pltpu.VMEM((width, ffn_cols), BF)] * 2, flops=ffn_flops,
        )

        def hop_add(kept, sent, first):
            return (kept.astype(F32) + fsdp_hop(sent, first).astype(F32)).astype(BF)

        ffn_b1 = hop_add(ffn_m1, ffn_s1, 1)
        ffn_b2 = hop_add(ffn_m2, ffn_s2, 2)

        def mid_three(pair, near, res, tot, cot, gains, fo, hid_out, grad_out):
            total = pair[...].astype(F32) + near[...].astype(F32)
            hat, inv = rms_stats(res[...])
            hid_out[half : half + 1, :] = fo[...]
            hid_out[half + 1 : half + 2, :] = jnp.sum(total * hat, axis=0, keepdims=True)
            grad = cot[pl.ds(group_start(), half), :].astype(F32)
            grad = grad + rms_back(total, gains[2:3, :], hat, inv)
            hid_out[:half, :] = grad
            hat, inv = rms_stats(tot[...])
            hid_out[half + 2 : half + 3, :] = jnp.sum(grad * hat, axis=0, keepdims=True)
            hid_out[half + 3 : half + 8, :] = gains[0:5, :]
            grad_out[...] = rms_back(grad, gains[1:2, :], hat, inv).astype(BF)

        grad_hidden, ga_own = call(
            mid_three, "mid_three", [shape((half + 8, width), F32), wide_b],
            [pair, z_near(pair), hidden_res, attn_total, cotangent, gw, ds_fo],
            hold=saved,
        )
        ga_oth = core_swap(ga_own)

        def attn_back(lens, *refs):
            a0, a1, att_r, pre_r, cos_ref, sin_ref, w_r = refs[:7]
            gq_out, gkv_out, part_keep, part_send, dsq, dsk, part = refs[7:]
            attn_r, q_r, k_r, v_r = (att_r.at[x, :] for x in (at_o, at_q, at_k, at_v))
            qp, kp, logt_r = (pre_r.at[x, :] for x in (at_q, at_k, at_o))
            scale_q, scale_k = pre_r[at_g : at_g + 1, :], pre_r[at_g + 1 : at_g + 2, :]
            grad_attn = jnp.concatenate([a0[...], a1[...]], axis=0)
            grad_heads = dot32(grad_attn, w_r[:, kvw + HD :]).astype(BF)
            delta = jnp.sum(
                grad_heads.astype(F32) * attn_r[...].astype(F32), axis=1, keepdims=True
            )
            allowed = mask_of(lens)
            scores = dot_nt(q_r[...], k_r[...])
            probs = jnp.where(allowed, jnp.exp(scores - logt_r[:, :1]), 0.0)
            grad_s = (probs * (dot_nt(grad_heads, v_r[...]) - delta)).astype(BF)
            grad_kn = rotate(dot_tn(grad_s, q_r[...]), cos_ref[...], -sin_ref[...])
            hat, inv = rms_stats(kp[...])
            dsk[...] = jnp.sum(grad_kn * hat, axis=0, keepdims=True)
            gkv_out[:, :HD] = rms_back(grad_kn, scale_k, hat, inv).astype(BF)
            gkv_out[:, HD:] = dot_tn(probs.astype(BF), grad_heads).astype(BF)
            part[...] = dot_nt(gkv_out[...], w_r[:, :kvw])
            grad_qr = dot32(grad_s, k_r[...]) * att_scale
            total_q = jnp.zeros((1, HD), F32)
            for i, place in enumerate(places()):
                mine = slice(i * half, (i + 1) * half)
                grad_qn = rotate(
                    grad_qr[mine], cos_ref[pl.ds(place, half), :], -sin_ref[pl.ds(place, half), :]
                )
                hat, inv = rms_stats(qp[mine, :])
                total_q = total_q + jnp.sum(grad_qn * hat, axis=0, keepdims=True)
                gq_out[mine, :] = rms_back(grad_qn, scale_q, hat, inv).astype(BF)
                part[pl.ds(place, half), :] += dot_nt(gq_out[mine, :], w_r[:, kvw : kvw + HD])
            dsq[...] = total_q
            part_keep[...] = part[:rows, :]
            part_send[...] = part[rows:, :].astype(BF)

        n_rest = stream - rows
        grad_q, grad_kv, part_keep, part_send, ds_q, ds_k = call(
            attn_back, "attn_back",
            [
                shape((n_q, HD), BF), shape((stream, kvw), BF), shape((rows, width), F32),
                shape((n_rest, width), BF), shape((1, HD), F32), shape((1, HD), F32),
            ],
            [ga_own, ga_oth, att_b, att_f, cos_t, sin_t, w_att],
            scalars=[lengths],
            scratch=[pltpu.VMEM((stream, width), F32)],
            hold=[act, grad_hidden] + tok_parts if two else [],
            flops=2 * stream * width * kvw + 10 * n_q * stream * HD, limit=limit,
        )

        quarter = half // 2

        def near_at():
            return lax.axis_index("tensor") % 2

        def share(kept, recv, keep_out, give_out):
            for g in range(2):
                to = slice(g * quarter, (g + 1) * quarter)
                for out, which in ((keep_out, near_at()), (give_out, 1 - near_at())):
                    at = pl.ds(pl.multiple_of(g * half + which * quarter, quarter), quarter)
                    out[to, :] = (kept[at, :] + recv[at, :].astype(F32)).astype(BF)

        if two:
            part_recv = core_swap(part_send)
            part_mine = part_keep
        else:
            part_mine = lax.psum_scatter(
                jnp.concatenate([part_keep, part_send.astype(F32)], axis=0),
                "context", scatter_dimension=0, tiled=True,
            )
            part_recv = jnp.zeros((rows, width), BF)
        row_keep, row_give = call(share, "share_rows", [wide_b, wide_b], [part_mine, part_recv])

        def attn_weights(*refs):
            toks = refs[:n_tok]
            act_r, gq, gkv, a0, a1, att_r, pk, ps, hid, dq, dk = refs[n_tok : n_tok + 11]
            kv_k, kv_s, qo_m, qo_s, full, ext = refs[n_tok + 11 :]
            attn_r = att_r.at[at_o, :]
            low, high = slice(0, half), slice(half, 2 * half)
            dai = jnp.zeros((1, width), F32)
            at = 0
            for tok in toks:
                hat, _ = rms_stats(tok[...].astype(F32))
                size = tok.shape[0]
                if size > rows:
                    dai = dai + jnp.sum(hat[:rows] * pk[...], axis=0, keepdims=True)
                    dai = dai + jnp.sum(hat[rows:] * ps[...].astype(F32), axis=0, keepdims=True)
                else:
                    piece = (pk if at == 0 else ps)[...].astype(F32)
                    dai = dai + jnp.sum(hat * piece, axis=0, keepdims=True)
                at += size
            wide = [dai] + [hid[half + i : half + i + 1, :] * 0.5 for i in (2, 1, 0)]
            slim = [dq[...], dk[...]]
            ext[...] = jnp.zeros(ext.shape, BF)
            row_w = lax.broadcasted_iota(jnp.int32, (EXTRA, block), 0)
            row_s = lax.broadcasted_iota(jnp.int32, (EXTRA, gblock), 0)
            for p in range(n_fsdp):
                tile = jnp.zeros((EXTRA, block), F32)
                for i, vec in enumerate(wide):
                    tile = jnp.where(row_w == i, vec[:, p * block : (p + 1) * block], tile)
                ext[p * EXTRA : (p + 1) * EXTRA, :block] = tile.astype(BF)
                tile = jnp.zeros((EXTRA, gblock), F32)
                for i, vec in enumerate(slim):
                    tile = jnp.where(row_s == i, vec[:, p * gblock : (p + 1) * gblock], tile)
                ext[p * EXTRA : (p + 1) * EXTRA, HD : HD + gblock] = tile.astype(BF)
            full[...] = dot_tn(act_r[...], gkv[...]).astype(BF)
            core = lax.axis_index("context") % 2
            for out, side in ((kv_k, core), (kv_s, 1 - core)):
                lanes = pl.ds(pl.multiple_of(side * HD, HD), HD)
                for i, step in enumerate((0, 2, 1, 3)):
                    at = i * blk_ext
                    from_row = pl.multiple_of((own_f() ^ step) * block, EXTRA)
                    out[at : at + block, :] = full[pl.ds(from_row, block), lanes]
                    from_row = pl.multiple_of((own_f() ^ step) * EXTRA, EXTRA)
                    out[at + block : at + blk_ext, :] = ext[pl.ds(from_row, EXTRA), lanes]
            place0, place1 = places()
            full[:, :HD] = (
                dot_tn(act_r[pl.ds(place0, half), :], gq[low, :])
                + dot_tn(act_r[pl.ds(place1, half), :], gq[high, :])
            ).astype(BF)
            full[:, HD:] = (
                dot_tn(a0[...], attn_r[low, :]) + dot_tn(a1[...], attn_r[high, :])
            ).astype(BF)
            put_grads(full, 2, qo_m, qo_s, block)

        kv_k, kv_s, qo_m, qo_s = call(
            attn_weights, "attn_weights",
            [shape((4 * blk_ext, HD), BF)] * 2 + [shape((2 * block, kvw), BF)] * 2,
            tok_parts
            + [act, tie(grad_q, row_keep, ffn_b1, ffn_b2), grad_kv, ga_own, ga_oth, att_b]
            + [part_keep, part_send, grad_hidden, ds_q, ds_k],
            scratch=[pltpu.VMEM((width, kvw), BF), pltpu.VMEM((n_fsdp * EXTRA, kvw), BF)],
            flops=2 * stream * width * kvw + 4 * n_q * width * HD, limit=limit,
        )

        def add(x, y):
            return (x.astype(F32) + y.astype(F32)).astype(BF)

        def last_add(both, hop):
            size = both.shape[0] // 2
            return across_pairs(both[:size].astype(F32) + hop.astype(F32)).astype(BF)

        row_near = z_near(row_give)
        kv_recv = core_swap(kv_s)
        ffn_l1 = fsdp_hop(ffn_b1[block:], 2)
        ffn_l2 = fsdp_hop(ffn_b2[block:], 1)
        row_near, kv_recv, ffn_l1, ffn_l2 = together(row_near, kv_recv, ffn_l1, ffn_l2)
        ffn_c1 = cross(last_add(ffn_b1, ffn_l1))
        ffn_c2 = cross(last_add(ffn_b2, ffn_l2))
        kv_both = add(kv_k[: 2 * blk_ext], kv_recv[: 2 * blk_ext])
        kv_h1 = fsdp_hop(add(kv_k[2 * blk_ext :], kv_recv[2 * blk_ext :]), 1)
        qo_h1 = fsdp_hop(qo_s, 2)

        def halve(kept, recv, keep_out, give_out):
            group = lax.axis_index("tensor") // 2
            for out, which in ((keep_out, group), (give_out, 1 - group)):
                at = pl.ds(pl.multiple_of(which * quarter, quarter), quarter)
                out[...] = (kept[at, :].astype(F32) + recv[at, :].astype(F32)).astype(BF)

        small_b = shape((quarter, width), BF)
        row_mine, row_far = call(halve, "halve_rows", [small_b, small_b], [row_keep, row_near])
        row_far = z_far(row_far)
        row_far, kv_h1, qo_h1, layer_oth = together(row_far, kv_h1, qo_h1, layer_oth)
        kv_both = add(kv_both, kv_h1)
        kv_h2 = fsdp_hop(kv_both[blk_ext:], 2)
        qo_both = add(qo_m, qo_h1)
        qo_h2 = fsdp_hop(qo_both[block:], 1)

        def last_norm(kept, recv, tok, hid, out):
            grad = kept[...].astype(F32) + recv[...].astype(F32)
            inner = pl.multiple_of(near_at() * quarter, quarter)
            at = pl.multiple_of(group_start() + inner, quarter)
            hat, inv = rms_stats(tok[pl.ds(at, quarter), :].astype(F32))
            hidden_part = hid[pl.ds(inner, quarter), :]
            gain = hid[half + 3 : half + 4, :]
            out[...] = (hidden_part + rms_back(grad, gain, hat, inv)).astype(BF)

        (row_done,) = call(
            last_norm, "last_norm", [small_b], [row_mine, row_far, tokens, grad_hidden]
        )
        row_fars, row_nears = z_far(row_done), z_near(row_done)
        row_fars, kv_h2, qo_h2 = together(row_fars, kv_h2, qo_h2)
        row_both = z_near(row_fars)
        kv_sum = last_add(kv_both, kv_h2)
        kv_n = z_near(kv_sum)
        qo_c = cross(last_add(qo_both, qo_h2))
        row_both, kv_n = together(row_both, kv_n)
        kv_sum = add(kv_sum, kv_n)
        kv_sum = add(kv_sum, z_far(kv_sum))
        kv_other = core_swap(kv_sum)

        qo_x, ffn_x1, ffn_x2 = core_swap(qo_c), core_swap(ffn_c1), core_swap(ffn_c2)

        def finish(
            l0, l1, r0, r1, r2, r3, qx, qy, fx1, fy1, fx2, fy2, kx, ky,
            layer_out, in_out, q_out, k_out, v_out, o_out, g_out, u_out, d_out, *gain_outs,
        ):
            layer_out[pl.ds(group_start(), half), :] = l0[...].astype(F32)
            layer_out[pl.ds(other_start(), half), :] = l1[...].astype(F32)
            group, near = lax.axis_index("tensor") // 2, near_at()
            for ref, g, n in (
                (r0, group, near), (r1, group, 1 - near),
                (r2, 1 - group, near), (r3, 1 - group, 1 - near),
            ):
                at = pl.multiple_of(g * half + n * quarter, quarter)
                in_out[pl.ds(at, quarter), :] = ref[...].astype(F32)
            q_out[...] = qx[:, :HD].astype(F32) + qy[:, :HD].astype(F32)
            o_out[...] = qx[:, HD:].astype(F32) + qy[:, HD:].astype(F32)
            both = fx1[...].astype(F32) + fy1[...].astype(F32)
            g_out[...] = both[:, :hidden]
            u_out[:, :split] = both[:, hidden:]
            both = fx2[...].astype(F32) + fy2[...].astype(F32)
            u_out[:, split:] = both[:, : hidden - split]
            d_out[...] = both[:, hidden - split :]
            first = lax.axis_index("context") % 2 == 0
            mine, other = kx[...].astype(F32), ky[...].astype(F32)
            left = jnp.where(first, mine, other)
            right = jnp.where(first, other, mine)
            k_out[...] = left[:block]
            v_out[...] = right[:block]
            for i in range(4):
                gain_outs[i][...] = left[block + i : block + i + 1, :block]
            for i in range(2):
                gain_outs[4 + i][...] = right[block + i : block + i + 1, :gblock]

        (
            layer_output, grad_input, grad_wq, grad_wk, grad_wv, grad_wo,
            grad_gate, grad_up, grad_down, *gain_grads,
        ) = call(
            finish, "finish",
            [shape((rows, width), F32)] * 2 + [shape((block, HD), F32)] * 4
            + [shape((block, hidden), F32)] * 3 + [shape((1, block), F32)] * 4
            + [shape((1, gblock), F32)] * 2,
            [
                layer_own, layer_oth, row_done, row_nears, row_fars, row_both,
                qo_c, qo_x, ffn_c1, ffn_x1, ffn_c2, ffn_x2, kv_sum, kv_other,
            ],
        )
        return (
            layer_output, grad_input, grad_wq, grad_wk, grad_wv, grad_wo.T,
            grad_gate, grad_up, grad_down.T, *[g.reshape(-1) for g in gain_grads],
        )

    return on_device


def solution(mesh):
    in_specs = (
        P(("fsdp", "context"), None),
        P("fsdp", None),
        P("fsdp", "tensor"),
        P("fsdp", None),
        P("fsdp", None),
        P("tensor", "fsdp"),
        P("fsdp", "tensor"),
        P("fsdp", "tensor"),
        P("tensor", "fsdp"),
        P("fsdp"),
        P("fsdp"),
        P("fsdp"),
        P("fsdp"),
        P("fsdp"),
        P("fsdp"),
        P(("fsdp", "context"), None),
    )
    out_specs = (
        P(("fsdp", "context"), None),
        P(("fsdp", "context"), None),
        P("fsdp", "tensor"),
        P("fsdp", None),
        P("fsdp", None),
        P("tensor", "fsdp"),
        P("fsdp", "tensor"),
        P("fsdp", "tensor"),
        P("tensor", "fsdp"),
        P("fsdp"),
        P("fsdp"),
        P("fsdp"),
        P("fsdp"),
        P("fsdp"),
        P("fsdp"),
    )
    on_device = make_program(mesh.shape["fsdp"], mesh.shape["context"], mesh.shape["tensor"])
    return jax.shard_map(
        on_device, mesh=mesh, in_specs=in_specs, out_specs=out_specs, check_vma=False
    )
```
